32 devices in a mesh: dp: 8 (over y, x, core), tensor: 4 (over z).
Axes of the slice: x: 2, y: 2, z: 4, core: 2. Of those that a mesh axis runs over, the one named last changes fastest.
Arguments:
- inputs: bfloat16 [16384, 768], P('dp'), may hold values from -6 to 6
- w_query: bfloat16 [768, 768], P(None, 'tensor'), may hold values from -0.21875 to 0.21875
- b_query: bfloat16 [768], P('tensor'), may hold values from -3 to 3
- w_key: bfloat16 [768, 768], P(None, 'tensor'), may hold values from -0.21875 to 0.21875
- w_value: bfloat16 [768, 768], P(None, 'tensor'), may hold values from -0.21875 to 0.21875
- b_value: bfloat16 [768], P('tensor'), may hold values from -3 to 3
- w_output: bfloat16 [768, 768], P('tensor'), may hold values from -6 to 6
- b_output: bfloat16 [768], replicated, may hold values from -3 to 3
- gain_attn: bfloat16 [768], replicated, may hold values from 0.5 to 1.5
- shift_attn: bfloat16 [768], replicated, may hold values from -3 to 3
- w_inner: bfloat16 [768, 3072], P(None, 'tensor'), may hold values from -0.21875 to 0.21875
- b_inner: bfloat16 [3072], P('tensor'), may hold values from -3 to 3
- w_outer: bfloat16 [3072, 768], P('tensor'), may hold values from -0.109375 to 0.109375
- b_outer: bfloat16 [768], replicated, may hold values from -3 to 3
- gain_ffn: bfloat16 [768], replicated, may hold values from 0.5 to 1.5
- shift_ffn: bfloat16 [768], replicated, may hold values from -3 to 3
- cotangent: bfloat16 [16384, 768], P('dp'), may hold values from -6 to 6
Outputs:
- layer_out: bfloat16 [16384, 768], P('dp')
- grad_inputs: float32 [16384, 768], P('dp')
- grad_w_query: float32 [768, 768], P('dp', 'tensor')
- grad_b_query: float32 [768], P('tensor')
- grad_w_key: float32 [768, 768], P('dp', 'tensor')
- grad_w_value: float32 [768, 768], P('dp', 'tensor')
- grad_b_value: float32 [768], P('tensor')
- grad_w_output: float32 [768, 768], P('tensor', 'dp')
- grad_b_output: float32 [768], replicated
- grad_gain_attn: float32 [768], replicated
- grad_shift_attn: float32 [768], replicated
- grad_w_inner: float32 [768, 3072], P('dp', 'tensor')
- grad_b_inner: float32 [3072], P('tensor')
- grad_w_outer: float32 [3072, 768], P('tensor', 'dp')
- grad_b_outer: float32 [768], replicated
- grad_gain_ffn: float32 [768], replicated
- grad_shift_ffn: float32 [768], replicated
The draws below stay inside these ranges and needn't reach their ends.
All inputs are finite; a program needn't handle non-finite values.
Results may differ from the reference program's by a relative error of at most 0.014.
Values sent between devices are 32-bit elements; how exact they have to be, the bound alone decides.
No kernel may reach another device: no remote copies, remote signals or barrier semaphores. Data moves between devices by JAX's collectives and lax.ppermute only.
A program may use at most 128 MiB of HBM per device.

```python
import jax
import jax.numpy as jnp
from jax import lax

D = 768
HEADS = 12
FF = 3072
HEAD_DIM = 64
LENGTH = 512
TOKENS = 16384


def level_of(stream_key, shape, pieces, low, top_value):
    level = 1.0
    for dim, blocks in pieces:
        heights = jax.random.uniform(jax.random.fold_in(jax.random.fold_in(stream_key, 6), dim), (blocks,), jnp.float32, low / len(pieces), top_value / len(pieces))
        level = level * jnp.repeat(jnp.exp(heights), shape[dim] // blocks).reshape((-1,) + (1,) * (len(shape) - 1 - dim))
    return level


def noise(stream_key, shape, spread, bound, pieces=(), kind=jnp.bfloat16):
    drawn = jax.random.normal(stream_key, shape, jnp.float32) * spread
    if len(pieces) > 0:
        drawn = level_of(stream_key, shape, pieces, -0.22, 0.18) * drawn
    return jnp.clip(drawn, min=-bound, max=bound).astype(kind)


def setup_inputs(seed: int = 0) -> dict:
    key_of = jax.random.split(jax.random.key(seed), 18)
    inputs = noise(key_of[0], (TOKENS, D), 1.0, 6.0, ((0, 8),))
    w_query = noise(key_of[1], (D, D), D ** -0.5, 0.21875, ((1, 4),))
    b_query = noise(key_of[2], (D,), 0.5, 3.0, ((0, 4),))
    w_key = noise(key_of[3], (D, D), D ** -0.5, 0.21875, ((1, 4),))
    w_value = noise(key_of[4], (D, D), D ** -0.5, 0.21875, ((1, 4),))
    b_value = noise(key_of[5], (D,), 0.5, 3.0, ((0, 4),))
    w_output = noise(key_of[6], (D, D), 1.0, 6.0, ((0, 4),))
    b_output = noise(key_of[7], (D,), 0.5, 3.0)
    gain_attn = jnp.clip(1.0 + 0.1 * jax.random.normal(key_of[8], (D,), jnp.float32), 0.5, 1.5).astype(jnp.bfloat16)
    shift_attn = noise(key_of[9], (D,), 0.5, 3.0)
    w_inner = noise(key_of[10], (D, FF), D ** -0.5, 0.21875, ((1, 4),))
    b_inner = noise(key_of[11], (FF,), 0.5, 3.0, ((0, 4),))
    w_outer = noise(key_of[12], (FF, D), FF ** -0.5, 0.109375, ((0, 4),))
    b_outer = noise(key_of[13], (D,), 0.5, 3.0)
    gain_ffn = jnp.clip(1.0 + 0.1 * jax.random.normal(key_of[14], (D,), jnp.float32), 0.5, 1.5).astype(jnp.bfloat16)
    shift_ffn = noise(key_of[15], (D,), 0.5, 3.0)
    cotangent = noise(key_of[16], (TOKENS, D), 1.0, 6.0, ((0, 8),))
    return {"inputs": inputs, "w_query": w_query, "b_query": b_query, "w_key": w_key, "w_value": w_value, "b_value": b_value, "w_output": w_output, "b_output": b_output, "gain_attn": gain_attn, "shift_attn": shift_attn, "w_inner": w_inner, "b_inner": b_inner, "w_outer": w_outer, "b_outer": b_outer, "gain_ffn": gain_ffn, "shift_ffn": shift_ffn, "cotangent": cotangent}


EPSILON = 1e-12
HIGH = lax.Precision.HIGHEST

@jax.custom_vjp
def low(v):
    return lax.optimization_barrier(v.astype(jnp.bfloat16)).astype(jnp.float32)

@jax.custom_vjp
def low_back(v):
    return v

def low_keep(v):
    return (low(v), None)

def low_pass(kept, grad):
    return (grad,)

def back_keep(v):
    return (v, None)

def back_low(kept, grad):
    return (low(grad),)
low.defvjp(low_keep, low_pass)
low_back.defvjp(back_keep, back_low)

def matmul(left, right):
    return jnp.dot(left, right, precision=HIGH)

def layer_norm(values, gain, shift):
    center = values - lax.optimization_barrier(jnp.mean(values, axis=-1, keepdims=True))
    variance = lax.optimization_barrier(jnp.mean(center * center, axis=-1, keepdims=True))
    return center * lax.rsqrt(variance + EPSILON) * gain + shift

def attend(triple):
    queries, key_rows, value_rows = triple
    scores = jnp.einsum('qhd,khd->hqk', queries, key_rows, precision=HIGH) * HEAD_DIM ** (-0.5)
    scores = low_back(scores)
    weights = jax.nn.softmax(scores, axis=-1)
    return jnp.einsum('hqk,khd->qhd', low(weights), value_rows, precision=HIGH)

def forward(inputs, w_query, b_query, w_key, w_value, b_value, w_output, b_output, gain_attn, shift_attn, w_inner, b_inner, w_outer, b_outer, gain_ffn, shift_ffn):
    rounded = low(inputs)
    queries = low(low_back(matmul(rounded, w_query) + b_query))
    key_rows = low(low_back(matmul(rounded, w_key)))
    value_rows = low(low_back(matmul(rounded, w_value) + b_value))
    split_shape = (-1, LENGTH, HEADS, HEAD_DIM)
    context = lax.map(jax.checkpoint(attend), (queries.reshape(split_shape), key_rows.reshape(split_shape), value_rows.reshape(split_shape)))
    context = low(low_back(context.reshape(inputs.shape[0], D)))
    attn = low_back(matmul(context, w_output) + b_output)
    hidden = layer_norm(inputs + attn, gain_attn, shift_attn)
    inner = low_back(matmul(low(hidden), w_inner) + b_inner)
    active = low(jax.nn.gelu(inner, approximate=False))
    outer = low_back(matmul(active, w_outer) + b_outer)
    return layer_norm(hidden + outer, gain_ffn, shift_ffn)

def reference(inputs, w_query, b_query, w_key, w_value, b_value, w_output, b_output, gain_attn, shift_attn, w_inner, b_inner, w_outer, b_outer, gain_ffn, shift_ffn, cotangent):
    params = tuple((item.astype(jnp.float32) for item in (inputs, w_query, b_query, w_key, w_value, b_value, w_output, b_output, gain_attn, shift_attn, w_inner, b_inner, w_outer, b_outer, gain_ffn, shift_ffn)))
    result, pullback = jax.vjp(forward, *params)
    grads = pullback(cotangent.astype(jnp.float32))
    return (result.astype(jnp.bfloat16), grads[0], grads[1], grads[2], grads[3], grads[4], grads[5], grads[6], grads[7], grads[8], grads[9], grads[10], grads[11], grads[12], grads[13], grads[14], grads[15])
```

```python
from functools import partial

import jax
import jax.numpy as jnp
from jax import lax
from jax.experimental import pallas as pl
from jax.experimental.pallas import tpu as pltpu
from jax.sharding import PartitionSpec as P

HEAD_DIM = 64
LENGTH = 512
EPSILON = 1e-12
F32 = jnp.float32
BF16 = jnp.bfloat16
LOG2E = 1.4426950408889634
SCALE = HEAD_DIM ** (-0.5)
fence = lax.optimization_barrier


def dot(left, right, dims):
    return lax.dot_general(left, right, (dims, ((), ())), preferred_element_type=F32)


ROWS = ((0,), (0,))
PLAIN = ((1,), (0,))
COLS = ((1,), (1,))


def norm_forward(values, gain, shift):
    center = values - jnp.mean(values, axis=-1, keepdims=True)
    inverse = lax.rsqrt(jnp.mean(center * center, axis=-1, keepdims=True) + EPSILON)
    normed = center * inverse
    return (normed * gain + shift, normed, inverse)


def norm_backward(upstream, gain, normed, inverse):
    scaled = upstream * gain
    first_mean = jnp.mean(scaled, axis=-1, keepdims=True)
    cross_mean = jnp.mean(scaled * normed, axis=-1, keepdims=True)
    grad_values = inverse * (scaled - first_mean - normed * cross_mean)
    return (grad_values, jnp.sum(upstream * normed, axis=0), jnp.sum(upstream, axis=0))


def attend_kernel(x_ref, wq_ref, wk_ref, wv_ref, bq_ref, bv_ref, out_ref):
    x = x_ref[...]
    q = (dot(x, wq_ref[...], PLAIN) + bq_ref[...]).astype(BF16)
    k = dot(x, wk_ref[...], PLAIN).astype(BF16)
    v = (dot(x, wv_ref[...], PLAIN) + bv_ref[...]).astype(BF16)
    for h in range(q.shape[1] // HEAD_DIM):
        cols = slice(h * HEAD_DIM, (h + 1) * HEAD_DIM)
        scores = dot(q[:, cols], k[:, cols], COLS)
        largest = jnp.max(scores, axis=-1, keepdims=True)
        expon = jnp.exp2((scores - largest) * (SCALE * LOG2E))
        totals = jnp.sum(expon, axis=-1, keepdims=True)
        context = dot(expon.astype(BF16), v[:, cols], PLAIN) / totals
        out_ref[:, cols] = context.astype(BF16).astype(F32)


def attend_forward(inputs, wq, bq, wk, wv, bv):
    rows, width = inputs.shape
    cols = wq.shape[1]
    whole = lambda a: pl.BlockSpec(a.shape, lambda i: (0, 0))
    args = (wq, wk, wv, bq, bv)
    flops = rows * (6 * width * cols + 4 * LENGTH * cols)
    return pl.pallas_call(
        attend_kernel,
        grid=(rows // LENGTH,),
        in_specs=[pl.BlockSpec((LENGTH, width), lambda i: (i, 0))] + [whole(a) for a in args],
        out_specs=pl.BlockSpec((LENGTH, cols), lambda i: (i, 0)),
        out_shape=jax.ShapeDtypeStruct((rows, cols), F32),
        cost_estimate=pl.CostEstimate(
            flops=flops, bytes_accessed=rows * (2 * width + 4 * cols), transcendentals=rows * LENGTH * 3
        ),
        compiler_params=pltpu.CompilerParams(vmem_limit_bytes=48 << 20),
        name="attend_forward",
    )(inputs, *args)


def attend_back_kernel(q_ref, k_ref, v_ref, g_ref, gq_ref, gk_ref, gv_ref):
    for h in range(q_ref.shape[1] // HEAD_DIM):
        cols = slice(h * HEAD_DIM, (h + 1) * HEAD_DIM)
        q, k, v, g = q_ref[:, cols], k_ref[:, cols], v_ref[:, cols], g_ref[:, cols]
        scores = dot(k, q, COLS)
        largest = jnp.max(scores, axis=0, keepdims=True)
        expon = jnp.exp2((scores - largest) * (SCALE * LOG2E))
        probs = expon * (1.0 / jnp.sum(expon, axis=0, keepdims=True))
        gv_ref[:, cols] = dot(probs.astype(BF16), g, PLAIN).astype(BF16)
        weighted = probs * dot(v, g, COLS)
        terms = jnp.sum(weighted, axis=0, keepdims=True)
        grad_scores = (weighted - probs * terms).astype(BF16)
        gq_ref[:, cols] = (dot(grad_scores, k, ROWS) * SCALE).astype(BF16)
        gk_ref[:, cols] = (dot(grad_scores, q, PLAIN) * SCALE).astype(BF16)


def attend_backward(q, k, v, g):
    rows, width = q.shape
    spec = pl.BlockSpec((LENGTH, 2 * HEAD_DIM), lambda i, j: (i, j))
    return pl.pallas_call(
        attend_back_kernel,
        grid=(rows // LENGTH, width // (2 * HEAD_DIM)),
        in_specs=[spec] * 4,
        out_specs=[spec] * 3,
        out_shape=[jax.ShapeDtypeStruct((rows, width), BF16)] * 3,
        cost_estimate=pl.CostEstimate(
            flops=rows * 10 * LENGTH * width,
            bytes_accessed=rows * width * 14,
            transcendentals=rows * LENGTH * (width // HEAD_DIM),
        ),
        compiler_params=pltpu.CompilerParams(vmem_limit_bytes=48 << 20),
        name="attend_backward",
    )(q, k, v, g)


def narrow_kernel(x_ref, out_ref):
    out_ref[...] = x_ref[...].reshape(out_ref.shape).astype(BF16)


def narrow(values, block_rows):
    rows, width = values.shape
    spec = pl.BlockSpec((block_rows, width), lambda i: (i, 0))
    return pl.pallas_call(
        narrow_kernel,
        grid=(rows // block_rows,),
        in_specs=[spec],
        out_specs=spec,
        out_shape=jax.ShapeDtypeStruct((rows, width), BF16),
        cost_estimate=pl.CostEstimate(flops=0, bytes_accessed=6 * rows * width, transcendentals=0),
        name="narrow",
    )(values)


def narrow_pieces(pieces):
    dp, tensor, share, width = pieces.shape
    if share % 8:
        whole = pieces.swapaxes(0, 1).reshape(tensor * dp * share, width)
        return narrow(whole, dp * share).reshape(tensor, dp * share, width)
    return pl.pallas_call(
        narrow_kernel,
        grid=(tensor,),
        in_specs=[pl.BlockSpec((dp, None, share, width), lambda i: (0, i, 0, 0))],
        out_specs=pl.BlockSpec((None, dp * share, width), lambda i: (i, 0, 0)),
        out_shape=jax.ShapeDtypeStruct((tensor, dp * share, width), BF16),
        cost_estimate=pl.CostEstimate(flops=0, bytes_accessed=6 * pieces.size, transcendentals=0),
        name="narrow_pieces",
    )(pieces)


def beside_kernel(x_ref, out_ref):
    out_ref[...] = jnp.concatenate([x_ref[i] for i in range(x_ref.shape[0])], axis=1).astype(BF16)


def narrow_beside(values):
    tensor, rows, cols = values.shape
    return pl.pallas_call(
        beside_kernel,
        out_shape=jax.ShapeDtypeStruct((rows, tensor * cols), BF16),
        cost_estimate=pl.CostEstimate(flops=0, bytes_accessed=6 * values.size, transcendentals=0),
        name="narrow_beside",
    )(values)


def gather_weight(local, dp, tensor):
    rows, width = local.shape
    share = rows // dp
    piece = lax.dynamic_slice_in_dim(local, lax.axis_index("dp") * share, share, 0).astype(F32)
    full = lax.all_gather(piece, ("dp", "tensor"), axis=0)
    return narrow_pieces(full.reshape(dp, tensor, share, width))


def scatter_grad(grad, tensor):
    part = lax.psum_scatter(grad, "dp", scatter_dimension=0, tiled=True)
    part = part.reshape(part.shape[0], tensor, -1).swapaxes(0, 1)
    return lax.psum_scatter(part, "tensor", scatter_dimension=0, tiled=False)


def shards(
    dp,
    tensor,
    inputs,
    w_query,
    b_query,
    w_key,
    w_value,
    b_value,
    w_output,
    b_output,
    gain_attn,
    shift_attn,
    w_inner,
    b_inner,
    w_outer,
    b_outer,
    gain_ffn,
    shift_ffn,
    cotangent,
):
    tok_rows, width = inputs.shape
    own_rows = tok_rows // tensor
    heads_cols = w_query.shape[1]
    ff_cols = w_inner.shape[1]
    z = lax.axis_index("tensor")
    own = lambda a: lax.dynamic_slice_in_dim(a, z * own_rows, own_rows, 0)
    row = lambda a: a.astype(F32)[None, :]

    lens = (heads_cols, heads_cols, ff_cols)
    vectors = jnp.concatenate([b_query, b_value, b_inner]).astype(F32)
    vectors = lax.all_gather(vectors, "tensor", axis=0)
    bq_full = vectors[:, :heads_cols].reshape(1, -1)
    bv_full = vectors[:, heads_cols : 2 * heads_cols].reshape(1, -1)
    bi_full = vectors[:, 2 * heads_cols :].reshape(1, -1)

    wo_full = gather_weight(w_output, dp, tensor).reshape(-1, width)
    wi_full = gather_weight(w_inner, dp, tensor)
    wu_full = gather_weight(w_outer, dp, tensor)
    qkv_local = jnp.concatenate([w_query.T, w_key.T, w_value.T], axis=0)
    qkv_full = gather_weight(qkv_local, dp, tensor).reshape(tensor, 3, heads_cols, width)
    wq_t, wk_t, wv_t = (qkv_full[:, i].reshape(-1, width) for i in range(3))

    context = attend_forward(inputs, w_query, row(b_query), w_key, w_value, row(b_value))
    context = context.reshape(tensor, own_rows, heads_cols)
    context = narrow_beside(lax.all_to_all(context, "tensor", 0, 0, tiled=True))


    x = own(inputs)
    gain_one, gain_two = row(gain_attn), row(gain_ffn)
    attn = dot(context, wo_full, PLAIN) + row(b_output)
    hidden, normed_attn, inverse_attn = norm_forward(x.astype(F32) + attn, gain_one, row(shift_attn))
    hidden_bf = hidden.astype(BF16)
    inner = jnp.concatenate([dot(hidden_bf, wi_full[i], PLAIN) for i in range(tensor)], axis=1) + bi_full
    active, gelu_pull = jax.vjp(partial(jax.nn.gelu, approximate=False), inner)
    active_bf = active.astype(BF16)
    outer = dot(active_bf, wu_full.reshape(-1, width), PLAIN) + row(b_outer)
    layer_out, normed_ffn, inverse_ffn = norm_forward(hidden + outer, gain_two, row(shift_ffn))
    layer_out = narrow(lax.all_gather(layer_out, "tensor", axis=0, tiled=True), own_rows)

    upstream = own(cotangent).astype(F32)
    grad_resid2, grad_gain_ffn, grad_shift_ffn = norm_backward(upstream, gain_two, normed_ffn, inverse_ffn)
    grad_outer = grad_resid2.astype(BF16)
    grad_b_outer = jnp.sum(grad_outer.astype(F32), axis=0)
    grad_active = dot(grad_outer, wu_full.reshape(-1, width), COLS)
    grad_inner = gelu_pull(grad_active)[0].astype(BF16)
    grad_b_inner = jnp.sum(grad_inner.astype(F32), axis=0)
    gu = scatter_grad(dot(grad_outer, active_bf, ROWS), tensor)
    gi = scatter_grad(dot(hidden_bf, grad_inner, ROWS), tensor)
    back = sum(dot(grad_inner[:, i * ff_cols : (i + 1) * ff_cols], wi_full[i], COLS) for i in range(tensor))
    grad_hidden = grad_resid2 + back
    grad_resid1, grad_gain_attn, grad_shift_attn = norm_backward(
        grad_hidden, gain_one, normed_attn, inverse_attn
    )
    grad_attn = grad_resid1.astype(BF16)
    grad_b_output = jnp.sum(grad_attn.astype(F32), axis=0)
    go = scatter_grad(dot(grad_attn, context, ROWS), tensor)
    grad_context = dot(grad_attn, wo_full, COLS).astype(BF16)

    queries = (dot(x, wq_t, COLS) + bq_full).astype(BF16)
    key_rows = dot(x, wk_t, COLS).astype(BF16)
    value_rows = (dot(x, wv_t, COLS) + bv_full).astype(BF16)
    grad_q, grad_k, grad_v = attend_backward(queries, key_rows, value_rows, grad_context)
    grad_x = grad_resid1 + dot(grad_q, wq_t, PLAIN) + dot(grad_k, wk_t, PLAIN) + dot(grad_v, wv_t, PLAIN)
    grad_inputs = lax.all_gather(grad_x, "tensor", axis=0, tiled=True)
    gq, gk, gv = (scatter_grad(dot(x, g, ROWS), tensor) for g in (grad_q, grad_k, grad_v))
    sums = lax.psum(
        jnp.concatenate(
            [
                jnp.sum(grad_q.astype(F32), axis=0),
                jnp.sum(grad_v.astype(F32), axis=0),
                grad_b_inner,
                grad_b_output,
                grad_gain_attn,
                grad_shift_attn,
                grad_b_outer,
                grad_gain_ffn,
                grad_shift_ffn,
            ]
        ),
        ("dp", "tensor"),
    )
    mine = lambda a, n: lax.dynamic_slice_in_dim(a, z * n, n, 0)
    edges = [0, width, 2 * width, 2 * width + ff_cols * tensor]
    s_bq, s_bv, s_bi = (sums[edges[i] : edges[i + 1]] for i in range(3))
    rest = sums[edges[3] :].reshape(6, width)
    return (
        layer_out,
        grad_inputs,
        gq,
        mine(s_bq, heads_cols),
        gk,
        gv,
        mine(s_bv, heads_cols),
        go.T,
        rest[0],
        rest[1],
        rest[2],
        gi,
        mine(s_bi, ff_cols),
        gu.T,
        rest[3],
        rest[4],
        rest[5],
    )


def solution(mesh):
    wide, tall, vector = P(None, "tensor"), P("tensor", None), P("tensor")
    tokens, both = P("dp", None), P("dp", "tensor")
    in_specs = (
        tokens, wide, vector, wide, wide, vector, tall, P(), P(), P(), wide, vector, tall, P(), P(), P(), tokens,
    )
    out_specs = (
        tokens, tokens, both, vector, both, both, vector, P("tensor", "dp"), P(), P(), P(), both, vector,
        P("tensor", "dp"), P(), P(), P(),
    )
    body = partial(shards, mesh.shape["dp"], mesh.shape["tensor"])
    return jax.shard_map(body, mesh=mesh, in_specs=in_specs, out_specs=out_specs, check_vma=False)
```

```python
from functools import partial

import jax
import jax.numpy as jnp
from jax import lax
from jax.experimental import pallas as pl
from jax.experimental.pallas import tpu as pltpu
from jax.sharding import PartitionSpec as P

HEAD_DIM = 64
LENGTH = 512
EPSILON = 1e-12
F32 = jnp.float32
BF16 = jnp.bfloat16
SCALE = HEAD_DIM ** (-0.5)
EXP_SCALE = SCALE * 1.4426950408889634
ROWS = ((0,), (0,))
PLAIN = ((1,), (0,))
COLS = ((1,), (1,))


def dot(left, right, dims):
    return lax.dot_general(left, right, (dims, ((), ())), preferred_element_type=F32)


def norm_forward(values, gain, shift):
    center = values - jnp.mean(values, axis=-1, keepdims=True)
    inverse = lax.rsqrt(jnp.mean(center * center, axis=-1, keepdims=True) + EPSILON)
    normed = center * inverse
    return (normed * gain + shift, normed, inverse)


def norm_backward(upstream, gain, normed, inverse):
    scaled = upstream * gain
    first_mean = jnp.mean(scaled, axis=-1, keepdims=True)
    cross_mean = jnp.mean(scaled * normed, axis=-1, keepdims=True)
    return inverse * (scaled - first_mean - normed * cross_mean)


def row_sums(values):
    return jnp.sum(values, axis=0, keepdims=True)


def call(kernel, name, grid, ins, outs, flops, exps=0, scratch=(), prefetch=None):
    moved = sum(a.size * a.dtype.itemsize for a, _, _ in ins)
    moved += sum(jnp.dtype(t).itemsize * functools_prod(s) for s, t, _, _ in outs)
    return pl.pallas_call(
        kernel,
        grid=grid,
        in_specs=[pl.BlockSpec(b, m) for _, b, m in ins],
        out_specs=[pl.BlockSpec(b, m) for _, _, b, m in outs],
        out_shape=[jax.ShapeDtypeStruct(s, t) for s, t, _, _ in outs],
        scratch_shapes=list(scratch),
        cost_estimate=pl.CostEstimate(flops=flops, bytes_accessed=moved, transcendentals=exps),
        compiler_params=pltpu.CompilerParams(vmem_limit_bytes=56 << 20),
        name=name,
    )(*(a for a, _, _ in ins))


def functools_prod(shape):
    total = 1
    for n in shape:
        total *= n
    return total


def attend_kernel(x_ref, w_ref, bias_ref, bo_ref, gain_ref, shift_ref, qkv_ref, ctx_ref, hid_ref, nrm_ref, inv_ref):
    slot = pl.program_id(1)
    cols = ctx_ref.shape[-1]
    x = x_ref[...]
    qkv = (dot(x, w_ref[: 3 * cols], COLS) + bias_ref[...]).astype(BF16)
    qkv_ref[...] = qkv
    parts = []
    for h in range(cols // HEAD_DIM):
        q, k, v = (qkv[:, i * cols + h * HEAD_DIM : i * cols + (h + 1) * HEAD_DIM] for i in range(3))
        scores = dot(q, k, COLS)
        largest = jnp.max(scores, axis=-1, keepdims=True)
        expon = jnp.exp2((scores - largest) * EXP_SCALE)
        totals = jnp.sum(expon, axis=-1, keepdims=True)
        parts.append((dot(expon.astype(BF16), v, PLAIN) / totals).astype(BF16))
    context = jnp.concatenate(parts, axis=1)
    ctx_ref[...] = context
    attn = dot(context, w_ref[3 * cols :], PLAIN)

    @pl.when(slot == 0)
    def _():
        hid_ref[...] = attn

    @pl.when(slot > 0)
    def _():
        hid_ref[...] += attn

    @pl.when(slot == pl.num_programs(1) - 1)
    def _():
        values = x.astype(F32) + hid_ref[...] + bo_ref[...]
        hidden, normed, inverse = norm_forward(values, gain_ref[...], shift_ref[...])
        hid_ref[...] = hidden
        nrm_ref[...] = normed
        inv_ref[...] = inverse


def attend_forward(x, weights, bias, b_output, gain, shift):
    rows, width = x.shape
    slots = weights.shape[0]
    cols = width // slots
    mine = lambda i, j: (i, 0)
    flat = lambda i, j: (0, 0)
    token = (LENGTH, width)
    vec = (1, width)
    return call(
        attend_kernel,
        "attend_forward",
        (rows // LENGTH, slots),
        [
            (x, token, mine),
            (weights, (None, width, width), lambda i, j: (j, 0, 0)),
            (bias, (None, 1, 3 * cols), lambda i, j: (j, 0, 0)),
            (b_output, vec, flat),
            (gain, vec, flat),
            (shift, vec, flat),
        ],
        [
            ((slots, rows, 3 * cols), BF16, (None, LENGTH, 3 * cols), lambda i, j: (j, i, 0)),
            ((slots, rows, cols), BF16, (None, LENGTH, cols), lambda i, j: (j, i, 0)),
            ((rows, width), F32, token, mine),
            ((rows, width), F32, token, mine),
            ((rows, 1), F32, (LENGTH, 1), mine),
        ],
        flops=rows * width * (8 * width + 4 * LENGTH),
        exps=rows * LENGTH * (width // HEAD_DIM),
    )


def attend_back_kernel(ga_ref, gr_ref, qkv_ref, w_ref, gqkv_ref, gx_ref, sum_ref):
    slot = pl.program_id(1)
    cols = qkv_ref.shape[-1] // 3
    gctx = dot(ga_ref[...], w_ref[3 * cols :], COLS).astype(BF16)
    for h in range(cols // HEAD_DIM):
        at = [slice(i * cols + h * HEAD_DIM, i * cols + (h + 1) * HEAD_DIM) for i in range(3)]
        q, k, v = (qkv_ref[:, s] for s in at)
        g = gctx[:, at[0]]
        scores = dot(k, q, COLS)
        largest = jnp.max(scores, axis=0, keepdims=True)
        expon = jnp.exp2((scores - largest) * EXP_SCALE)
        probs = expon * (1.0 / row_sums(expon))
        gqkv_ref[:, at[2]] = dot(probs.astype(BF16), g, PLAIN).astype(BF16)
        weighted = probs * dot(v, g, COLS)
        grad_scores = (weighted - probs * row_sums(weighted)).astype(BF16)
        gqkv_ref[:, at[0]] = (dot(grad_scores, k, ROWS) * SCALE).astype(BF16)
        gqkv_ref[:, at[1]] = (dot(grad_scores, q, PLAIN) * SCALE).astype(BF16)
    grads = gqkv_ref[...]
    sums = row_sums(grads.astype(F32))
    back = dot(grads, w_ref[: 3 * cols], PLAIN)
    sum_ref[...] = sums

    @pl.when(slot == 0)
    def _():
        gx_ref[...] = gr_ref[...] + back

    @pl.when(slot > 0)
    def _():
        gx_ref[...] += back


def attend_backward(grad_attn, grad_resid, qkv, weights):
    rows, width = grad_attn.shape
    slots = weights.shape[0]
    cols = width // slots
    mine = lambda i, j: (i, 0)
    token = (LENGTH, width)
    heads = (None, LENGTH, 3 * cols)
    return call(
        attend_back_kernel,
        "attend_backward",
        (rows // LENGTH, slots),
        [
            (grad_attn, token, mine),
            (grad_resid, token, mine),
            (qkv, heads, lambda i, j: (j, i, 0)),
            (weights, (None, width, width), lambda i, j: (j, 0, 0)),
        ],
        [
            ((slots, rows, 3 * cols), BF16, heads, lambda i, j: (j, i, 0)),
            ((rows, width), F32, token, mine),
            ((rows // LENGTH, slots, 1, 3 * cols), F32, (None, None, 1, 3 * cols), lambda i, j: (i, j, 0, 0)),
        ],
        flops=rows * width * (8 * width + 10 * LENGTH),
        exps=rows * LENGTH * (width // HEAD_DIM),
    )


def inner_kernel(h_ref, w_ref, b_ref, act_ref, slope_ref):
    inner = dot(h_ref[...].astype(BF16), w_ref[...], PLAIN) + b_ref[...]
    phi = 0.5 + 0.5 * lax.erf(inner * (0.5**0.5))
    bell = jnp.exp2(inner * inner * (-0.5 * 1.4426950408889634)) * 0.3989422804014327
    act_ref[...] = (inner * phi).astype(BF16)
    slope_ref[...] = phi + inner * bell


def inner_forward(hidden, weights, bias):
    rows, width = hidden.shape
    slots, _, units = weights.shape
    slot = lambda i, j: (i, j, 0)
    block = LENGTH // 2
    return call(
        inner_kernel,
        "inner_forward",
        (slots, rows // block),
        [
            (hidden, (block, width), lambda i, j: (j, 0)),
            (weights, (None, width, units), lambda i, j: (i, 0, 0)),
            (bias, (None, 1, units), lambda i, j: (i, 0, 0)),
        ],
        [
            ((slots, rows, units), BF16, (None, block, units), slot),
            ((slots, rows, units), F32, (None, block, units), slot),
        ],
        flops=2 * rows * width * slots * units,
        exps=2 * rows * slots * units,
    )


def outer_kernel(act_ref, w_ref, hid_ref, cot_ref, bo_ref, gain_ref, shift_ref, out_ref, gr_ref, go_ref, sum_ref):
    slot = pl.program_id(1)
    outer = dot(act_ref[...], w_ref[...], PLAIN)

    @pl.when(slot == 0)
    def _():
        out_ref[...] = outer

    @pl.when(slot > 0)
    def _():
        out_ref[...] += outer

    @pl.when(slot == pl.num_programs(1) - 1)
    def _():
        gain = gain_ref[...]
        values = hid_ref[...] + (out_ref[...] + bo_ref[...])
        layer_out, normed, inverse = norm_forward(values, gain, shift_ref[...])
        out_ref[...] = layer_out
        upstream = cot_ref[...].astype(F32)
        grad = norm_backward(upstream, gain, normed, inverse)
        rounded = grad.astype(BF16)
        gr_ref[...] = grad
        go_ref[...] = rounded
        sum_ref[0:1] = row_sums(upstream * normed)
        sum_ref[1:2] = row_sums(upstream)
        sum_ref[2:3] = row_sums(rounded.astype(F32))


def outer_forward(active, weights, hidden, cotangent, b_outer, gain, shift):
    rows, width = hidden.shape
    slots, units, _ = weights.shape
    mine = lambda i, j: (i, 0)
    flat = lambda i, j: (0, 0)
    token = (LENGTH, width)
    vec = (1, width)
    return call(
        outer_kernel,
        "outer_forward",
        (rows // LENGTH, slots),
        [
            (active, (None, LENGTH, units), lambda i, j: (j, i, 0)),
            (weights, (None, units, width), lambda i, j: (j, 0, 0)),
            (hidden, token, mine),
            (cotangent, token, mine),
            (b_outer, vec, flat),
            (gain, vec, flat),
            (shift, vec, flat),
        ],
        [
            ((rows, width), F32, token, mine),
            ((rows, width), F32, token, mine),
            ((rows, width), BF16, token, mine),
            ((rows // LENGTH, 8, width), F32, (None, 8, width), lambda i, j: (i, 0, 0)),
        ],
        flops=2 * rows * width * slots * units,
    )


def inner_back_kernel(go_ref, wu_ref, slope_ref, wi_ref, gr_ref, nrm_ref, inv_ref, gain_ref,
                      gi_ref, g1_ref, ga_ref, bsum_ref, sum_ref):
    slot = pl.program_id(1)
    grad_inner = (dot(go_ref[...], wu_ref[...], COLS) * slope_ref[...]).astype(BF16)
    gi_ref[...] = grad_inner
    bsum_ref[...] = row_sums(grad_inner.astype(F32))
    back = dot(grad_inner, wi_ref[...], COLS)

    @pl.when(slot == 0)
    def _():
        g1_ref[...] = gr_ref[...] + back

    @pl.when(slot > 0)
    def _():
        g1_ref[...] += back

    @pl.when(slot == pl.num_programs(1) - 1)
    def _():
        upstream, normed = g1_ref[...], nrm_ref[...]
        grad = norm_backward(upstream, gain_ref[...], normed, inv_ref[...])
        rounded = grad.astype(BF16)
        g1_ref[...] = grad
        ga_ref[...] = rounded
        sum_ref[0:1] = row_sums(upstream * normed)
        sum_ref[1:2] = row_sums(upstream)
        sum_ref[2:3] = row_sums(rounded.astype(F32))


def inner_backward(grad_outer, w_outer, slope, w_inner, grad_resid2, normed, inverse, gain):
    rows, width = grad_outer.shape
    slots, units, _ = w_outer.shape
    mine = lambda i, j: (i, 0)
    token = (LENGTH, width)
    slot = lambda i, j: (j, i, 0)
    weight = lambda i, j: (j, 0, 0)
    return call(
        inner_back_kernel,
        "inner_backward",
        (rows // LENGTH, slots),
        [
            (grad_outer, token, mine),
            (w_outer, (None, units, width), weight),
            (slope, (None, LENGTH, units), slot),
            (w_inner, (None, width, units), weight),
            (grad_resid2, token, mine),
            (normed, token, mine),
            (inverse, (LENGTH, 1), mine),
            (gain, (1, width), lambda i, j: (0, 0)),
        ],
        [
            ((slots, rows, units), BF16, (None, LENGTH, units), slot),
            ((rows, width), F32, token, mine),
            ((rows, width), BF16, token, mine),
            ((rows // LENGTH, slots, 1, units), F32, (None, None, 1, units), lambda i, j: (i, j, 0, 0)),
            ((rows // LENGTH, 8, width), F32, (None, 8, width), lambda i, j: (i, 0, 0)),
        ],
        flops=4 * rows * width * slots * units,
    )


def narrow_kernel(x_ref, out_ref):
    out_ref[...] = x_ref[...].astype(BF16)


def narrow(values, block_rows):
    rows, width = values.shape
    at = lambda i: (i, 0)
    block = (block_rows, width)
    out = ((rows, width), BF16, block, at)
    return call(narrow_kernel, "narrow", (rows // block_rows,), [(values, block, at)], [out], 0)[0]


def shift_to(values, tensor, k):
    return lax.ppermute(values, "tensor", [(i, (i + k) % tensor) for i in range(tensor)])


def flip(values, bit):
    return lax.ppermute(values, "dp", [(i, i ^ bit) for i in range(8)])


def assemble_kernel(where_ref, local_ref, *refs):
    *pieces, out_ref, hold, sems = refs
    share = pieces[0].shape[1]
    copies = []
    for n, piece in enumerate(pieces):
        start = pl.multiple_of(where_ref[n], 8)
        copies.append(pltpu.make_async_copy(piece, hold.at[:, pl.ds(start, share)], sems.at[n]))
        copies[-1].start()
    out_ref[0] = local_ref[...]
    for copy in copies:
        copy.wait()
    for k in range(hold.shape[0]):
        out_ref[k + 1] = hold[k].astype(BF16)


def assemble(local, where, pieces):
    rows, width = local.shape
    others = pieces[0].shape[0]
    out = (others + 1, rows, width)
    return pl.pallas_call(
        assemble_kernel,
        in_specs=[pl.BlockSpec(memory_space=pltpu.SMEM), pl.BlockSpec(memory_space=pltpu.VMEM)]
        + [pl.BlockSpec(memory_space=pl.ANY)] * len(pieces),
        out_specs=pl.BlockSpec(memory_space=pltpu.VMEM),
        out_shape=jax.ShapeDtypeStruct(out, BF16),
        scratch_shapes=[pltpu.VMEM((others, rows, width), F32), pltpu.SemaphoreType.DMA((len(pieces),))],
        cost_estimate=pl.CostEstimate(flops=0, bytes_accessed=others * rows * width * 6, transcendentals=0),
        compiler_params=pltpu.CompilerParams(vmem_limit_bytes=56 << 20),
        name="assemble",
    )(where, local, *pieces)


def gather_weight(local, dp, tensor):
    rows, width = local.shape
    share = rows // dp
    me = lax.axis_index("dp")
    piece = lax.dynamic_slice_in_dim(local, me * share, share, 0).astype(F32)
    slots = jnp.stack([shift_to(piece, tensor, k) for k in range(1, tensor)])
    if dp != 8 or share % 16:
        full = lax.all_gather(slots, "dp", axis=1).reshape((tensor - 1) * rows, width)
        full = narrow(full, rows).reshape(tensor - 1, rows, width)
        return jnp.concatenate([local[None], full], axis=0)
    half = share // 2
    first = {0: slots[:, :half]}
    second = {0: slots[:, half:]}
    for held, order in ((first, (2, 4)), (second, (4, 2))):
        for bit in order + (1,):
            for rel in list(held):
                held[rel | bit] = flip(held[rel], bit)
    pieces, where = [], []
    for held, offset in ((first, 0), (second, half)):
        for rel, array in held.items():
            pieces.append(array)
            where.append((me ^ rel) * share + offset)
    return assemble(local, jnp.stack(where), pieces)


def slot_sum(part, tensor):
    total = part[0]
    for k in range(1, tensor):
        total = total + shift_to(part[k], tensor, tensor - k)
    return total


def block_order(width):
    me = lax.axis_index("dp")
    share = width // 8
    rel = jnp.array([7, 5, 3, 1, 6, 4, 2, 0])
    position = lax.broadcasted_iota(jnp.int32, (width, width), 1)
    source = (me ^ rel[jnp.arange(width) // share]) * share + jnp.arange(width) % share
    del position
    return (lax.broadcasted_iota(jnp.int32, (width, width), 0) == source[None, :]).astype(BF16)


def scatter_grad(left, rights, order, dp, tensor):
    width = left.shape[1]
    share = width // dp
    right = jnp.concatenate(list(rights), axis=1)
    cols = right.shape[1] // tensor
    if order is None:
        part = lax.psum_scatter(dot(left, right, ROWS), "dp", scatter_dimension=0, tiled=True)
    else:
        left = dot(left, order, PLAIN).astype(BF16)
        send = dot(left[:, : 4 * share], right, ROWS)
        keep = dot(left[:, 4 * share :], right, ROWS)
        held = keep + flip(send, 1)
        mid = right.shape[1] // 2
        a, b = held[:, :mid], held[:, mid:]
        pick = lambda v, i: v[i * share : (i + 1) * share]
        a_send = jnp.concatenate([pick(a, 0), pick(a, 2)], axis=0)
        a_keep = jnp.concatenate([pick(a, 1), pick(a, 3)], axis=0)
        a = a_keep + flip(a_send, 2)
        b = b[2 * share :] + flip(b[: 2 * share], 4)
        a = pick(a, 1) + flip(pick(a, 0), 4)
        b = pick(b, 1) + flip(pick(b, 0), 2)
        part = jnp.concatenate([a, b], axis=1)
    return slot_sum([part[:, k * cols : (k + 1) * cols] for k in range(tensor)], tensor)


def shards(
    dp,
    tensor,
    inputs,
    w_query,
    b_query,
    w_key,
    w_value,
    b_value,
    w_output,
    b_output,
    gain_attn,
    shift_attn,
    w_inner,
    b_inner,
    w_outer,
    b_outer,
    gain_ffn,
    shift_ffn,
    cotangent,
):
    tok_rows, width = inputs.shape
    own_rows = tok_rows // tensor
    cols = w_query.shape[1]
    z = lax.axis_index("tensor")
    own = lambda a: lax.dynamic_slice_in_dim(a, z * own_rows, own_rows, 0)
    row = lambda a: a.astype(F32)[None, :]

    vectors = row(jnp.concatenate([b_query, jnp.zeros_like(b_query), b_value, b_inner]))
    vectors = jnp.stack([vectors] + [shift_to(vectors, tensor, k) for k in range(1, tensor)])
    qkv_bias, inner_bias = vectors[..., : 3 * cols], vectors[..., 3 * cols :]

    attn_local = jnp.concatenate([w_query.T, w_key.T, w_value.T, w_output], axis=0)
    attn_full = gather_weight(attn_local, dp, tensor)
    inner_full = gather_weight(w_inner, dp, tensor)
    outer_full = gather_weight(w_outer, dp, tensor)

    x, gain_one, gain_two = own(inputs), row(gain_attn), row(gain_ffn)
    qkv, context, hidden, normed, inverse = attend_forward(
        x, attn_full, qkv_bias, row(b_output), gain_one, row(shift_attn)
    )
    active, slope = inner_forward(hidden, inner_full, inner_bias)
    layer_out, grad_resid2, grad_outer, sums_two = outer_forward(
        active, outer_full, hidden, own(cotangent), row(b_outer), gain_two, row(shift_ffn)
    )
    layer_out = narrow(lax.all_gather(layer_out, "tensor", axis=0, tiled=True), own_rows)

    order = block_order(width) if dp == 8 and width % 64 == 0 else None
    gu = scatter_grad(grad_outer, active, order, dp, tensor)
    grad_inner, grad_resid1, grad_attn, inner_sums, sums_one = inner_backward(
        grad_outer, outer_full, slope, inner_full, grad_resid2, normed, inverse, gain_one
    )
    gi = scatter_grad(hidden.astype(BF16), grad_inner, order, dp, tensor)
    go = scatter_grad(grad_attn, context, order, dp, tensor)
    grad_qkv, grad_x, qkv_sums = attend_backward(grad_attn, grad_resid1, qkv, attn_full)
    grad_inputs = lax.all_gather(grad_x, "tensor", axis=0, tiled=True)
    gqkv = scatter_grad(x, grad_qkv, order, dp, tensor)

    by_slot = jnp.concatenate([jnp.sum(qkv_sums, axis=0), jnp.sum(inner_sums, axis=0)], axis=-1)
    by_place = by_slot[(z - jnp.arange(tensor)) % tensor].reshape(-1)
    rest = jnp.concatenate([jnp.sum(sums_one, axis=0)[:3], jnp.sum(sums_two, axis=0)[:3]]).reshape(-1)
    sums = lax.psum(jnp.concatenate([by_place, rest]), ("dp", "tensor"))
    span = by_place.shape[0] // tensor
    mine = lax.dynamic_slice_in_dim(sums, z * span, span, 0)
    rest = sums[by_place.shape[0] :].reshape(6, width)
    return (
        layer_out,
        grad_inputs,
        gqkv[:, :cols],
        mine[:cols],
        gqkv[:, cols : 2 * cols],
        gqkv[:, 2 * cols :],
        mine[2 * cols : 3 * cols],
        go.T,
        rest[2],
        rest[0],
        rest[1],
        gi,
        mine[3 * cols :],
        gu.T,
        rest[5],
        rest[3],
        rest[4],
    )


def solution(mesh):
    wide, tall, vector = P(None, "tensor"), P("tensor", None), P("tensor")
    tokens, both = P("dp", None), P("dp", "tensor")
    in_specs = (
        tokens, wide, vector, wide, wide, vector, tall, P(), P(), P(), wide, vector, tall, P(), P(), P(), tokens,
    )
    out_specs = (
        tokens, tokens, both, vector, both, both, vector, P("tensor", "dp"), P(), P(), P(), both, vector,
        P("tensor", "dp"), P(), P(), P(),
    )
    body = partial(shards, mesh.shape["dp"], mesh.shape["tensor"])
    return jax.shard_map(body, mesh=mesh, in_specs=in_specs, out_specs=out_specs, check_vma=False)
```

```python
import math
from functools import partial

import jax
import jax.numpy as jnp
from jax import lax
from jax.experimental import pallas as pl
from jax.experimental.pallas import tpu as pltpu
from jax.sharding import PartitionSpec as P

HEAD_DIM = 64
LENGTH = 512
EPSILON = 1e-12
F32 = jnp.float32
BF16 = jnp.bfloat16
SCALE = HEAD_DIM ** (-0.5)
EXP_SCALE = SCALE * 1.4426950408889634
ROWS = ((0,), (0,))
PLAIN = ((1,), (0,))
COLS = ((1,), (1,))


def dot(left, right, dims):
    return lax.dot_general(left, right, (dims, ((), ())), preferred_element_type=F32)


def norm_forward(values, gain, shift):
    center = values - jnp.mean(values, axis=-1, keepdims=True)
    inverse = lax.rsqrt(jnp.mean(center * center, axis=-1, keepdims=True) + EPSILON)
    normed = center * inverse
    return (normed * gain + shift, normed, inverse)


def norm_backward(upstream, gain, normed, inverse):
    scaled = upstream * gain
    first_mean = jnp.mean(scaled, axis=-1, keepdims=True)
    cross_mean = jnp.mean(scaled * normed, axis=-1, keepdims=True)
    return inverse * (scaled - first_mean - normed * cross_mean)


def row_sums(values):
    return jnp.sum(values, axis=0, keepdims=True)


def size_of(shape, dtype):
    return math.prod(shape) * jnp.dtype(dtype).itemsize


def call(kernel, name, grid, ins, outs, flops, exps=0, scratch=(), prefetch=None, moved=None):
    if moved is None:
        moved = sum(size_of(a.shape, a.dtype) for a, _, _ in ins) + sum(size_of(s, t) for s, t, _, _ in outs)
    lead = () if prefetch is None else (prefetch,)
    return pl.pallas_call(
        kernel,
        grid_spec=pltpu.PrefetchScalarGridSpec(
            num_scalar_prefetch=len(lead),
            grid=grid,
            in_specs=[pl.BlockSpec(b, m) for _, b, m in ins],
            out_specs=[pl.BlockSpec(b, m) for _, _, b, m in outs],
            scratch_shapes=list(scratch),
        ),
        out_shape=[jax.ShapeDtypeStruct(s, t) for s, t, _, _ in outs],
        cost_estimate=pl.CostEstimate(flops=flops, bytes_accessed=moved, transcendentals=exps),
        compiler_params=pltpu.CompilerParams(vmem_limit_bytes=56 << 20),
        name=name,
    )(*lead, *(a for a, _, _ in ins))


def attend_kernel(x_ref, w_ref, bias_ref, ctx_ref):
    cols = w_ref.shape[0] // 3
    parts = []
    qkv = (dot(x_ref[...], w_ref[...], COLS) + bias_ref[...]).astype(BF16)
    for h in range(cols // HEAD_DIM):
        q, k, v = (qkv[:, i * cols + h * HEAD_DIM : i * cols + (h + 1) * HEAD_DIM] for i in range(3))
        scores = dot(q, k, COLS)
        largest = jnp.max(scores, axis=-1, keepdims=True)
        expon = jnp.exp2((scores - largest) * EXP_SCALE)
        totals = jnp.sum(expon, axis=-1, keepdims=True)
        parts.append((dot(expon.astype(BF16), v, PLAIN) / totals).astype(BF16).astype(F32))
    context = jnp.concatenate(parts, axis=1)
    step = ctx_ref.shape[0]
    folds = [context[i * step : (i + 1) * step] for i in range(LENGTH // step)]
    ctx_ref[...] = jnp.concatenate(folds, axis=1)


def fold_of(cols):
    return 1 if cols % 128 == 0 else 2


def attend_forward(inputs, weights, bias):
    rows, width = inputs.shape
    cols = weights.shape[0] // 3
    fold = fold_of(cols)
    flat = lambda i: (0, 0)
    return call(
        attend_kernel,
        "attend_forward",
        (rows // LENGTH,),
        [
            (inputs, (LENGTH, width), lambda i: (i, 0)),
            (weights, weights.shape, flat),
            (bias, bias.shape, flat),
        ],
        [((rows // fold, fold * cols), F32, (LENGTH // fold, fold * cols), lambda i: (i, 0))],
        flops=rows * cols * (6 * width + 4 * LENGTH),
        exps=rows * LENGTH * (cols // HEAD_DIM),
    )[0]


def output_kernel(slot_ref, x_ref, ctx_ref, w_ref, vec_ref, low_ref, hid_ref, hbf_ref, nrm_ref, inv_ref):
    del slot_ref
    slot = pl.program_id(1)
    cols = low_ref.shape[-1]
    folds = [ctx_ref[:, i : i + cols] for i in range(0, ctx_ref.shape[-1], cols)]
    context = jnp.concatenate(folds, axis=0).astype(BF16)
    low_ref[...] = context
    attn = dot(context, w_ref[...], PLAIN)

    @pl.when(slot == 0)
    def _():
        hid_ref[...] = attn

    @pl.when(slot > 0)
    def _():
        hid_ref[...] += attn

    @pl.when(slot == pl.num_programs(1) - 1)
    def _():
        values = x_ref[...].astype(F32) + hid_ref[...] + vec_ref[0:1]
        hidden, normed, inverse = norm_forward(values, vec_ref[1:2], vec_ref[2:3])
        hid_ref[...] = hidden
        hbf_ref[...] = hidden.astype(BF16)
        nrm_ref[...] = normed
        inv_ref[...] = inverse


def output_forward(slots_at, x, context, weights, vectors):
    rows, width = x.shape
    slots, cols, _ = weights.shape
    mine = lambda i, j, at: (i, 0)
    flat = lambda i, j, at: (0, 0)
    token = (LENGTH, width)
    heads = (None, LENGTH, cols)
    return call(
        output_kernel,
        "output_forward",
        (rows // LENGTH, slots),
        [
            (x, token, mine),
            (context, (None, LENGTH // fold_of(cols), fold_of(cols) * cols), lambda i, j, at: (at[j], i, 0)),
            (weights, (None, cols, width), lambda i, j, at: (j, 0, 0)),
            (vectors, vectors.shape, flat),
        ],
        [
            ((slots, rows, cols), BF16, heads, lambda i, j, at: (j, i, 0)),
            ((rows, width), F32, token, mine),
            ((rows, width), BF16, token, mine),
            ((rows, width), F32, token, mine),
            ((rows, 1), F32, (LENGTH, 1), mine),
        ],
        flops=2 * rows * width * width,
        prefetch=slots_at,
    )


def attend_back_kernel(x_ref, ga_ref, gr_ref, w_ref, wo_ref, bias_ref, gqkv_ref, gx_ref, sum_ref):
    slot = pl.program_id(1)
    cols = wo_ref.shape[0]
    gctx = dot(ga_ref[...], wo_ref[...], COLS).astype(BF16)
    qkv = (dot(x_ref[...], w_ref[...], COLS) + bias_ref[...]).astype(BF16)
    for h in range(cols // HEAD_DIM):
        at = [slice(i * cols + h * HEAD_DIM, i * cols + (h + 1) * HEAD_DIM) for i in range(3)]
        q, k, v = (qkv[:, s] for s in at)
        g = gctx[:, at[0]]
        scores = dot(k, q, COLS)
        largest = jnp.max(scores, axis=0, keepdims=True)
        expon = jnp.exp2((scores - largest) * EXP_SCALE)
        probs = expon * (1.0 / row_sums(expon))
        gqkv_ref[:, at[2]] = dot(probs.astype(BF16), g, PLAIN).astype(BF16)
        weighted = probs * dot(v, g, COLS)
        grad_scores = (weighted - probs * row_sums(weighted)).astype(BF16)
        gqkv_ref[:, at[0]] = (dot(grad_scores, k, ROWS) * SCALE).astype(BF16)
        gqkv_ref[:, at[1]] = (dot(grad_scores, q, PLAIN) * SCALE).astype(BF16)
    grads = gqkv_ref[...]
    sum_ref[...] = row_sums(grads.astype(F32))
    back = dot(grads, w_ref[...], PLAIN)

    @pl.when(slot == 0)
    def _():
        gx_ref[...] = gr_ref[...] + back

    @pl.when(slot > 0)
    def _():
        gx_ref[...] += back


def attend_backward(x, grad_attn, grad_resid, weights, w_output, bias):
    rows, width = grad_attn.shape
    slots, cols, _ = w_output.shape
    mine = lambda i, j: (i, 0)
    token = (LENGTH, width)
    heads = (None, LENGTH, 3 * cols)
    weight = lambda i, j: (j, 0, 0)
    return call(
        attend_back_kernel,
        "attend_backward",
        (rows // LENGTH, slots),
        [
            (x, token, mine),
            (grad_attn, token, mine),
            (grad_resid, token, mine),
            (weights, (None, 3 * cols, width), weight),
            (w_output, (None, cols, width), weight),
            (bias, (None, 1, 3 * cols), weight),
        ],
        [
            ((slots, rows, 3 * cols), BF16, heads, lambda i, j: (j, i, 0)),
            ((rows, width), F32, token, mine),
            ((rows // LENGTH, slots, 1, 3 * cols), F32, (None, None, 1, 3 * cols), lambda i, j: (i, j, 0, 0)),
        ],
        flops=0,
        moved=0,
    )


def inner_kernel(h_ref, w_ref, b_ref, act_ref, slope_ref):
    inner = dot(h_ref[...], w_ref[...], PLAIN) + b_ref[...]
    phi = 0.5 + 0.5 * lax.erf(inner * (0.5**0.5))
    bell = jnp.exp2(inner * inner * (-0.5 * 1.4426950408889634)) * 0.3989422804014327
    act_ref[...] = (inner * phi).astype(BF16)
    slope_ref[...] = phi + inner * bell


def inner_forward(hidden, weights, bias):
    rows, width = hidden.shape
    slots, _, units = weights.shape
    slot = lambda i, j: (i, j, 0)
    block = LENGTH // 2
    return call(
        inner_kernel,
        "inner_forward",
        (slots, rows // block),
        [
            (hidden, (block, width), lambda i, j: (j, 0)),
            (weights, (None, width, units), lambda i, j: (i, 0, 0)),
            (bias, (None, 1, units), lambda i, j: (i, 0, 0)),
        ],
        [
            ((slots, rows, units), BF16, (None, block, units), slot),
            ((slots, rows, units), F32, (None, block, units), slot),
        ],
        flops=2 * rows * width * slots * units,
        exps=2 * rows * slots * units,
    )


def outer_kernel(act_ref, w_ref, hid_ref, cot_ref, vec_ref, out_ref, gr_ref, go_ref, sum_ref):
    slot = pl.program_id(1)
    outer = dot(act_ref[...], w_ref[...], PLAIN)

    @pl.when(slot == 0)
    def _():
        out_ref[...] = outer

    @pl.when(slot > 0)
    def _():
        out_ref[...] += outer

    @pl.when(slot == pl.num_programs(1) - 1)
    def _():
        gain = vec_ref[4:5]
        values = hid_ref[...] + (out_ref[...] + vec_ref[3:4])
        layer_out, normed, inverse = norm_forward(values, gain, vec_ref[5:6])
        out_ref[...] = layer_out
        upstream = cot_ref[...].astype(F32)
        grad = norm_backward(upstream, gain, normed, inverse)
        rounded = grad.astype(BF16)
        gr_ref[...] = grad
        go_ref[...] = rounded
        sum_ref[0:1] = row_sums(upstream * normed)
        sum_ref[1:2] = row_sums(upstream)
        sum_ref[2:3] = row_sums(rounded.astype(F32))


def outer_forward(active, weights, hidden, cotangent, vectors):
    rows, width = hidden.shape
    slots, units, _ = weights.shape
    mine = lambda i, j: (i, 0)
    flat = lambda i, j: (0, 0)
    token = (LENGTH, width)
    return call(
        outer_kernel,
        "outer_forward",
        (rows // LENGTH, slots),
        [
            (active, (None, LENGTH, units), lambda i, j: (j, i, 0)),
            (weights, (None, units, width), lambda i, j: (j, 0, 0)),
            (hidden, token, mine),
            (cotangent, token, mine),
            (vectors, vectors.shape, flat),
        ],
        [
            ((rows, width), F32, token, mine),
            ((rows, width), F32, token, mine),
            ((rows, width), BF16, token, mine),
            ((rows // LENGTH, 8, width), F32, (None, 8, width), lambda i, j: (i, 0, 0)),
        ],
        flops=2 * rows * width * slots * units,
    )


def inner_back_kernel(go_ref, wu_ref, slope_ref, wi_ref, gr_ref, nrm_ref, inv_ref, vec_ref,
                      gi_ref, g1_ref, ga_ref, bsum_ref, sum_ref):
    slot = pl.program_id(1)
    grad_inner = (dot(go_ref[...], wu_ref[...], COLS) * slope_ref[...]).astype(BF16)
    gi_ref[...] = grad_inner
    bsum_ref[...] = row_sums(grad_inner.astype(F32))
    back = dot(grad_inner, wi_ref[...], COLS)

    @pl.when(slot == 0)
    def _():
        g1_ref[...] = gr_ref[...] + back

    @pl.when(slot > 0)
    def _():
        g1_ref[...] += back

    @pl.when(slot == pl.num_programs(1) - 1)
    def _():
        upstream, normed = g1_ref[...], nrm_ref[...]
        grad = norm_backward(upstream, vec_ref[1:2], normed, inv_ref[...])
        rounded = grad.astype(BF16)
        g1_ref[...] = grad
        ga_ref[...] = rounded
        sum_ref[0:1] = row_sums(upstream * normed)
        sum_ref[1:2] = row_sums(upstream)
        sum_ref[2:3] = row_sums(rounded.astype(F32))


def inner_backward(grad_outer, w_outer, slope, w_inner, grad_resid2, normed, inverse, vectors):
    rows, width = grad_outer.shape
    slots, units, _ = w_outer.shape
    mine = lambda i, j: (i, 0)
    token = (LENGTH, width)
    slot = lambda i, j: (j, i, 0)
    weight = lambda i, j: (j, 0, 0)
    return call(
        inner_back_kernel,
        "inner_backward",
        (rows // LENGTH, slots),
        [
            (grad_outer, token, mine),
            (w_outer, (None, units, width), weight),
            (slope, (None, LENGTH, units), slot),
            (w_inner, (None, width, units), weight),
            (grad_resid2, token, mine),
            (normed, token, mine),
            (inverse, (LENGTH, 1), mine),
            (vectors, vectors.shape, lambda i, j: (0, 0)),
        ],
        [
            ((slots, rows, units), BF16, (None, LENGTH, units), slot),
            ((rows, width), F32, token, mine),
            ((rows, width), BF16, token, mine),
            ((rows // LENGTH, slots, 1, units), F32, (None, None, 1, units), lambda i, j: (i, j, 0, 0)),
            ((rows // LENGTH, 8, width), F32, (None, 8, width), lambda i, j: (i, 0, 0)),
        ],
        flops=0,
        moved=0,
    )


def narrow_kernel(x_ref, out_ref):
    out_ref[...] = x_ref[...].astype(BF16)


def narrow(values, block_rows):
    rows, width = values.shape
    at = lambda i: (i, 0)
    block = (block_rows, width)
    out = ((rows, width), BF16, block, at)
    return call(narrow_kernel, "narrow", (rows // block_rows,), [(values, block, at)], [out], 0)[0]


def shift_to(values, tensor, k):
    return lax.ppermute(values, "tensor", [(i, (i + k) % tensor) for i in range(tensor)])


def flip(values, bit):
    return lax.ppermute(values, "dp", [(i, i ^ bit) for i in range(8)])


def stage(*values):
    return lax.optimization_barrier(values)


def slots_kernel(slot_ref, local_ref, x_ref, out_ref):
    del slot_ref
    first = pl.program_id(0) == 0

    @pl.when(first)
    def _():
        out_ref[...] = local_ref[...]

    @pl.when(jnp.logical_not(first))
    def _():
        out_ref[...] = x_ref[...].reshape(out_ref.shape).astype(BF16)


def gather_plain(local, dp, tensor):
    rows, width = local.shape
    share = rows // dp
    piece = lax.dynamic_slice_in_dim(local, lax.axis_index("dp") * share, share, 0).astype(F32)
    full = lax.all_gather(piece, ("dp", "tensor"), axis=0).reshape(dp, tensor, share, width)
    order = (lax.axis_index("tensor") - jnp.arange(tensor, dtype=jnp.int32)) % tensor
    if share % 8:
        full = full.swapaxes(0, 1).reshape(1, tensor, rows, width)
    lead, _, part, _ = full.shape
    return pl.pallas_call(
        slots_kernel,
        grid_spec=pltpu.PrefetchScalarGridSpec(
            num_scalar_prefetch=1,
            grid=(tensor,),
            in_specs=[
                pl.BlockSpec((rows, width), lambda i, slot: (0, 0)),
                pl.BlockSpec((lead, None, part, width), lambda i, slot: (0, slot[i], 0, 0)),
            ],
            out_specs=pl.BlockSpec((None, rows, width), lambda i, slot: (i, 0, 0)),
        ),
        out_shape=jax.ShapeDtypeStruct((tensor, rows, width), BF16),
        cost_estimate=pl.CostEstimate(flops=0, bytes_accessed=6 * full.size, transcendentals=0),
        compiler_params=pltpu.CompilerParams(vmem_limit_bytes=48 << 20),
        name="slots",
    )(order, local, full)


def assemble_kernel(plan, *refs):
    where_ref, refs = refs[0], refs[1:]
    count = len(plan)
    targets = (len(refs) - count - 1) // 3
    locals_, pieces, outs, holds, sems = (
        refs[:targets],
        refs[targets : targets + count],
        refs[targets + count : 2 * targets + count],
        refs[2 * targets + count : -1],
        refs[-1],
    )
    copies = []
    for piece, spans in zip(pieces, plan):
        for i, source, rows, target in spans:
            start = pl.multiple_of(where_ref[len(copies)], 8)
            copies.append(
                pltpu.make_async_copy(
                    piece.at[i, :, pl.ds(source, rows)],
                    holds[target].at[:, pl.ds(start, rows)],
                    sems.at[len(copies)],
                )
            )
            copies[-1].start()
    for local, out in zip(locals_, outs):
        out[0] = local[...]
    for copy in copies:
        copy.wait()
    for hold, out in zip(holds, outs):
        for k in range(hold.shape[0]):
            out[k + 1] = hold[k].astype(BF16)


def assemble(locals_, pieces):
    width = locals_[0].shape[1]
    others = pieces[0][0].shape[1]
    where, plan = [], []
    for _, parts in pieces:
        plan.append([])
        for entry, sender, base, spans in parts:
            for row, rows, target, offset in spans:
                plan[-1].append((entry, base + row, rows, target))
                where.append(sender * (locals_[target].shape[0] // 8) + offset)
    total = sum(w.shape[0] for w in locals_)
    space = pl.BlockSpec(memory_space=pltpu.VMEM)
    return pl.pallas_call(
        partial(assemble_kernel, plan),
        in_specs=[pl.BlockSpec(memory_space=pltpu.SMEM)]
        + [space] * len(locals_)
        + [pl.BlockSpec(memory_space=pl.ANY)] * len(pieces),
        out_specs=[space] * len(locals_),
        out_shape=[jax.ShapeDtypeStruct((others + 1,) + w.shape, BF16) for w in locals_],
        scratch_shapes=[pltpu.VMEM((others,) + w.shape, F32) for w in locals_]
        + [pltpu.SemaphoreType.DMA((len(where),))],
        cost_estimate=pl.CostEstimate(flops=0, bytes_accessed=others * total * width * 6, transcendentals=0),
        compiler_params=pltpu.CompilerParams(vmem_limit_bytes=48 << 20),
        name="assemble",
    )(jnp.stack(where), *locals_, *(array for array, _ in pieces))


def shares(weights, dp=8):
    me = lax.axis_index("dp")
    cut = [lax.dynamic_slice_in_dim(w, me * (w.shape[0] // dp), w.shape[0] // dp, 0) for w in weights]
    return jnp.concatenate(cut, axis=0).astype(F32)


def across(values, tensor):
    return [shift_to(values, tensor, k) for k in range(1, tensor)]


def wide(v, w):
    return jnp.concatenate([v, w], axis=0)


def other_core(*values):
    return tuple(flip(v, 1) for v in values)


def halves(arrived, rows):
    return jnp.stack([v[:rows] for v in arrived])[None], jnp.stack([v[rows:] for v in arrived])[None]


def full_weights(locals_, a, b, ay, bx, c, d):
    me = lax.axis_index("dp")
    cut_at, end = a.shape[2], a.shape[2] + b.shape[2]
    ends = [0]
    for w in locals_:
        ends.append(ends[-1] + w.shape[0] // 8)

    def spans(first, last):
        found = []
        for target in range(len(locals_)):
            low, high = max(first, ends[target]), min(last, ends[target + 1])
            if low < high:
                found.append((low - first, high - low, target, low - ends[target]))
        return found

    upper = lambda rels: [(i, me ^ r, 0, spans(0, cut_at)) for i, r in enumerate(rels)]
    lower = lambda rels: [(i, me ^ r, 0, spans(cut_at, end)) for i, r in enumerate(rels)]
    pieces = [
        (a, upper((0, 2))),
        (b, lower((0, 4))),
        (ay, upper((4, 6))),
        (bx, lower((2, 6))),
        (c[0], upper((1, 3))),
        (c[1], lower((1, 5))),
        (d[0], upper((5, 7))),
        (d[1], lower((3, 7))),
    ]
    return assemble(locals_, pieces)


def block_order(width):
    me = lax.axis_index("dp")
    share = width // 8
    rel = jnp.array([7, 5, 3, 1, 6, 4, 2, 0])
    source = (me ^ rel[jnp.arange(width) // share]) * share + jnp.arange(width) % share
    return (lax.broadcasted_iota(jnp.int32, (width, width), 0) == source[None, :]).astype(BF16)


def grad_kernel(count, *refs):
    order_ref, refs = refs[0], refs[1:]
    lefts, rights, (send_ref, keep_ref), holds = (
        refs[:count], refs[count : 2 * count], refs[2 * count : 2 * count + 2], refs[2 * count + 2 :],
    )

    @pl.when(pl.program_id(0) == 0)
    def _():
        for left, hold in zip(lefts, holds):
            hold[...] = dot(left[...], order_ref[...], PLAIN).astype(BF16)

    half = send_ref.shape[0]
    start = 0
    for hold, right in zip(holds, rights):
        span = slice(start, start + right.shape[-1])
        value = dot(hold[...], right[...], ROWS)
        send_ref[:, span] = value[:half]
        keep_ref[:, span] = value[half:]
        start = span.stop


def grad_rows(order, pairs):
    rows, width = pairs[0][0].shape
    slots = pairs[0][1].shape[0]
    cols = sum(r.shape[-1] for _, r in pairs)
    flat = lambda j: (0, 0)
    ins = [(order, order.shape, flat)]
    ins += [(left, left.shape, flat) for left, _ in pairs]
    ins += [(right, (None,) + right.shape[1:], lambda j: (j, 0, 0)) for _, right in pairs]
    out = ((width // 2, slots * cols), F32, (width // 2, cols), lambda j: (0, j))
    scratch = [pltpu.VMEM((rows, width), BF16)] * len(pairs)
    return call(
        partial(grad_kernel, len(pairs)), "grad_rows", (slots,), ins, [out, out], 0, 0, scratch, moved=0
    )


def full_kernel(left_ref, right_ref, out_ref):
    out_ref[...] = dot(left_ref[...], right_ref[...], ROWS)


def grad_full(left, right):
    rows, width = left.shape
    slots, _, cols = right.shape
    return call(
        full_kernel,
        "grad_full",
        (slots,),
        [(left, left.shape, lambda j: (0, 0)), (right, (None, rows, cols), lambda j: (j, 0, 0))],
        [((width, slots * cols), F32, (width, cols), lambda j: (0, j))],
        flops=0,
        moved=0,
    )[0]


def split_paths(held, share):
    mid = held.shape[1] // 2
    pick = lambda i, cols: held[i * share : (i + 1) * share, cols]
    a, b = slice(None, mid), slice(mid, None)
    join = lambda i, j, cols: jnp.concatenate([pick(i, cols), pick(j, cols)], axis=0)
    return (join(0, 2, a), join(1, 3, a)), (join(0, 1, b), join(2, 3, b))


def columns_by_slot(left, right, tensor):
    part = jnp.concatenate([left, right], axis=1)
    cols = part.shape[1] // tensor
    return [part[:, k * cols : (k + 1) * cols] for k in range(tensor)]


def up(values, tensor, step):
    return lax.ppermute(values, "tensor", [(i, i + 1) for i in range(step)])


def down(values, tensor, step):
    return lax.ppermute(values, "tensor", [(i, i - 1) for i in range(tensor - step, tensor)])


def swap(values, tensor, bit):
    return lax.ppermute(values, "tensor", [(i, i ^ bit) for i in range(tensor)])


def scatter_plain(left, right, dp, tensor):
    grad = jnp.concatenate([dot(left, right[k], ROWS) for k in range(tensor)], axis=1)
    part = lax.psum_scatter(grad, "dp", scatter_dimension=0, tiled=True)
    cols = part.shape[1] // tensor
    part = [part[:, k * cols : (k + 1) * cols] for k in range(tensor)]
    return sum((shift_to(part[k], tensor, tensor - k) for k in range(1, tensor)), part[0])


def shards(
    dp,
    tensor,
    inputs,
    w_query,
    b_query,
    w_key,
    w_value,
    b_value,
    w_output,
    b_output,
    gain_attn,
    shift_attn,
    w_inner,
    b_inner,
    w_outer,
    b_outer,
    gain_ffn,
    shift_ffn,
    cotangent,
):
    tok_rows, width = inputs.shape
    own_rows = tok_rows // tensor
    cols = w_query.shape[1]
    z = lax.axis_index("tensor")
    own = lambda a: lax.dynamic_slice_in_dim(a, z * own_rows, own_rows, 0)
    row = lambda a: a.astype(F32)[None, :]

    vectors = row(jnp.concatenate([b_query, jnp.zeros_like(b_query), b_value, b_inner]))
    qkv_local = jnp.concatenate([w_query.T, w_key.T, w_value.T], axis=0)
    x, cot = own(inputs), own(cotangent)
    rows_of = (b_output, gain_attn, shift_attn, b_outer, gain_ffn, shift_ffn, b_outer, b_outer)
    wide_vectors = jnp.stack(rows_of).astype(F32)
    slots_at = (z - jnp.arange(tensor, dtype=jnp.int32)) % tensor
    staged = (
        dp == 8 and tensor == 4 and own_rows == LENGTH and width % 128 == 0
        and w_inner.shape == w_outer.shape == (width, width) and cols % 64 == 0
    )

    def rest_of_attention(context, weights):
        return output_forward(slots_at, x, context, weights, wide_vectors)

    def outer_half(active, weights, hidden):
        return outer_forward(active, weights, hidden, cot, wide_vectors)

    def small_sums(qkv_sums, inner_sums, sums_one, sums_two):
        by_slot = jnp.concatenate([jnp.sum(qkv_sums, axis=0), jnp.sum(inner_sums, axis=0)], axis=-1)
        by_place = by_slot[slots_at].reshape(-1)
        rest = jnp.concatenate([jnp.sum(sums_one, axis=0)[:3], jnp.sum(sums_two, axis=0)[:3]]).reshape(-1)
        return jnp.concatenate([by_place, rest])

    local_bias = vectors[:, : 3 * cols]
    context = attend_forward(inputs, qkv_local, local_bias)
    context = context.reshape(tensor, -1, context.shape[1])
    if not staged:
        vectors = jnp.stack([vectors] + across(vectors, tensor))
        qkv_bias, inner_bias = vectors[..., : 3 * cols], vectors[..., 3 * cols :]
        inner_full, output_full, outer_full, qkv_full = (
            gather_plain(w, dp, tensor) for w in (w_inner, w_output, w_outer, qkv_local)
        )
        context = lax.all_to_all(context, "tensor", 0, 0, tiled=True)
        context, hidden, hidden_bf, normed, inverse = rest_of_attention(context, output_full)
        active, slope = inner_forward(hidden_bf, inner_full, inner_bias)
        layer_out, grad_resid2, grad_outer, sums_two = outer_half(active, outer_full, hidden)
        layer_out = lax.all_gather(layer_out, "tensor", axis=0, tiled=True)
        grad_inner, grad_resid1, grad_attn, inner_sums, sums_one = inner_backward(
            grad_outer, outer_full, slope, inner_full, grad_resid2, normed, inverse, wide_vectors
        )
        grad_qkv, grad_x, qkv_sums = attend_backward(x, grad_attn, grad_resid1, qkv_full, output_full, qkv_bias)
        grad_inputs = lax.all_gather(grad_x, "tensor", axis=0, tiled=True)
        gu = scatter_plain(grad_outer, active, dp, tensor)
        gi = scatter_plain(hidden_bf, grad_inner, dp, tensor)
        go = scatter_plain(grad_attn, context, dp, tensor)
        gqkv = scatter_plain(x, grad_qkv, dp, tensor)
        sums = lax.psum(small_sums(qkv_sums, inner_sums, sums_one, sums_two), ("dp", "tensor"))
    else:
        order = block_order(width)
        share = width // 8
        p1, p2, p3 = shares([w_inner, w_output]), shares([w_outer]), shares([qkv_local])
        n1, n2, n3 = (-(-p.shape[0] // 16) * 8 for p in (p1, p2, p3))

        z1, arrived = across(p1, tensor), across(vectors, tensor)
        vectors = jnp.stack([vectors] + arrived)
        a1, b1 = halves(z1, n1)
        a1, b1, p2, context, vectors = stage(a1, b1, p2, context, vectors)
        qkv_bias, inner_bias = vectors[..., : 3 * cols], vectors[..., 3 * cols :]

        ax, by, z2 = flip(a1, 2), flip(b1, 4), across(p2, tensor)
        a1, b1, (a2, b2) = wide(a1, ax), wide(b1, by), halves(z2, n2)
        a1, b1, a2, b2, context, x, order = stage(a1, b1, a2, b2, context, x, order)

        c1 = other_core(a1, b1)
        context, *c1 = stage(context, *c1)
        context = lax.all_to_all(context, "tensor", 0, 0, tiled=True)
        ay1, bx1, ax, by = flip(a1, 4), flip(b1, 2), flip(a2, 2), flip(b2, 4)
        a2, b2 = wide(a2, ax), wide(b2, by)
        ay1, bx1, a2, b2, context, p3 = stage(ay1, bx1, a2, b2, context, p3)

        d1, ay2, bx2 = other_core(ay1, bx1), flip(a2, 4), flip(b2, 2)
        inner_full, output_full = full_weights([w_inner, w_output], a1, b1, ay1, bx1, c1, d1)
        context, hidden, hidden_bf, normed, inverse = rest_of_attention(context, output_full)
        ay2, bx2, p3, hidden_bf = stage(ay2, bx2, p3, hidden_bf)

        c2, d2, z3 = other_core(a2, b2), other_core(ay2, bx2), across(p3, tensor)
        active, slope = inner_forward(hidden_bf, inner_full, inner_bias)
        *c2, dx, dy, active = stage(*c2, *d2, active)
        (outer_full,) = full_weights([w_outer], a2, b2, ay2, bx2, c2, (dx, dy))
        layer_out, grad_resid2, grad_outer, sums_two = outer_half(active, outer_full, hidden)
        a3, b3 = halves(z3, n3)
        a3, b3, layer_out, grad_outer = stage(a3, b3, layer_out, grad_outer)

        layer_out = lax.all_gather(layer_out, "tensor", axis=0, tiled=True)
        ax, by = flip(a3, 2), flip(b3, 4)
        part1 = grad_full(grad_outer, active)
        a3, b3 = wide(a3, ax), wide(b3, by)
        a3, b3, part1, grad_outer = stage(a3, b3, part1, grad_outer)

        part1 = lax.psum_scatter(part1, "dp", scatter_dimension=0, tiled=True)
        ay3, bx3, c3 = flip(a3, 4), flip(b3, 2), other_core(a3, b3)
        grad_inner, grad_resid1, grad_attn, inner_sums, sums_one = inner_backward(
            grad_outer, outer_full, slope, inner_full, grad_resid2, normed, inverse, wide_vectors
        )
        ay3, bx3, grad_inner, grad_attn = stage(ay3, bx3, grad_inner, grad_attn)

        d3 = other_core(ay3, bx3)
        part2 = grad_full(hidden_bf, grad_inner)
        *d3, part2, grad_attn = stage(*d3, part2, grad_attn)

        part2 = lax.psum_scatter(part2, "dp", scatter_dimension=0, tiled=True)
        (qkv_full,) = full_weights([qkv_local], a3, b3, ay3, bx3, c3, d3)
        grad_qkv, grad_x, qkv_sums = attend_backward(x, grad_attn, grad_resid1, qkv_full, output_full, qkv_bias)
        grad_qkv, grad_x = stage(grad_qkv, grad_x)

        grad_inputs = lax.all_gather(grad_x, "tensor", axis=0, tiled=True)
        send, keep = grad_rows(order, [(x, grad_qkv), (grad_attn, context)])
        extra = small_sums(qkv_sums, inner_sums, sums_one, sums_two)
        extra = jnp.pad(extra, (0, -extra.shape[0] % (8 * width))).reshape(-1, width)
        send, extra = stage(send, extra)

        got = flip(send, 1)
        extra = extra + flip(extra, 1)
        (a, ak), (b, bk) = split_paths(keep + got, share)
        a, b, extra, layer_out = stage(a, b, extra, layer_out)

        ax, by = flip(a, 2), flip(b, 4)
        extra = extra + flip(extra, 2)
        a, b = ak + ax, bk + by
        a_send, b_send, extra = stage(a[:share], b[:share], extra)

        ay, bx = flip(a_send, 4), flip(b_send, 2)
        extra = extra + flip(extra, 4)
        part3 = jnp.concatenate([a[share:] + ay, b[share:] + bx], axis=1)
        parts = wide(wide(part1, part2), part3)
        parts = [parts[:, k * width : (k + 1) * width] for k in range(tensor)]
        u, d, extra = stage(parts[1], parts[3], extra)

        u, d = up(u, tensor, 1), down(d, tensor, 1)
        extra = extra + swap(extra, tensor, 1)
        u, d, extra = stage(parts[2] + u, parts[2] + d, extra)

        u, d = up(u, tensor, 2), down(d, tensor, 2)
        extra = extra + swap(extra, tensor, 2)
        u, d = stage(parts[3] + u, parts[1] + d)

        parts = parts[0] + up(u, tensor, 3) + down(d, tensor, 3)
        gu, gi, gqkv = parts[:share], parts[share : 2 * share], parts[2 * share :]
        gqkv, go = gqkv[:, : 3 * cols], gqkv[:, 3 * cols :]
        sums = extra.reshape(-1)

    layer_out = narrow(layer_out, own_rows)
    span = 3 * cols + w_inner.shape[1]
    mine = lax.dynamic_slice_in_dim(sums, z * span, span, 0)
    rest = sums[span * tensor :][: 6 * width].reshape(6, width)
    return (
        layer_out,
        grad_inputs,
        gqkv[:, :cols],
        mine[:cols],
        gqkv[:, cols : 2 * cols],
        gqkv[:, 2 * cols :],
        mine[2 * cols : 3 * cols],
        go.T,
        rest[2],
        rest[0],
        rest[1],
        gi,
        mine[3 * cols :],
        gu.T,
        rest[5],
        rest[3],
        rest[4],
    )


def solution(mesh):
    wide, tall, vector = P(None, "tensor"), P("tensor", None), P("tensor")
    tokens, both = P("dp", None), P("dp", "tensor")
    in_specs = (
        tokens, wide, vector, wide, wide, vector, tall, P(), P(), P(), wide, vector, tall, P(), P(), P(), tokens,
    )
    out_specs = (
        tokens, tokens, both, vector, both, both, vector, P("tensor", "dp"), P(), P(), P(), both, vector,
        P("tensor", "dp"), P(), P(), P(),
    )
    body = partial(shards, mesh.shape["dp"], mesh.shape["tensor"])
    return jax.shard_map(body, mesh=mesh, in_specs=in_specs, out_specs=out_specs, check_vma=False)
```

```python
import math
from functools import partial

import jax
import jax.numpy as jnp
from jax import lax
from jax.experimental import pallas as pl
from jax.experimental.pallas import tpu as pltpu
from jax.sharding import PartitionSpec as P

HEAD_DIM = 64
LENGTH = 512
EPSILON = 1e-12
F32 = jnp.float32
BF16 = jnp.bfloat16
SCALE = HEAD_DIM ** (-0.5)
EXP_SCALE = SCALE * 1.4426950408889634
ROWS = ((0,), (0,))
PLAIN = ((1,), (0,))
COLS = ((1,), (1,))


def dot(left, right, dims):
    return lax.dot_general(left, right, (dims, ((), ())), preferred_element_type=F32)


def norm_forward(values, gain, shift):
    center = values - jnp.mean(values, axis=-1, keepdims=True)
    inverse = lax.rsqrt(jnp.mean(center * center, axis=-1, keepdims=True) + EPSILON)
    normed = center * inverse
    return (normed * gain + shift, normed, inverse)


def norm_backward(upstream, gain, normed, inverse):
    scaled = upstream * gain
    first_mean = jnp.mean(scaled, axis=-1, keepdims=True)
    cross_mean = jnp.mean(scaled * normed, axis=-1, keepdims=True)
    return inverse * (scaled - first_mean - normed * cross_mean)


def by_rows(rows, step, body, carry=()):
    return lax.fori_loop(0, rows // step, lambda i, c: body(pl.ds(pl.multiple_of(i * step, step), step), c), carry)


def row_sums(values):
    return jnp.sum(values, axis=0, keepdims=True)


def size_of(shape, dtype):
    return math.prod(shape) * jnp.dtype(dtype).itemsize


def call(kernel, name, grid, ins, outs, flops, exps=0, scratch=(), prefetch=None, moved=None):
    if moved is None:
        moved = sum(size_of(a.shape, a.dtype) for a, _, _ in ins) + sum(size_of(s, t) for s, t, _, _ in outs)
    lead = () if prefetch is None else (prefetch,)
    return pl.pallas_call(
        kernel,
        grid_spec=pltpu.PrefetchScalarGridSpec(
            num_scalar_prefetch=len(lead),
            grid=grid,
            in_specs=[pl.BlockSpec(b, m) for _, b, m in ins],
            out_specs=[pl.BlockSpec(b, m) for _, _, b, m in outs],
            scratch_shapes=list(scratch),
        ),
        out_shape=[jax.ShapeDtypeStruct(s, t) for s, t, _, _ in outs],
        cost_estimate=pl.CostEstimate(flops=flops, bytes_accessed=moved, transcendentals=exps),
        compiler_params=pltpu.CompilerParams(vmem_limit_bytes=56 << 20),
        name=name,
    )(*lead, *(a for a, _, _ in ins))


def attend_kernel(x_ref, w_ref, bias_ref, ctx_ref):
    cols = w_ref.shape[0] // 3
    parts = []
    qkv = (dot(x_ref[...], w_ref[...], COLS) + bias_ref[...]).astype(BF16)
    for h in range(cols // HEAD_DIM):
        q, k, v = (qkv[:, i * cols + h * HEAD_DIM : i * cols + (h + 1) * HEAD_DIM] for i in range(3))
        scores = dot(q, k, COLS)
        largest = jnp.max(scores, axis=-1, keepdims=True)
        expon = jnp.exp2((scores - largest) * EXP_SCALE)
        totals = jnp.sum(expon, axis=-1, keepdims=True)
        parts.append((dot(expon.astype(BF16), v, PLAIN) / totals).astype(BF16).astype(F32))
    context = jnp.concatenate(parts, axis=1)
    step = ctx_ref.shape[0]
    folds = [context[i * step : (i + 1) * step] for i in range(LENGTH // step)]
    ctx_ref[...] = jnp.concatenate(folds, axis=1)


def fold_of(cols):
    return 1 if cols % 128 == 0 else 2


def attend_forward(inputs, weights, bias):
    rows, width = inputs.shape
    cols = weights.shape[0] // 3
    fold = fold_of(cols)
    flat = lambda i: (0, 0)
    return call(
        attend_kernel,
        "attend_forward",
        (rows // LENGTH,),
        [
            (inputs, (LENGTH, width), lambda i: (i, 0)),
            (weights, weights.shape, flat),
            (bias, bias.shape, flat),
        ],
        [((rows // fold, fold * cols), F32, (LENGTH // fold, fold * cols), lambda i: (i, 0))],
        flops=rows * cols * (6 * width + 4 * LENGTH),
        exps=rows * LENGTH * (cols // HEAD_DIM),
    )[0]


def output_kernel(slot_ref, x_ref, ctx_ref, w_ref, vec_ref, low_ref, hid_ref, hbf_ref, nrm_ref, inv_ref):
    del slot_ref
    slot = pl.program_id(1)
    cols = low_ref.shape[-1]
    folds = [ctx_ref[:, i : i + cols] for i in range(0, ctx_ref.shape[-1], cols)]
    context = jnp.concatenate(folds, axis=0).astype(BF16)
    low_ref[...] = context
    attn = dot(context, w_ref[...], PLAIN)

    @pl.when(slot == 0)
    def _():
        hid_ref[...] = attn

    @pl.when(slot > 0)
    def _():
        hid_ref[...] += attn

    @pl.when(slot == pl.num_programs(1) - 1)
    def _():
        bias, gain, shift = vec_ref[0:1], vec_ref[1:2], vec_ref[2:3]

        def block(at, carry):
            values = x_ref[at].astype(F32) + hid_ref[at] + bias
            hidden, normed, inverse = norm_forward(values, gain, shift)
            hid_ref[at] = hidden
            hbf_ref[at] = hidden.astype(BF16)
            nrm_ref[at] = normed
            inv_ref[at] = inverse
            return carry

        by_rows(LENGTH, 256, block)


def output_forward(slots_at, x, context, weights, vectors):
    rows, width = x.shape
    slots, cols, _ = weights.shape
    mine = lambda i, j, at: (i, 0)
    flat = lambda i, j, at: (0, 0)
    token = (LENGTH, width)
    heads = (None, LENGTH, cols)
    return call(
        output_kernel,
        "output_forward",
        (rows // LENGTH, slots),
        [
            (x, token, mine),
            (context, (None, LENGTH // fold_of(cols), fold_of(cols) * cols), lambda i, j, at: (at[j], i, 0)),
            (weights, (None, cols, width), lambda i, j, at: (j, 0, 0)),
            (vectors, vectors.shape, flat),
        ],
        [
            ((slots, rows, cols), BF16, heads, lambda i, j, at: (j, i, 0)),
            ((rows, width), F32, token, mine),
            ((rows, width), BF16, token, mine),
            ((rows, width), F32, token, mine),
            ((rows, 1), F32, (LENGTH, 1), mine),
        ],
        flops=2 * rows * width * width,
        prefetch=slots_at,
    )


def attend_back_kernel(x_ref, ga_ref, gr_ref, w_ref, wo_ref, bias_ref, ctx_ref, gw_ref, gx_ref, sum_ref, gqkv_ref):
    slot = pl.program_id(1)
    cols = wo_ref.shape[0]
    gctx = dot(ga_ref[...], wo_ref[...], COLS).astype(BF16)
    qkv = (dot(x_ref[...], w_ref[...], COLS) + bias_ref[...]).astype(BF16)
    for h in range(cols // HEAD_DIM):
        at = [slice(i * cols + h * HEAD_DIM, i * cols + (h + 1) * HEAD_DIM) for i in range(3)]
        q, k, v = (qkv[:, s] for s in at)
        g = gctx[:, at[0]]
        scores = dot(k, q, COLS)
        largest = jnp.max(scores, axis=0, keepdims=True)
        expon = jnp.exp2((scores - largest) * EXP_SCALE)
        probs = expon * (1.0 / row_sums(expon))
        gqkv_ref[:, at[2]] = dot(probs.astype(BF16), g, PLAIN).astype(BF16)
        weighted = probs * dot(v, g, COLS)
        grad_scores = (weighted - probs * row_sums(weighted)).astype(BF16)
        gqkv_ref[:, at[0]] = (dot(grad_scores, k, ROWS) * SCALE).astype(BF16)
        gqkv_ref[:, at[1]] = (dot(grad_scores, q, PLAIN) * SCALE).astype(BF16)
    grads = gqkv_ref[...]
    sum_ref[...] = row_sums(grads.astype(F32))
    back = dot(grads, w_ref[...], PLAIN)
    gw_ref[:, : 3 * cols] = dot(x_ref[...], grads, ROWS)
    gw_ref[:, 3 * cols :] = dot(ga_ref[...], ctx_ref[...], ROWS)

    @pl.when(slot == 0)
    def _():
        gx_ref[...] = gr_ref[...] + back

    @pl.when(slot > 0)
    def _():
        gx_ref[...] += back


def attend_backward(x, grad_attn, grad_resid, weights, w_output, bias, context):
    rows, width = grad_attn.shape
    slots, cols, _ = w_output.shape
    mine = lambda i, j: (i, 0)
    token = (LENGTH, width)
    weight = lambda i, j: (j, 0, 0)
    return call(
        attend_back_kernel,
        "attend_backward",
        (rows // LENGTH, slots),
        [
            (x, token, mine),
            (grad_attn, token, mine),
            (grad_resid, token, mine),
            (weights, (None, 3 * cols, width), weight),
            (w_output, (None, cols, width), weight),
            (bias, (None, 1, 3 * cols), weight),
            (context, (None, LENGTH, cols), lambda i, j: (j, i, 0)),
        ],
        [
            ((width, slots * 4 * cols), F32, (width, 4 * cols), lambda i, j: (0, j)),
            ((rows, width), F32, token, mine),
            ((rows // LENGTH, slots, 1, 3 * cols), F32, (None, None, 1, 3 * cols), lambda i, j: (i, j, 0, 0)),
        ],
        flops=0,
        moved=0,
        scratch=[pltpu.VMEM((LENGTH, 3 * cols), BF16)],
    )


def inner_kernel(h_ref, w_ref, b_ref, act_ref, slope_ref):
    inner = dot(h_ref[...], w_ref[...], PLAIN) + b_ref[...]
    phi = 0.5 + 0.5 * lax.erf(inner * (0.5**0.5))
    bell = jnp.exp2(inner * inner * (-0.5 * 1.4426950408889634)) * 0.3989422804014327
    act_ref[...] = (inner * phi).astype(BF16)
    slope_ref[...] = phi + inner * bell


def inner_forward(hidden, weights, bias):
    rows, width = hidden.shape
    slots, _, units = weights.shape
    slot = lambda i, j: (i, j, 0)
    block = LENGTH // 2
    return call(
        inner_kernel,
        "inner_forward",
        (slots, rows // block),
        [
            (hidden, (block, width), lambda i, j: (j, 0)),
            (weights, (None, width, units), lambda i, j: (i, 0, 0)),
            (bias, (None, 1, units), lambda i, j: (i, 0, 0)),
        ],
        [
            ((slots, rows, units), BF16, (None, block, units), slot),
            ((slots, rows, units), F32, (None, block, units), slot),
        ],
        flops=2 * rows * width * slots * units,
        exps=2 * rows * slots * units,
    )


def outer_kernel(act_ref, w_ref, hid_ref, cot_ref, vec_ref, out_ref, gr_ref, go_ref, sum_ref):
    slot = pl.program_id(1)
    outer = dot(act_ref[...], w_ref[...], PLAIN)

    @pl.when(slot == 0)
    def _():
        out_ref[...] = outer

    @pl.when(slot > 0)
    def _():
        out_ref[...] += outer

    @pl.when(slot == pl.num_programs(1) - 1)
    def _():
        bias, gain, shift = vec_ref[3:4], vec_ref[4:5], vec_ref[5:6]

        def block(at, sums):
            values = hid_ref[at] + (out_ref[at] + bias)
            layer_out, normed, inverse = norm_forward(values, gain, shift)
            out_ref[at] = layer_out
            upstream = cot_ref[at].astype(F32)
            grad = norm_backward(upstream, gain, normed, inverse)
            rounded = grad.astype(BF16)
            gr_ref[at] = grad
            go_ref[at] = rounded
            found = (upstream * normed, upstream, rounded.astype(F32))
            return tuple(s + row_sums(f) for s, f in zip(sums, found))

        for i, total in enumerate(by_rows(LENGTH, 256, block, (jnp.zeros_like(gain),) * 3)):
            sum_ref[i : i + 1] = total


def outer_forward(active, weights, hidden, cotangent, vectors):
    rows, width = hidden.shape
    slots, units, _ = weights.shape
    mine = lambda i, j: (i, 0)
    flat = lambda i, j: (0, 0)
    token = (LENGTH, width)
    return call(
        outer_kernel,
        "outer_forward",
        (rows // LENGTH, slots),
        [
            (active, (None, LENGTH, units), lambda i, j: (j, i, 0)),
            (weights, (None, units, width), lambda i, j: (j, 0, 0)),
            (hidden, token, mine),
            (cotangent, token, mine),
            (vectors, vectors.shape, flat),
        ],
        [
            ((rows, width), F32, token, mine),
            ((rows, width), F32, token, mine),
            ((rows, width), BF16, token, mine),
            ((rows // LENGTH, 8, width), F32, (None, 8, width), lambda i, j: (i, 0, 0)),
        ],
        flops=2 * rows * width * slots * units,
    )


def inner_back_kernel(go_ref, wu_ref, slope_ref, wi_ref, gr_ref, nrm_ref, inv_ref, vec_ref,
                      gi_ref, g1_ref, ga_ref, bsum_ref, sum_ref):
    slot = pl.program_id(1)
    grad_inner = (dot(go_ref[...], wu_ref[...], COLS) * slope_ref[...]).astype(BF16)
    gi_ref[...] = grad_inner
    bsum_ref[...] = row_sums(grad_inner.astype(F32))
    back = dot(grad_inner, wi_ref[...], COLS)

    @pl.when(slot == 0)
    def _():
        g1_ref[...] = gr_ref[...] + back

    @pl.when(slot > 0)
    def _():
        g1_ref[...] += back

    @pl.when(slot == pl.num_programs(1) - 1)
    def _():
        gain = vec_ref[1:2]

        def block(at, sums):
            upstream, normed = g1_ref[at], nrm_ref[at]
            grad = norm_backward(upstream, gain, normed, inv_ref[at])
            rounded = grad.astype(BF16)
            g1_ref[at] = grad
            ga_ref[at] = rounded
            found = (upstream * normed, upstream, rounded.astype(F32))
            return tuple(s + row_sums(f) for s, f in zip(sums, found))

        for i, total in enumerate(by_rows(LENGTH, 256, block, (jnp.zeros_like(gain),) * 3)):
            sum_ref[i : i + 1] = total


def inner_backward(grad_outer, w_outer, slope, w_inner, grad_resid2, normed, inverse, vectors):
    rows, width = grad_outer.shape
    slots, units, _ = w_outer.shape
    mine = lambda i, j: (i, 0)
    token = (LENGTH, width)
    slot = lambda i, j: (j, i, 0)
    weight = lambda i, j: (j, 0, 0)
    return call(
        inner_back_kernel,
        "inner_backward",
        (rows // LENGTH, slots),
        [
            (grad_outer, token, mine),
            (w_outer, (None, units, width), weight),
            (slope, (None, LENGTH, units), slot),
            (w_inner, (None, width, units), weight),
            (grad_resid2, token, mine),
            (normed, token, mine),
            (inverse, (LENGTH, 1), mine),
            (vectors, vectors.shape, lambda i, j: (0, 0)),
        ],
        [
            ((slots, rows, units), BF16, (None, LENGTH, units), slot),
            ((rows, width), F32, token, mine),
            ((rows, width), BF16, token, mine),
            ((rows // LENGTH, slots, 1, units), F32, (None, None, 1, units), lambda i, j: (i, j, 0, 0)),
            ((rows // LENGTH, 8, width), F32, (None, 8, width), lambda i, j: (i, 0, 0)),
        ],
        flops=0,
        moved=0,
    )


def narrow_kernel(x_ref, out_ref):
    out_ref[...] = x_ref[...].astype(BF16)


def narrow(values, block_rows):
    rows, width = values.shape
    at = lambda i: (i, 0)
    block = (block_rows, width)
    out = ((rows, width), BF16, block, at)
    return call(narrow_kernel, "narrow", (rows // block_rows,), [(values, block, at)], [out], 0)[0]


def shift_to(values, tensor, k):
    return lax.ppermute(values, "tensor", [(i, (i + k) % tensor) for i in range(tensor)])


def flip(values, bit):
    return lax.ppermute(values, "dp", [(i, i ^ bit) for i in range(8)])


def stage(*values):
    return lax.optimization_barrier(values)


def slots_kernel(slot_ref, local_ref, x_ref, out_ref):
    del slot_ref
    first = pl.program_id(0) == 0

    @pl.when(first)
    def _():
        out_ref[...] = local_ref[...]

    @pl.when(jnp.logical_not(first))
    def _():
        out_ref[...] = x_ref[...].reshape(out_ref.shape).astype(BF16)


def gather_plain(local, dp, tensor):
    rows, width = local.shape
    share = rows // dp
    piece = lax.dynamic_slice_in_dim(local, lax.axis_index("dp") * share, share, 0).astype(F32)
    full = lax.all_gather(piece, ("dp", "tensor"), axis=0).reshape(dp, tensor, share, width)
    order = (lax.axis_index("tensor") - jnp.arange(tensor, dtype=jnp.int32)) % tensor
    if share % 8:
        full = full.swapaxes(0, 1).reshape(1, tensor, rows, width)
    lead, _, part, _ = full.shape
    return pl.pallas_call(
        slots_kernel,
        grid_spec=pltpu.PrefetchScalarGridSpec(
            num_scalar_prefetch=1,
            grid=(tensor,),
            in_specs=[
                pl.BlockSpec((rows, width), lambda i, slot: (0, 0)),
                pl.BlockSpec((lead, None, part, width), lambda i, slot: (0, slot[i], 0, 0)),
            ],
            out_specs=pl.BlockSpec((None, rows, width), lambda i, slot: (i, 0, 0)),
        ),
        out_shape=jax.ShapeDtypeStruct((tensor, rows, width), BF16),
        cost_estimate=pl.CostEstimate(flops=0, bytes_accessed=6 * full.size, transcendentals=0),
        compiler_params=pltpu.CompilerParams(vmem_limit_bytes=48 << 20),
        name="slots",
    )(order, local, full)


def assemble_kernel(plan, *refs):
    where_ref, refs = refs[0], refs[1:]
    count = len(plan)
    targets = (len(refs) - count - 1) // 3
    locals_, pieces, outs, holds, sems = (
        refs[:targets],
        refs[targets : targets + count],
        refs[targets + count : 2 * targets + count],
        refs[2 * targets + count : -1],
        refs[-1],
    )
    copies = []
    for piece, spans in zip(pieces, plan):
        for i, source, rows, target in spans:
            start = pl.multiple_of(where_ref[len(copies)], 8)
            copies.append(
                pltpu.make_async_copy(
                    piece.at[i, :, pl.ds(source, rows)],
                    holds[target].at[:, pl.ds(start, rows)],
                    sems.at[len(copies)],
                )
            )
            copies[-1].start()
    for local, out in zip(locals_, outs):
        out[0] = local[...]
    for copy in copies:
        copy.wait()
    for hold, out in zip(holds, outs):
        for k in range(hold.shape[0]):

            def block(at, carry, k=k, hold=hold, out=out):
                out[k + 1, at] = hold[k, at].astype(BF16)
                return carry

            by_rows(hold.shape[1], 96, block)


def assemble(locals_, pieces):
    width = locals_[0].shape[1]
    others = pieces[0][0].shape[1]
    where, plan = [], []
    for _, parts in pieces:
        plan.append([])
        for entry, sender, base, spans in parts:
            for row, rows, target, offset in spans:
                plan[-1].append((entry, base + row, rows, target))
                where.append(sender * (locals_[target].shape[0] // 8) + offset)
    total = sum(w.shape[0] for w in locals_)
    space = pl.BlockSpec(memory_space=pltpu.VMEM)
    return pl.pallas_call(
        partial(assemble_kernel, plan),
        in_specs=[pl.BlockSpec(memory_space=pltpu.SMEM)]
        + [space] * len(locals_)
        + [pl.BlockSpec(memory_space=pl.ANY)] * len(pieces),
        out_specs=[space] * len(locals_),
        out_shape=[jax.ShapeDtypeStruct((others + 1,) + w.shape, BF16) for w in locals_],
        scratch_shapes=[pltpu.VMEM((others,) + w.shape, F32) for w in locals_]
        + [pltpu.SemaphoreType.DMA((len(where),))],
        cost_estimate=pl.CostEstimate(flops=0, bytes_accessed=others * total * width * 6, transcendentals=0),
        compiler_params=pltpu.CompilerParams(vmem_limit_bytes=48 << 20),
        name="assemble",
    )(jnp.stack(where), *locals_, *(array for array, _ in pieces))


def shares(weights, dp=8):
    me = lax.axis_index("dp")
    cut = [lax.dynamic_slice_in_dim(w, me * (w.shape[0] // dp), w.shape[0] // dp, 0) for w in weights]
    return jnp.concatenate(cut, axis=0).astype(F32)


def across(values, tensor):
    return [shift_to(values, tensor, k) for k in range(1, tensor)]


def wide(v, w):
    return jnp.concatenate([v, w], axis=0)


def other_core(*values):
    return tuple(flip(v, 1) for v in values)


def copy_kernel(plan, count, *refs):
    ins, outs = refs[:count], refs[count:]
    for source, source_at, target, target_at in plan:
        outs[target][target_at] = ins[source][source_at]


def copies(ins, shapes, plan):
    space = pl.BlockSpec(memory_space=pltpu.VMEM)
    return pl.pallas_call(
        partial(copy_kernel, plan, len(ins)),
        in_specs=[space] * len(ins),
        out_specs=[space] * len(shapes),
        out_shape=[jax.ShapeDtypeStruct(shape, F32) for shape in shapes],
        cost_estimate=pl.CostEstimate(flops=0, bytes_accessed=0, transcendentals=0),
        compiler_params=pltpu.CompilerParams(vmem_limit_bytes=32 << 20),
        name="copies",
    )(*ins)


def halves(arrived, upper):
    rows, width = arrived[0].shape
    n = len(arrived)
    plan = [(k, (slice(0, upper),), 0, (0, k)) for k in range(n)]
    plan += [(k, (slice(upper, rows),), 1, (0, k)) for k in range(n)]
    return copies(arrived, [(1, n, upper, width), (1, n, rows - upper, width)], plan)


def join(a, ax, b, by):
    _, n, upper, width = a.shape
    lower = b.shape[2]
    plan = []
    for i, (v, w) in enumerate(((a, b), (ax, by))):
        every = slice(None)
        plan += [(2 * i, (0,), 0, (i,)), (2 * i + 1, (0,), 1, (i,))]
        plan += [(2 * i, (0,), 2, (i, every, slice(0, upper))), (2 * i + 1, (0,), 2, (i, every, slice(upper, upper + lower)))]
    shapes = [(2, n, upper, width), (2, n, lower, width), (2, n, upper + lower, width)]
    return copies([a, b, ax, by], shapes, plan)


def full_weights(locals_, a, b, ay, bx, c, d):
    me = lax.axis_index("dp")
    cut_at, end = a.shape[2], a.shape[2] + b.shape[2]
    ends = [0]
    for w in locals_:
        ends.append(ends[-1] + w.shape[0] // 8)

    def spans(first, last):
        found = []
        for target in range(len(locals_)):
            low, high = max(first, ends[target]), min(last, ends[target + 1])
            if low < high:
                found.append((low - first, high - low, target, low - ends[target]))
        return found

    upper = lambda rels: [(i, me ^ r, 0, spans(0, cut_at)) for i, r in enumerate(rels)]
    lower = lambda rels, base=0: [(i, me ^ r, base, spans(cut_at, end)) for i, r in enumerate(rels)]
    pieces = [
        (a, upper((0, 2))),
        (b, lower((0, 4))),
        (ay, upper((4, 6))),
        (bx, lower((2, 6))),
        (c, upper((1, 3)) + lower((1, 5), cut_at)),
        (d[0], upper((5, 7))),
        (d[1], lower((3, 7))),
    ]
    return assemble(locals_, pieces)


def block_order(width):
    me = lax.axis_index("dp")
    share = width // 8
    rel = jnp.array([7, 5, 3, 1, 6, 4, 2, 0])
    source = (me ^ rel[jnp.arange(width) // share]) * share + jnp.arange(width) % share
    return (lax.broadcasted_iota(jnp.int32, (width, width), 0) == source[None, :]).astype(BF16)


def grad_kernel(count, *refs):
    order_ref, refs = refs[0], refs[1:]
    lefts, rights, (send_ref, keep_ref), holds = (
        refs[:count], refs[count : 2 * count], refs[2 * count : 2 * count + 2], refs[2 * count + 2 :],
    )

    @pl.when(pl.program_id(0) == 0)
    def _():
        for left, hold in zip(lefts, holds):
            hold[...] = dot(left[...], order_ref[...], PLAIN).astype(BF16)

    half = send_ref.shape[0]
    start = 0
    for hold, right in zip(holds, rights):
        span = slice(start, start + right.shape[-1])
        value = dot(hold[...], right[...], ROWS)
        send_ref[:, span] = value[:half]
        keep_ref[:, span] = value[half:]
        start = span.stop


def grad_rows(order, pairs):
    rows, width = pairs[0][0].shape
    slots = pairs[0][1].shape[0]
    cols = sum(r.shape[-1] for _, r in pairs)
    flat = lambda j: (0, 0)
    ins = [(order, order.shape, flat)]
    ins += [(left, left.shape, flat) for left, _ in pairs]
    ins += [(right, (None,) + right.shape[1:], lambda j: (j, 0, 0)) for _, right in pairs]
    out = ((width // 2, slots * cols), F32, (width // 2, cols), lambda j: (0, j))
    scratch = [pltpu.VMEM((rows, width), BF16)] * len(pairs)
    return call(
        partial(grad_kernel, len(pairs)), "grad_rows", (slots,), ins, [out, out], 0, 0, scratch, moved=0
    )


def full_kernel(count, *refs):
    lefts, rights, out_ref = refs[:count], refs[count:-1], refs[-1]
    start = 0
    for left, right in zip(lefts, rights):
        span = slice(start, start + right.shape[-1])
        out_ref[:, span] = dot(left[...], right[...], ROWS)
        start = span.stop


def grad_full(*pairs):
    rows, width = pairs[0][0].shape
    slots = pairs[0][1].shape[0]
    cols = sum(r.shape[-1] for _, r in pairs)
    ins = [(left, left.shape, lambda j: (0, 0)) for left, _ in pairs]
    ins += [(right, (None,) + right.shape[1:], lambda j: (j, 0, 0)) for _, right in pairs]
    return call(
        partial(full_kernel, len(pairs)),
        "grad_full",
        (slots,),
        ins,
        [((width, slots * cols), F32, (width, cols), lambda j: (0, j))],
        flops=0,
        moved=0,
    )[0]


def split_paths(held, share):
    mid = held.shape[1] // 2
    pick = lambda i, cols: held[i * share : (i + 1) * share, cols]
    a, b = slice(None, mid), slice(mid, None)
    join = lambda i, j, cols: jnp.concatenate([pick(i, cols), pick(j, cols)], axis=0)
    return (join(0, 2, a), join(1, 3, a)), (join(0, 1, b), join(2, 3, b))


def scatter_plain(grad, tensor):
    part = lax.psum_scatter(grad, "dp", scatter_dimension=0, tiled=True)
    part = columns(part, tensor)
    return sum((shift_to(part[k], tensor, tensor - k) for k in range(1, tensor)), part[0])


def columns(part, tensor):
    cols = part.shape[1] // tensor
    return [part[:, k * cols : (k + 1) * cols] for k in range(tensor)]


def up(values, tensor, step):
    return lax.ppermute(values, "tensor", [(i, i + 1) for i in range(step)])


def down(values, tensor, step):
    return lax.ppermute(values, "tensor", [(i, i - 1) for i in range(tensor - step, tensor)])


def place_kernel(z_ref, own_ref, *refs):
    *others, out_ref = refs
    count = len(others) // 2
    below, above = others[:count], others[count:]
    away = pl.program_id(0) - z_ref[0]

    @pl.when(away == 0)
    def _():
        out_ref[...] = own_ref[...]

    for k in range(count):

        @pl.when(away == -(k + 1))
        def _(k=k):
            out_ref[...] = below[k][...]

        @pl.when(away == k + 1)
        def _(k=k):
            out_ref[...] = above[k][...]


def place(own, below, above):
    rows, width = own.shape
    count = len(below) + 1
    whole = (rows, width)
    return call(
        place_kernel,
        "place",
        (count,),
        [(v, whole, lambda i, z: (0, 0)) for v in (own, *below, *above)],
        [((count * rows, width), F32, whole, lambda i, z: (i, 0))],
        flops=0,
        moved=0,
        prefetch=lax.axis_index("tensor").astype(jnp.int32).reshape(1),
    )[0]


def onward(values, tensor, step):
    u, d = values
    u = lax.ppermute(u, "tensor", [(i, i + 1) for i in range(step - 1, tensor - 1)])
    d = lax.ppermute(d, "tensor", [(i, i - 1) for i in range(1, tensor - step + 1)])
    return u, d


def swap(values, tensor, bit):
    return lax.ppermute(values, "tensor", [(i, i ^ bit) for i in range(tensor)])


def shards(
    dp,
    tensor,
    inputs,
    w_query,
    b_query,
    w_key,
    w_value,
    b_value,
    w_output,
    b_output,
    gain_attn,
    shift_attn,
    w_inner,
    b_inner,
    w_outer,
    b_outer,
    gain_ffn,
    shift_ffn,
    cotangent,
):
    tok_rows, width = inputs.shape
    own_rows = tok_rows // tensor
    cols = w_query.shape[1]
    z = lax.axis_index("tensor")
    own = lambda a: lax.dynamic_slice_in_dim(a, z * own_rows, own_rows, 0)
    row = lambda a: a.astype(F32)[None, :]

    vectors = row(jnp.concatenate([b_query, jnp.zeros_like(b_query), b_value, b_inner]))
    qkv_local = jnp.concatenate([w_query.T, w_key.T, w_value.T], axis=0)
    x, cot = own(inputs), own(cotangent)
    rows_of = (b_output, gain_attn, shift_attn, b_outer, gain_ffn, shift_ffn, b_outer, b_outer)
    wide_vectors = jnp.stack(rows_of).astype(F32)
    slots_at = (z - jnp.arange(tensor, dtype=jnp.int32)) % tensor
    staged = (
        dp == 8 and tensor == 4 and own_rows == LENGTH and width % 128 == 0
        and w_inner.shape == w_outer.shape == (width, width) and cols % 64 == 0
    )

    def rest_of_attention(context, weights):
        return output_forward(slots_at, x, context, weights, wide_vectors)

    def outer_half(active, weights, hidden):
        return outer_forward(active, weights, hidden, cot, wide_vectors)

    def small_sums(qkv_sums, inner_sums, sums_one, sums_two):
        by_slot = jnp.concatenate([jnp.sum(qkv_sums, axis=0), jnp.sum(inner_sums, axis=0)], axis=-1)
        by_place = by_slot[slots_at].reshape(-1)
        rest = jnp.concatenate([jnp.sum(sums_one, axis=0)[:3], jnp.sum(sums_two, axis=0)[:3]]).reshape(-1)
        return jnp.concatenate([by_place, rest])

    local_bias = vectors[:, : 3 * cols]
    context = attend_forward(inputs, qkv_local, local_bias)
    context = context.reshape(tensor, -1, context.shape[1])
    if not staged:
        vectors = jnp.stack([vectors] + across(vectors, tensor))
        qkv_bias, inner_bias = vectors[..., : 3 * cols], vectors[..., 3 * cols :]
        inner_full, output_full, outer_full, qkv_full = (
            gather_plain(w, dp, tensor) for w in (w_inner, w_output, w_outer, qkv_local)
        )
        context = lax.all_to_all(context, "tensor", 0, 0, tiled=True)
        context, hidden, hidden_bf, normed, inverse = rest_of_attention(context, output_full)
        active, slope = inner_forward(hidden_bf, inner_full, inner_bias)
        layer_out, grad_resid2, grad_outer, sums_two = outer_half(active, outer_full, hidden)
        layer_out = narrow(lax.all_gather(layer_out, "tensor", axis=0, tiled=True), own_rows)
        grad_inner, grad_resid1, grad_attn, inner_sums, sums_one = inner_backward(
            grad_outer, outer_full, slope, inner_full, grad_resid2, normed, inverse, wide_vectors
        )
        part3, grad_x, qkv_sums = attend_backward(x, grad_attn, grad_resid1, qkv_full, output_full, qkv_bias, context)
        grad_inputs = lax.all_gather(grad_x, "tensor", axis=0, tiled=True)
        gu = scatter_plain(grad_full((grad_outer, active)), tensor)
        gi = scatter_plain(grad_full((hidden_bf, grad_inner)), tensor)
        gqkv = scatter_plain(part3, tensor)
        gqkv, go = gqkv[:, : 3 * cols], gqkv[:, 3 * cols :]
        sums = lax.psum(small_sums(qkv_sums, inner_sums, sums_one, sums_two), ("dp", "tensor"))
    else:
        order = block_order(width)
        share = width // 8
        p1, p2, p3 = shares([w_inner, w_output]), shares([w_outer]), shares([qkv_local])
        n1, n2, n3 = (-(-p.shape[0] // 16) * 8 for p in (p1, p2, p3))

        z1, arrived = across(p1, tensor), across(vectors, tensor)
        vectors = jnp.stack([vectors] + arrived)
        a1, b1 = halves(z1, n1)
        a1, b1, p2, context, vectors = stage(a1, b1, p2, context, vectors)
        qkv_bias, inner_bias = vectors[..., : 3 * cols], vectors[..., 3 * cols :]

        ax, by, z2 = flip(a1, 2), flip(b1, 4), across(p2, tensor)
        a1, b1, ab1 = join(a1, ax, b1, by)
        a2, b2 = halves(z2, n2)
        a1, b1, ab1, a2, b2, context, x, order = stage(a1, b1, ab1, a2, b2, context, x, order)

        c1 = flip(ab1, 1)
        context, c1 = stage(context, c1)
        context = lax.all_to_all(context, "tensor", 0, 0, tiled=True)
        ay1, bx1, ax, by = flip(a1, 4), flip(b1, 2), flip(a2, 2), flip(b2, 4)
        a2, b2, ab2 = join(a2, ax, b2, by)
        d1 = other_core(ay1, bx1)
        ay1, bx1, a2, b2, ab2, p3 = stage(ay1, bx1, a2, b2, ab2, p3)

        c2, ay2, bx2 = flip(ab2, 1), flip(a2, 4), flip(b2, 2)
        inner_full, output_full = full_weights([w_inner, w_output], a1, b1, ay1, bx1, c1, d1)
        context, hidden, hidden_bf, normed, inverse = rest_of_attention(context, output_full)
        c2, ay2, bx2, p3, hidden_bf = stage(c2, ay2, bx2, p3, hidden_bf)

        d2, z3 = other_core(ay2, bx2), across(p3, tensor)
        active, slope = inner_forward(hidden_bf, inner_full, inner_bias)
        *d2, active = stage(*d2, active)

        (outer_full,) = full_weights([w_outer], a2, b2, ay2, bx2, c2, d2)
        layer_out, grad_resid2, grad_outer, sums_two = outer_half(active, outer_full, hidden)
        a3, b3 = halves(z3, n3)
        a3, b3, layer_out, grad_outer = stage(a3, b3, layer_out, grad_outer)

        layer_out = lax.all_gather(layer_out, "tensor", axis=0, tiled=True)
        ax, by = flip(a3, 2), flip(b3, 4)
        part1 = grad_full((grad_outer, active))
        a3, b3, ab3 = join(a3, ax, b3, by)
        a3, b3, ab3, part1, grad_outer = stage(a3, b3, ab3, part1, grad_outer)

        part1 = lax.psum_scatter(part1, "dp", scatter_dimension=0, tiled=True)
        ay3, bx3, c3 = flip(a3, 4), flip(b3, 2), flip(ab3, 1)
        grad_inner, grad_resid1, grad_attn, inner_sums, sums_one = inner_backward(
            grad_outer, outer_full, slope, inner_full, grad_resid2, normed, inverse, wide_vectors
        )
        ay3, bx3, grad_inner, grad_attn = stage(ay3, bx3, grad_inner, grad_attn)

        d3 = other_core(ay3, bx3)
        send, keep = grad_rows(order, [(hidden_bf, grad_inner)])
        *d3, send, grad_attn = stage(*d3, send, grad_attn)

        got = flip(send, 1)
        (qkv_full,) = full_weights([qkv_local], a3, b3, ay3, bx3, c3, d3)
        (a, ak), (b, bk) = split_paths(keep + got, share)
        a, b, qkv_full, grad_attn = stage(a, b, qkv_full, grad_attn)

        ax, by = flip(a, 2), flip(b, 4)
        part3, grad_x, qkv_sums = attend_backward(
            x, grad_attn, grad_resid1, qkv_full, output_full, qkv_bias, context
        )
        a, b = ak + ax, bk + by
        a_send, b_send, part3, grad_x = stage(a[:share], b[:share], part3, grad_x)

        part3 = lax.psum_scatter(part3, "dp", scatter_dimension=0, tiled=True)
        g1 = onward((grad_x, grad_x), tensor, 1)
        ay, bx = flip(a_send, 4), flip(b_send, 2)
        part2 = jnp.concatenate([a[share:] + ay, b[share:] + bx], axis=1)
        extra = small_sums(qkv_sums, inner_sums, sums_one, sums_two)
        extra = jnp.pad(extra, (0, -extra.shape[0] % (8 * width))).reshape(-1, width)
        extra = extra + flip(extra, 1)
        layer_out = narrow(layer_out, own_rows)
        first = columns(wide(part1, part2), tensor)
        g2 = onward(g1, tensor, 2)
        _, _, extra, first[0], first[1], first[2], first[3], layer_out = stage(*g1, extra, *first, layer_out)

        u, d = up(first[1], tensor, 1), down(first[3], tensor, 1)
        extra = extra + flip(extra, 2)
        g3 = onward(g2, tensor, 3)
        _, _, u, d, part3, extra = stage(*g2, first[2] + u, first[2] + d, part3, extra)

        u, d = up(u, tensor, 2), down(d, tensor, 2)
        last = columns(part3, tensor)
        v, w = up(last[1], tensor, 1), down(last[3], tensor, 1)
        extra = extra + flip(extra, 4)
        _, _, u, d, v, w, extra = stage(*g3, first[3] + u, first[1] + d, last[2] + v, last[2] + w, extra)

        u, d, v, w = up(u, tensor, 3), down(d, tensor, 3), up(v, tensor, 2), down(w, tensor, 2)
        extra = extra + swap(extra, tensor, 1)
        grad_inputs = place(grad_x, [g1[0], g2[0], g3[0]], [g1[1], g2[1], g3[1]])
        gu = first[0] + u + d
        v, w, extra, gu, grad_inputs = stage(last[3] + v, last[1] + w, extra, gu, grad_inputs)

        gqkv = last[0] + up(v, tensor, 3) + down(w, tensor, 3)
        extra = extra + swap(extra, tensor, 2)
        gu, gi = gu[:share], gu[share:]
        gqkv, go = gqkv[:, : 3 * cols], gqkv[:, 3 * cols :]
        sums = extra.reshape(-1)

    span = 3 * cols + w_inner.shape[1]
    mine = lax.dynamic_slice_in_dim(sums, z * span, span, 0)
    rest = sums[span * tensor :][: 6 * width].reshape(6, width)
    return (
        layer_out,
        grad_inputs,
        gqkv[:, :cols],
        mine[:cols],
        gqkv[:, cols : 2 * cols],
        gqkv[:, 2 * cols :],
        mine[2 * cols : 3 * cols],
        go.T,
        rest[2],
        rest[0],
        rest[1],
        gi,
        mine[3 * cols :],
        gu.T,
        rest[5],
        rest[3],
        rest[4],
    )


def solution(mesh):
    wide, tall, vector = P(None, "tensor"), P("tensor", None), P("tensor")
    tokens, both = P("dp", None), P("dp", "tensor")
    in_specs = (
        tokens, wide, vector, wide, wide, vector, tall, P(), P(), P(), wide, vector, tall, P(), P(), P(), tokens,
    )
    out_specs = (
        tokens, tokens, both, vector, both, both, vector, P("tensor", "dp"), P(), P(), P(), both, vector,
        P("tensor", "dp"), P(), P(), P(),
    )
    body = partial(shards, mesh.shape["dp"], mesh.shape["tensor"])
    return jax.shard_map(body, mesh=mesh, in_specs=in_specs, out_specs=out_specs, check_vma=False)
```

```python
import math
from functools import partial
from typing import NamedTuple

import jax
import jax.numpy as jnp
from jax import lax
from jax.experimental import pallas as pl
from jax.experimental.pallas import tpu as pltpu
from jax.sharding import PartitionSpec as P

HEAD_DIM = 64
LENGTH = 512
EPSILON = 1e-12
F32 = jnp.float32
BF16 = jnp.bfloat16
SCALE = HEAD_DIM ** (-0.5)
EXP_SCALE = SCALE * 1.4426950408889634
ROWS = ((0,), (0,))
PLAIN = ((1,), (0,))
COLS = ((1,), (1,))


def dot(left, right, dims):
    return lax.dot_general(left, right, (dims, ((), ())), preferred_element_type=F32)


def norm_forward(values, gain, shift):
    center = values - jnp.mean(values, axis=-1, keepdims=True)
    inverse = lax.rsqrt(jnp.mean(center * center, axis=-1, keepdims=True) + EPSILON)
    normed = center * inverse
    return (normed * gain + shift, normed, inverse)


def norm_backward(upstream, gain, normed, inverse):
    scaled = upstream * gain
    first_mean = jnp.mean(scaled, axis=-1, keepdims=True)
    cross_mean = jnp.mean(scaled * normed, axis=-1, keepdims=True)
    return inverse * (scaled - first_mean - normed * cross_mean)


def by_rows(rows, step, body, carry=()):
    return lax.fori_loop(0, rows // step, lambda i, c: body(pl.ds(pl.multiple_of(i * step, step), step), c), carry)


def row_sums(values):
    return jnp.sum(values, axis=0, keepdims=True)


def size_of(shape, dtype):
    return math.prod(shape) * jnp.dtype(dtype).itemsize


def call(kernel, name, grid, ins, outs, flops, exps=0, scratch=(), prefetch=None, moved=None):
    if moved is None:
        moved = sum(size_of(a.shape, a.dtype) for a, _, _ in ins) + sum(size_of(s, t) for s, t, _, _ in outs)
    lead = () if prefetch is None else (prefetch,)
    return pl.pallas_call(
        kernel,
        grid_spec=pltpu.PrefetchScalarGridSpec(
            num_scalar_prefetch=len(lead),
            grid=grid,
            in_specs=[pl.BlockSpec(memory_space=m) if b is None else pl.BlockSpec(b, m) for _, b, m in ins],
            out_specs=[pl.BlockSpec(b, m) for _, _, b, m in outs],
            scratch_shapes=list(scratch),
        ),
        out_shape=[jax.ShapeDtypeStruct(s, t) for s, t, _, _ in outs],
        cost_estimate=pl.CostEstimate(flops=flops, bytes_accessed=moved, transcendentals=exps),
        compiler_params=pltpu.CompilerParams(vmem_limit_bytes=56 << 20),
        name=name,
    )(*lead, *(a for a, _, _ in ins))


class Stream(NamedTuple):
    local: jax.Array
    target: int
    pieces: list


def plan_of(locals_, pieces, wanted):
    plan, where = [], []
    for _, parts in pieces:
        plan.append([])
        for entry, sender, base, spans in parts:
            for row, rows, target, offset in spans:
                if target in wanted:
                    plan[-1].append((entry, base + row, rows, wanted.index(target)))
                    where.append(sender * (locals_[wanted.index(target)].shape[0] // 8) + offset)
    return plan, jnp.stack(where)


def piece_copies(plan, where_ref, pieces, holds, sems):
    found = []
    for piece, spans in zip(pieces, plan):
        for i, source, rows, target in spans:
            start = pl.multiple_of(where_ref[len(found)], 8)
            found.append(
                pltpu.make_async_copy(
                    piece.at[i, :, pl.ds(source, rows)], holds[target].at[:, pl.ds(start, rows)], sems.at[len(found)]
                )
            )
    return found


def call_with(body, name, grid, slot_of, weights, ins, outs, flops, exps=0, prefetch=None):
    axes = len(grid)
    at = lambda *ids: (slot_of(*ids[:axes]), 0, 0)
    if not isinstance(weights, Stream):
        ins = [(weights, (None,) + weights.shape[1:], at)] + ins
        if prefetch is not None:
            return *call(lambda _, *refs: body(*refs), name, grid, ins, outs, flops, exps, prefetch=prefetch), weights
        return *call(body, name, grid, ins, outs, flops, exps), weights
    local, target, pieces = weights
    others = pieces[0][0].shape[1]
    plan, where = plan_of([local], pieces, [target])
    used = [n for n, spans in enumerate(plan) if spans]
    plan, arrays = [plan[n] for n in used], [pieces[n][0] for n in used]
    lead, count, inner = int(prefetch is not None), len(arrays), len(ins)

    def kernel(*refs):
        refs = refs[lead:]
        where_ref, local_ref, refs = refs[0], refs[1], refs[2:]
        piece_refs, refs = refs[:count], refs[count:]
        full_ref, hold, sems = refs[-3:]
        ids = [pl.program_id(n) for n in range(axes)]
        slot = slot_of(*ids)
        first = sum(ids) == slot
        moves = piece_copies(plan, where_ref, piece_refs, [hold], sems)

        @pl.when(jnp.logical_and(first, slot == 0))
        def _():
            for move in moves:
                move.start()
            full_ref[...] = local_ref[...]

        @pl.when(jnp.logical_and(first, slot == 1))
        def _():
            for move in moves:
                move.wait()

        @pl.when(jnp.logical_and(first, slot > 0))
        def _():
            full_ref[...] = hold[jnp.maximum(slot - 1, 0)].astype(BF16)

        body(full_ref, *refs[:-3])

    rows, width = local.shape
    flat = lambda *ids: (0, 0)
    more = [(where, None, pltpu.SMEM), (local, local.shape, flat)] + [(a, None, pl.ANY) for a in arrays]
    full = ((others + 1, rows, width), BF16, (None, rows, width), at)
    scratch = [pltpu.VMEM((others, rows, width), F32), pltpu.SemaphoreType.DMA((where.shape[0],))]
    return call(kernel, name, grid, more + ins, outs + [full], flops, exps, scratch, prefetch)


def attend_kernel(x_ref, w_ref, bias_ref, ctx_ref):
    cols = w_ref.shape[0] // 3
    parts = []
    qkv = (dot(x_ref[...], w_ref[...], COLS) + bias_ref[...]).astype(BF16)
    for h in range(cols // HEAD_DIM):
        q, k, v = (qkv[:, i * cols + h * HEAD_DIM : i * cols + (h + 1) * HEAD_DIM] for i in range(3))
        scores = dot(q, k, COLS)
        largest = jnp.max(scores, axis=-1, keepdims=True)
        expon = jnp.exp2((scores - largest) * EXP_SCALE)
        totals = jnp.sum(expon, axis=-1, keepdims=True)
        parts.append((dot(expon.astype(BF16), v, PLAIN) / totals).astype(BF16).astype(F32))
    context = jnp.concatenate(parts, axis=1)
    step = ctx_ref.shape[0]
    folds = [context[i * step : (i + 1) * step] for i in range(LENGTH // step)]
    ctx_ref[...] = jnp.concatenate(folds, axis=1)


def fold_of(cols):
    return 1 if cols % 128 == 0 else 2


def attend_forward(inputs, weights, bias):
    rows, width = inputs.shape
    cols = weights.shape[0] // 3
    fold = fold_of(cols)
    flat = lambda i: (0, 0)
    return call(
        attend_kernel,
        "attend_forward",
        (rows // LENGTH,),
        [
            (inputs, (LENGTH, width), lambda i: (i, 0)),
            (weights, weights.shape, flat),
            (bias, bias.shape, flat),
        ],
        [((rows // fold, fold * cols), F32, (LENGTH // fold, fold * cols), lambda i: (i, 0))],
        flops=rows * cols * (6 * width + 4 * LENGTH),
        exps=rows * LENGTH * (cols // HEAD_DIM),
    )[0]


def output_kernel(w_ref, x_ref, ctx_ref, vec_ref, low_ref, hid_ref, hbf_ref, nrm_ref, inv_ref):
    slot = pl.program_id(1)
    cols = low_ref.shape[-1]
    folds = [ctx_ref[:, i : i + cols] for i in range(0, ctx_ref.shape[-1], cols)]
    context = jnp.concatenate(folds, axis=0).astype(BF16)
    low_ref[...] = context
    attn = dot(context, w_ref[...], PLAIN)

    @pl.when(slot == 0)
    def _():
        hid_ref[...] = attn

    @pl.when(slot > 0)
    def _():
        hid_ref[...] += attn

    @pl.when(slot == pl.num_programs(1) - 1)
    def _():
        bias, gain, shift = vec_ref[0:1], vec_ref[1:2], vec_ref[2:3]

        def block(at, carry):
            values = x_ref[at].astype(F32) + hid_ref[at] + bias
            hidden, normed, inverse = norm_forward(values, gain, shift)
            hid_ref[at] = hidden
            hbf_ref[at] = hidden.astype(BF16)
            nrm_ref[at] = normed
            inv_ref[at] = inverse
            return carry

        by_rows(LENGTH, 256, block)


def output_forward(slots_at, x, context, weights, vectors):
    rows, width = x.shape
    slots = slots_at.shape[0]
    cols = width // slots
    mine = lambda i, j, at: (i, 0)
    flat = lambda i, j, at: (0, 0)
    token = (LENGTH, width)
    heads = (None, LENGTH, cols)
    return call_with(
        output_kernel,
        "output_forward",
        (rows // LENGTH, slots),
        lambda i, j: j,
        weights,
        [
            (x, token, mine),
            (context, (None, LENGTH // fold_of(cols), fold_of(cols) * cols), lambda i, j, at: (at[j], i, 0)),
            (vectors, vectors.shape, flat),
        ],
        [
            ((slots, rows, cols), BF16, heads, lambda i, j, at: (j, i, 0)),
            ((rows, width), F32, token, mine),
            ((rows, width), BF16, token, mine),
            ((rows, width), F32, token, mine),
            ((rows, 1), F32, (LENGTH, 1), mine),
        ],
        flops=2 * rows * width * width,
        prefetch=slots_at,
    )


def attend_back_kernel(x_ref, ga_ref, gr_ref, w_ref, wo_ref, bias_ref, ctx_ref, gw_ref, gx_ref, sum_ref, gqkv_ref):
    slot = pl.program_id(1)
    cols = wo_ref.shape[0]
    gctx = dot(ga_ref[...], wo_ref[...], COLS).astype(BF16)
    qkv = (dot(x_ref[...], w_ref[...], COLS) + bias_ref[...]).astype(BF16)
    for h in range(cols // HEAD_DIM):
        at = [slice(i * cols + h * HEAD_DIM, i * cols + (h + 1) * HEAD_DIM) for i in range(3)]
        q, k, v = (qkv[:, s] for s in at)
        g = gctx[:, at[0]]
        scores = dot(k, q, COLS)
        largest = jnp.max(scores, axis=0, keepdims=True)
        expon = jnp.exp2((scores - largest) * EXP_SCALE)
        probs = expon * (1.0 / row_sums(expon))
        gqkv_ref[:, at[2]] = dot(probs.astype(BF16), g, PLAIN).astype(BF16)
        weighted = probs * dot(v, g, COLS)
        grad_scores = (weighted - probs * row_sums(weighted)).astype(BF16)
        gqkv_ref[:, at[0]] = (dot(grad_scores, k, ROWS) * SCALE).astype(BF16)
        gqkv_ref[:, at[1]] = (dot(grad_scores, q, PLAIN) * SCALE).astype(BF16)
    grads = gqkv_ref[...]
    sum_ref[...] = row_sums(grads.astype(F32))
    back = dot(grads, w_ref[...], PLAIN)
    gw_ref[:, : 3 * cols] = dot(x_ref[...], grads, ROWS)
    gw_ref[:, 3 * cols :] = dot(ga_ref[...], ctx_ref[...], ROWS)

    @pl.when(slot == 0)
    def _():
        gx_ref[...] = gr_ref[...] + back

    @pl.when(slot > 0)
    def _():
        gx_ref[...] += back


def attend_backward(x, grad_attn, grad_resid, weights, w_output, bias, context):
    rows, width = grad_attn.shape
    slots, cols, _ = w_output.shape
    mine = lambda i, j: (i, 0)
    token = (LENGTH, width)
    weight = lambda i, j: (j, 0, 0)
    return call(
        attend_back_kernel,
        "attend_backward",
        (rows // LENGTH, slots),
        [
            (x, token, mine),
            (grad_attn, token, mine),
            (grad_resid, token, mine),
            (weights, (None, 3 * cols, width), weight),
            (w_output, (None, cols, width), weight),
            (bias, (None, 1, 3 * cols), weight),
            (context, (None, LENGTH, cols), lambda i, j: (j, i, 0)),
        ],
        [
            ((width, slots * 4 * cols), F32, (width, 4 * cols), lambda i, j: (0, j)),
            ((rows, width), F32, token, mine),
            ((rows // LENGTH, slots, 1, 3 * cols), F32, (None, None, 1, 3 * cols), lambda i, j: (i, j, 0, 0)),
        ],
        flops=0,
        moved=0,
        scratch=[pltpu.VMEM((LENGTH, 3 * cols), BF16)],
    )


def inner_kernel(w_ref, h_ref, b_ref, act_ref, slope_ref):
    inner = dot(h_ref[...], w_ref[...], PLAIN) + b_ref[...]
    phi = 0.5 + 0.5 * lax.erf(inner * (0.5**0.5))
    bell = jnp.exp2(inner * inner * (-0.5 * 1.4426950408889634)) * 0.3989422804014327
    act_ref[...] = (inner * phi).astype(BF16)
    slope_ref[...] = phi + inner * bell


def inner_forward(hidden, weights, bias):
    rows, width = hidden.shape
    slots, _, units = bias.shape
    slot = lambda i, j: (i, j, 0)
    block = LENGTH // 2
    return call_with(
        inner_kernel,
        "inner_forward",
        (slots, rows // block),
        lambda i, j: i,
        weights,
        [
            (hidden, (block, width), lambda i, j: (j, 0)),
            (bias, (None, 1, units), lambda i, j: (i, 0, 0)),
        ],
        [
            ((slots, rows, units), BF16, (None, block, units), slot),
            ((slots, rows, units), F32, (None, block, units), slot),
        ],
        flops=2 * rows * width * slots * units,
        exps=2 * rows * slots * units,
    )


def outer_kernel(w_ref, act_ref, hid_ref, vec_ref, out_ref, nrm_ref, inv_ref):
    slot = pl.program_id(1)
    outer = dot(act_ref[...], w_ref[...], PLAIN)

    @pl.when(slot == 0)
    def _():
        out_ref[...] = outer

    @pl.when(slot > 0)
    def _():
        out_ref[...] += outer

    @pl.when(slot == pl.num_programs(1) - 1)
    def _():
        bias, gain, shift = vec_ref[3:4], vec_ref[4:5], vec_ref[5:6]

        def block(at, carry):
            values = hid_ref[at] + (out_ref[at] + bias)
            layer_out, normed, inverse = norm_forward(values, gain, shift)
            out_ref[at] = layer_out
            nrm_ref[at] = normed
            inv_ref[at] = inverse
            return carry

        by_rows(LENGTH, 256, block)


def outer_forward(active, weights, hidden, vectors):
    rows, width = hidden.shape
    slots, _, units = active.shape
    mine = lambda i, j: (i, 0)
    token = (LENGTH, width)
    return call_with(
        outer_kernel,
        "outer_forward",
        (rows // LENGTH, slots),
        lambda i, j: j,
        weights,
        [
            (active, (None, LENGTH, units), lambda i, j: (j, i, 0)),
            (hidden, token, mine),
            (vectors, vectors.shape, lambda i, j: (0, 0)),
        ],
        [
            ((rows, width), F32, token, mine),
            ((rows, width), F32, token, mine),
            ((rows, 1), F32, (LENGTH, 1), mine),
        ],
        flops=2 * rows * width * slots * units,
    )


def last_norm_kernel(cot_ref, nrm_ref, inv_ref, vec_ref, gr_ref, go_ref, sum_ref):
    upstream, normed = cot_ref[...].astype(F32), nrm_ref[...]
    grad = norm_backward(upstream, vec_ref[4:5], normed, inv_ref[...])
    rounded = grad.astype(BF16)
    gr_ref[...] = grad
    go_ref[...] = rounded
    found = (upstream * normed, upstream, rounded.astype(F32))

    @pl.when(pl.program_id(0) == 0)
    def _():
        sum_ref[...] = jnp.zeros_like(sum_ref)

    for i, value in enumerate(found):
        sum_ref[i : i + 1] += row_sums(value)


def last_norm_backward(cotangent, normed, inverse, vectors):
    rows, width = normed.shape
    block = 128
    mine = lambda i: (i, 0)
    flat = lambda i: (0, 0)
    token = (block, width)
    return call(
        last_norm_kernel,
        "last_norm_backward",
        (rows // block,),
        [
            (cotangent, token, mine),
            (normed, token, mine),
            (inverse, (block, 1), mine),
            (vectors, vectors.shape, flat),
        ],
        [
            ((rows, width), F32, token, mine),
            ((rows, width), BF16, token, mine),
            ((8, width), F32, (8, width), flat),
        ],
        flops=0,
        moved=0,
    )


def inner_back_kernel(go_ref, wu_ref, slope_ref, wi_ref, gr_ref, nrm_ref, inv_ref, vec_ref,
                      gi_ref, g1_ref, ga_ref, bsum_ref, sum_ref):
    slot = pl.program_id(1)
    grad_inner = (dot(go_ref[...], wu_ref[...], COLS) * slope_ref[...]).astype(BF16)
    gi_ref[...] = grad_inner
    bsum_ref[...] = row_sums(grad_inner.astype(F32))
    back = dot(grad_inner, wi_ref[...], COLS)

    @pl.when(slot == 0)
    def _():
        g1_ref[...] = gr_ref[...] + back

    @pl.when(slot > 0)
    def _():
        g1_ref[...] += back

    @pl.when(slot == pl.num_programs(1) - 1)
    def _():
        gain = vec_ref[1:2]

        def block(at, sums):
            upstream, normed = g1_ref[at], nrm_ref[at]
            grad = norm_backward(upstream, gain, normed, inv_ref[at])
            rounded = grad.astype(BF16)
            g1_ref[at] = grad
            ga_ref[at] = rounded
            found = (upstream * normed, upstream, rounded.astype(F32))
            return tuple(s + row_sums(f) for s, f in zip(sums, found))

        for i, total in enumerate(by_rows(LENGTH, 256, block, (jnp.zeros_like(gain),) * 3)):
            sum_ref[i : i + 1] = total


def inner_backward(grad_outer, w_outer, slope, w_inner, grad_resid2, normed, inverse, vectors):
    rows, width = grad_outer.shape
    slots, units, _ = w_outer.shape
    mine = lambda i, j: (i, 0)
    token = (LENGTH, width)
    slot = lambda i, j: (j, i, 0)
    weight = lambda i, j: (j, 0, 0)
    return call(
        inner_back_kernel,
        "inner_backward",
        (rows // LENGTH, slots),
        [
            (grad_outer, token, mine),
            (w_outer, (None, units, width), weight),
            (slope, (None, LENGTH, units), slot),
            (w_inner, (None, width, units), weight),
            (grad_resid2, token, mine),
            (normed, token, mine),
            (inverse, (LENGTH, 1), mine),
            (vectors, vectors.shape, lambda i, j: (0, 0)),
        ],
        [
            ((slots, rows, units), BF16, (None, LENGTH, units), slot),
            ((rows, width), F32, token, mine),
            ((rows, width), BF16, token, mine),
            ((rows // LENGTH, slots, 1, units), F32, (None, None, 1, units), lambda i, j: (i, j, 0, 0)),
            ((rows // LENGTH, 8, width), F32, (None, 8, width), lambda i, j: (i, 0, 0)),
        ],
        flops=0,
        moved=0,
    )


def narrow_kernel(x_ref, out_ref):
    out_ref[...] = x_ref[...].astype(BF16)


def narrow(values, block_rows):
    rows, width = values.shape
    at = lambda i: (i, 0)
    block = (block_rows, width)
    out = ((rows, width), BF16, block, at)
    return call(narrow_kernel, "narrow", (rows // block_rows,), [(values, block, at)], [out], 0)[0]


def shift_to(values, tensor, k):
    return lax.ppermute(values, "tensor", [(i, (i + k) % tensor) for i in range(tensor)])


def flip(values, bit):
    return lax.ppermute(values, "dp", [(i, i ^ bit) for i in range(8)])


def stage(*values):
    return lax.optimization_barrier(values)


def slots_kernel(slot_ref, local_ref, x_ref, out_ref):
    del slot_ref
    first = pl.program_id(0) == 0

    @pl.when(first)
    def _():
        out_ref[...] = local_ref[...]

    @pl.when(jnp.logical_not(first))
    def _():
        out_ref[...] = x_ref[...].reshape(out_ref.shape).astype(BF16)


def gather_plain(local, dp, tensor):
    rows, width = local.shape
    share = rows // dp
    piece = lax.dynamic_slice_in_dim(local, lax.axis_index("dp") * share, share, 0).astype(F32)
    full = lax.all_gather(piece, ("dp", "tensor"), axis=0).reshape(dp, tensor, share, width)
    order = (lax.axis_index("tensor") - jnp.arange(tensor, dtype=jnp.int32)) % tensor
    if share % 8:
        full = full.swapaxes(0, 1).reshape(1, tensor, rows, width)
    lead, _, part, _ = full.shape
    return pl.pallas_call(
        slots_kernel,
        grid_spec=pltpu.PrefetchScalarGridSpec(
            num_scalar_prefetch=1,
            grid=(tensor,),
            in_specs=[
                pl.BlockSpec((rows, width), lambda i, slot: (0, 0)),
                pl.BlockSpec((lead, None, part, width), lambda i, slot: (0, slot[i], 0, 0)),
            ],
            out_specs=pl.BlockSpec((None, rows, width), lambda i, slot: (i, 0, 0)),
        ),
        out_shape=jax.ShapeDtypeStruct((tensor, rows, width), BF16),
        cost_estimate=pl.CostEstimate(flops=0, bytes_accessed=6 * full.size, transcendentals=0),
        compiler_params=pltpu.CompilerParams(vmem_limit_bytes=48 << 20),
        name="slots",
    )(order, local, full)


def assemble_kernel(plan, where_ref, local_ref, *refs):
    *pieces, out_ref, hold, sems = refs
    moves = piece_copies(plan, where_ref, pieces, [hold], sems)
    for move in moves:
        move.start()
    out_ref[0] = local_ref[...]
    for move in moves:
        move.wait()
    for k in range(hold.shape[0]):

        def block(at, carry, k=k):
            out_ref[k + 1, at] = hold[k, at].astype(BF16)
            return carry

        by_rows(hold.shape[1], 96, block)


def assemble(stream):
    local, target, pieces = stream
    rows, width = local.shape
    others = pieces[0][0].shape[1]
    plan, where = plan_of([local], pieces, [target])
    space = pl.BlockSpec(memory_space=pltpu.VMEM)
    return pl.pallas_call(
        partial(assemble_kernel, plan),
        in_specs=[pl.BlockSpec(memory_space=pltpu.SMEM), space] + [pl.BlockSpec(memory_space=pl.ANY)] * len(pieces),
        out_specs=space,
        out_shape=jax.ShapeDtypeStruct((others + 1, rows, width), BF16),
        scratch_shapes=[pltpu.VMEM((others, rows, width), F32), pltpu.SemaphoreType.DMA((where.shape[0],))],
        cost_estimate=pl.CostEstimate(flops=0, bytes_accessed=others * rows * width * 6, transcendentals=0),
        compiler_params=pltpu.CompilerParams(vmem_limit_bytes=48 << 20),
        name="assemble",
    )(where, local, *(array for array, _ in pieces))


def shares(weights, dp=8):
    me = lax.axis_index("dp")
    cut = [lax.dynamic_slice_in_dim(w, me * (w.shape[0] // dp), w.shape[0] // dp, 0) for w in weights]
    return jnp.concatenate(cut, axis=0).astype(F32)


def across(values, tensor):
    return [shift_to(values, tensor, k) for k in range(1, tensor)]


def wide(v, w):
    return jnp.concatenate([v, w], axis=0)


def other_core(*values):
    return tuple(flip(v, 1) for v in values)


def copy_kernel(plan, count, *refs):
    ins, outs = refs[:count], refs[count:]
    for source, source_at, target, target_at in plan:
        outs[target][target_at] = ins[source][source_at]


def copies(ins, shapes, plan):
    space = pl.BlockSpec(memory_space=pltpu.VMEM)
    return pl.pallas_call(
        partial(copy_kernel, plan, len(ins)),
        in_specs=[space] * len(ins),
        out_specs=[space] * len(shapes),
        out_shape=[jax.ShapeDtypeStruct(shape, F32) for shape in shapes],
        cost_estimate=pl.CostEstimate(flops=0, bytes_accessed=0, transcendentals=0),
        compiler_params=pltpu.CompilerParams(vmem_limit_bytes=32 << 20),
        name="copies",
    )(*ins)


def halves(arrived, upper):
    rows, width = arrived[0].shape
    n = len(arrived)
    plan = [(k, (slice(0, upper),), 0, (0, k)) for k in range(n)]
    plan += [(k, (slice(upper, rows),), 1, (0, k)) for k in range(n)]
    return copies(arrived, [(1, n, upper, width), (1, n, rows - upper, width)], plan)


def join(a, ax, b, by):
    _, n, upper, width = a.shape
    lower = b.shape[2]
    plan = []
    for i, (v, w) in enumerate(((a, b), (ax, by))):
        every = slice(None)
        plan += [(2 * i, (0,), 0, (i,)), (2 * i + 1, (0,), 1, (i,))]
        plan += [(2 * i, (0,), 2, (i, every, slice(0, upper))), (2 * i + 1, (0,), 2, (i, every, slice(upper, upper + lower)))]
    shapes = [(2, n, upper, width), (2, n, lower, width), (2, n, upper + lower, width)]
    return copies([a, b, ax, by], shapes, plan)


def pieces_of(locals_, a, b, ay, bx, c, d):
    me = lax.axis_index("dp")
    cut_at, end = a.shape[2], a.shape[2] + b.shape[2]
    ends = [0]
    for w in locals_:
        ends.append(ends[-1] + w.shape[0] // 8)

    def spans(first, last):
        found = []
        for target in range(len(locals_)):
            low, high = max(first, ends[target]), min(last, ends[target + 1])
            if low < high:
                found.append((low - first, high - low, target, low - ends[target]))
        return found

    upper = lambda rels: [(i, me ^ r, 0, spans(0, cut_at)) for i, r in enumerate(rels)]
    lower = lambda rels, base=0: [(i, me ^ r, base, spans(cut_at, end)) for i, r in enumerate(rels)]
    return [
        (a, upper((0, 2))),
        (b, lower((0, 4))),
        (ay, upper((4, 6))),
        (bx, lower((2, 6))),
        (c, upper((1, 3)) + lower((1, 5), cut_at)),
        (d[0], upper((5, 7))),
        (d[1], lower((3, 7))),
    ]


def block_order(width):
    me = lax.axis_index("dp")
    share = width // 8
    rel = jnp.array([7, 5, 3, 1, 6, 4, 2, 0])
    source = (me ^ rel[jnp.arange(width) // share]) * share + jnp.arange(width) % share
    return (lax.broadcasted_iota(jnp.int32, (width, width), 0) == source[None, :]).astype(BF16)


def grad_kernel(count, *refs):
    order_ref, refs = refs[0], refs[1:]
    lefts, rights, (send_ref, keep_ref), holds = (
        refs[:count], refs[count : 2 * count], refs[2 * count : 2 * count + 2], refs[2 * count + 2 :],
    )

    @pl.when(pl.program_id(0) == 0)
    def _():
        for left, hold in zip(lefts, holds):
            hold[...] = dot(left[...], order_ref[...], PLAIN).astype(BF16)

    half = send_ref.shape[0]
    start = 0
    for hold, right in zip(holds, rights):
        span = slice(start, start + right.shape[-1])
        value = dot(hold[...], right[...], ROWS)
        send_ref[:, span] = value[:half]
        keep_ref[:, span] = value[half:]
        start = span.stop


def grad_rows(order, pairs):
    rows, width = pairs[0][0].shape
    slots = pairs[0][1].shape[0]
    cols = sum(r.shape[-1] for _, r in pairs)
    flat = lambda j: (0, 0)
    ins = [(order, order.shape, flat)]
    ins += [(left, left.shape, flat) for left, _ in pairs]
    ins += [(right, (None,) + right.shape[1:], lambda j: (j, 0, 0)) for _, right in pairs]
    out = ((width // 2, slots * cols), F32, (width // 2, cols), lambda j: (0, j))
    scratch = [pltpu.VMEM((rows, width), BF16)] * len(pairs)
    return call(
        partial(grad_kernel, len(pairs)), "grad_rows", (slots,), ins, [out, out], 0, 0, scratch, moved=0
    )


def full_kernel(count, *refs):
    lefts, rights, out_ref = refs[:count], refs[count:-1], refs[-1]
    start = 0
    for left, right in zip(lefts, rights):
        span = slice(start, start + right.shape[-1])
        out_ref[:, span] = dot(left[...], right[...], ROWS)
        start = span.stop


def grad_full(*pairs):
    rows, width = pairs[0][0].shape
    slots = pairs[0][1].shape[0]
    cols = sum(r.shape[-1] for _, r in pairs)
    ins = [(left, left.shape, lambda j: (0, 0)) for left, _ in pairs]
    ins += [(right, (None,) + right.shape[1:], lambda j: (j, 0, 0)) for _, right in pairs]
    return call(
        partial(full_kernel, len(pairs)),
        "grad_full",
        (slots,),
        ins,
        [((width, slots * cols), F32, (width, cols), lambda j: (0, j))],
        flops=0,
        moved=0,
    )[0]


def split_paths(held, share):
    mid = held.shape[1] // 2
    pick = lambda i, cols: held[i * share : (i + 1) * share, cols]
    a, b = slice(None, mid), slice(mid, None)
    join = lambda i, j, cols: jnp.concatenate([pick(i, cols), pick(j, cols)], axis=0)
    return (join(0, 2, a), join(1, 3, a)), (join(0, 1, b), join(2, 3, b))


def scatter_plain(grad, tensor):
    part = lax.psum_scatter(grad, "dp", scatter_dimension=0, tiled=True)
    part = columns(part, tensor)
    return sum((shift_to(part[k], tensor, tensor - k) for k in range(1, tensor)), part[0])


def columns(part, tensor):
    cols = part.shape[1] // tensor
    return [part[:, k * cols : (k + 1) * cols] for k in range(tensor)]


def up(values, tensor, step):
    return lax.ppermute(values, "tensor", [(i, i + 1) for i in range(step)])


def down(values, tensor, step):
    return lax.ppermute(values, "tensor", [(i, i - 1) for i in range(tensor - step, tensor)])


def place_kernel(z_ref, own_ref, *refs):
    *others, out_ref = refs
    count = len(others) // 2
    below, above = others[:count], others[count:]
    away = pl.program_id(0) - z_ref[0]

    @pl.when(away == 0)
    def _():
        out_ref[...] = own_ref[...]

    for k in range(count):

        @pl.when(away == -(k + 1))
        def _(k=k):
            out_ref[...] = below[k][...]

        @pl.when(away == k + 1)
        def _(k=k):
            out_ref[...] = above[k][...]


def place(own, below, above):
    rows, width = own.shape
    count = len(below) + 1
    whole = (rows, width)
    return call(
        place_kernel,
        "place",
        (count,),
        [(v, whole, lambda i, z: (0, 0)) for v in (own, *below, *above)],
        [((count * rows, width), F32, whole, lambda i, z: (i, 0))],
        flops=0,
        moved=0,
        prefetch=lax.axis_index("tensor").astype(jnp.int32).reshape(1),
    )[0]


def onward(values, tensor, step):
    u, d = values
    u = lax.ppermute(u, "tensor", [(i, i + 1) for i in range(step - 1, tensor - 1)])
    d = lax.ppermute(d, "tensor", [(i, i - 1) for i in range(1, tensor - step + 1)])
    return u, d


def swap(values, tensor, bit):
    return lax.ppermute(values, "tensor", [(i, i ^ bit) for i in range(tensor)])


def shards(
    dp,
    tensor,
    inputs,
    w_query,
    b_query,
    w_key,
    w_value,
    b_value,
    w_output,
    b_output,
    gain_attn,
    shift_attn,
    w_inner,
    b_inner,
    w_outer,
    b_outer,
    gain_ffn,
    shift_ffn,
    cotangent,
):
    tok_rows, width = inputs.shape
    own_rows = tok_rows // tensor
    cols = w_query.shape[1]
    z = lax.axis_index("tensor")
    own = lambda a: lax.dynamic_slice_in_dim(a, z * own_rows, own_rows, 0)
    row = lambda a: a.astype(F32)[None, :]

    vectors = row(jnp.concatenate([b_query, jnp.zeros_like(b_query), b_value, b_inner]))
    qkv_local = jnp.concatenate([w_query.T, w_key.T, w_value.T], axis=0)
    x, cot = own(inputs), own(cotangent)
    rows_of = (b_output, gain_attn, shift_attn, b_outer, gain_ffn, shift_ffn, b_outer, b_outer)
    wide_vectors = jnp.stack(rows_of).astype(F32)
    slots_at = (z - jnp.arange(tensor, dtype=jnp.int32)) % tensor
    staged = (
        dp == 8 and tensor == 4 and own_rows == LENGTH and width % 128 == 0
        and w_inner.shape == w_outer.shape == (width, width) and cols % 64 == 0
    )

    def rest_of_attention(context, weights):
        return output_forward(slots_at, x, context, weights, wide_vectors)


    def small_sums(qkv_sums, inner_sums, sums_one, sums_two):
        by_slot = jnp.concatenate([jnp.sum(qkv_sums, axis=0), jnp.sum(inner_sums, axis=0)], axis=-1)
        by_place = by_slot[slots_at].reshape(-1)
        rest = jnp.concatenate([jnp.sum(sums_one, axis=0)[:3], sums_two[:3]]).reshape(-1)
        return jnp.concatenate([by_place, rest])

    local_bias = vectors[:, : 3 * cols]
    context = attend_forward(inputs, qkv_local, local_bias)
    context = context.reshape(tensor, -1, context.shape[1])
    if not staged:
        vectors = jnp.stack([vectors] + across(vectors, tensor))
        qkv_bias, inner_bias = vectors[..., : 3 * cols], vectors[..., 3 * cols :]
        inner_full, output_full, outer_full, qkv_full = (
            gather_plain(w, dp, tensor) for w in (w_inner, w_output, w_outer, qkv_local)
        )
        context = lax.all_to_all(context, "tensor", 0, 0, tiled=True)
        context, hidden, hidden_bf, normed, inverse, output_full = rest_of_attention(context, output_full)
        active, slope, inner_full = inner_forward(hidden_bf, inner_full, inner_bias)
        layer_out, normed_two, inverse_two, outer_full = outer_forward(active, outer_full, hidden, wide_vectors)
        grad_resid2, grad_outer, sums_two = last_norm_backward(cot, normed_two, inverse_two, wide_vectors)
        layer_out = narrow(lax.all_gather(layer_out, "tensor", axis=0, tiled=True), own_rows)
        grad_inner, grad_resid1, grad_attn, inner_sums, sums_one = inner_backward(
            grad_outer, outer_full, slope, inner_full, grad_resid2, normed, inverse, wide_vectors
        )
        part3, grad_x, qkv_sums = attend_backward(x, grad_attn, grad_resid1, qkv_full, output_full, qkv_bias, context)
        grad_inputs = lax.all_gather(grad_x, "tensor", axis=0, tiled=True)
        gu = scatter_plain(grad_full((grad_outer, active)), tensor)
        gi = scatter_plain(grad_full((hidden_bf, grad_inner)), tensor)
        gqkv = scatter_plain(part3, tensor)
        gqkv, go = gqkv[:, : 3 * cols], gqkv[:, 3 * cols :]
        sums = lax.psum(small_sums(qkv_sums, inner_sums, sums_one, sums_two), ("dp", "tensor"))
    else:
        order = block_order(width)
        share = width // 8
        p1, p2, p3 = shares([w_inner, w_output]), shares([w_outer]), shares([qkv_local])
        n1, n2, n3 = (-(-p.shape[0] // 16) * 8 for p in (p1, p2, p3))

        z1, arrived = across(p1, tensor), across(vectors, tensor)
        vectors = jnp.stack([vectors] + arrived)
        a1, b1 = halves(z1, n1)
        a1, b1, p2, context, vectors = stage(a1, b1, p2, context, vectors)
        qkv_bias, inner_bias = vectors[..., : 3 * cols], vectors[..., 3 * cols :]

        ax, by, z2 = flip(a1, 2), flip(b1, 4), across(p2, tensor)
        a1, b1, ab1 = join(a1, ax, b1, by)
        a2, b2 = halves(z2, n2)
        a1, b1, ab1, a2, b2, context, x, order = stage(a1, b1, ab1, a2, b2, context, x, order)

        c1 = flip(ab1, 1)
        context, c1 = stage(context, c1)
        context = lax.all_to_all(context, "tensor", 0, 0, tiled=True)
        ay1, bx1, ax, by = flip(a1, 4), flip(b1, 2), flip(a2, 2), flip(b2, 4)
        a2, b2, ab2 = join(a2, ax, b2, by)
        d1 = other_core(ay1, bx1)
        ay1, bx1, a2, b2, ab2, p3 = stage(ay1, bx1, a2, b2, ab2, p3)

        c2, ay2, bx2 = flip(ab2, 1), flip(a2, 4), flip(b2, 2)
        pieces = pieces_of([w_inner, w_output], a1, b1, ay1, bx1, c1, d1)
        context, hidden, hidden_bf, normed, inverse, output_full = rest_of_attention(context, Stream(w_output, 1, pieces))
        active, slope, inner_full = inner_forward(hidden_bf, Stream(w_inner, 0, pieces), inner_bias)
        c2, ay2, bx2, p3, active = stage(c2, ay2, bx2, p3, active)

        d2, z3 = other_core(ay2, bx2), across(p3, tensor)
        pieces = pieces_of([w_outer], a2, b2, ay2, bx2, c2, d2)
        layer_out, normed_two, inverse_two, outer_full = outer_forward(
            active, Stream(w_outer, 0, pieces), hidden, wide_vectors
        )
        *z3, layer_out, normed_two = stage(*z3, layer_out, normed_two)

        layer_out = lax.all_gather(layer_out, "tensor", axis=0, tiled=True)
        a3, b3 = halves(z3, n3)
        ax, by = flip(a3, 2), flip(b3, 4)
        grad_resid2, grad_outer, sums_two = last_norm_backward(cot, normed_two, inverse_two, wide_vectors)
        part1 = grad_full((grad_outer, active))
        a3, b3, ab3 = join(a3, ax, b3, by)
        a3, b3, ab3, part1, grad_outer = stage(a3, b3, ab3, part1, grad_outer)

        part1 = lax.psum_scatter(part1, "dp", scatter_dimension=0, tiled=True)
        ay3, bx3, c3 = flip(a3, 4), flip(b3, 2), flip(ab3, 1)
        grad_inner, grad_resid1, grad_attn, inner_sums, sums_one = inner_backward(
            grad_outer, outer_full, slope, inner_full, grad_resid2, normed, inverse, wide_vectors
        )
        ay3, bx3, grad_inner, grad_attn = stage(ay3, bx3, grad_inner, grad_attn)

        d3 = other_core(ay3, bx3)
        send, keep = grad_rows(order, [(hidden_bf, grad_inner)])
        *d3, send, grad_attn = stage(*d3, send, grad_attn)

        got = flip(send, 1)
        qkv_full = assemble(Stream(qkv_local, 0, pieces_of([qkv_local], a3, b3, ay3, bx3, c3, d3)))
        (a, ak), (b, bk) = split_paths(keep + got, share)
        a, b, qkv_full, grad_attn = stage(a, b, qkv_full, grad_attn)

        ax, by = flip(a, 2), flip(b, 4)
        part3, grad_x, qkv_sums = attend_backward(
            x, grad_attn, grad_resid1, qkv_full, output_full, qkv_bias, context
        )
        a, b = ak + ax, bk + by
        a_send, b_send = stage(a[:share], b[:share])

        part3 = lax.psum_scatter(part3, "dp", scatter_dimension=0, tiled=True)
        g1 = onward((grad_x, grad_x), tensor, 1)
        ay, bx = flip(a_send, 4), flip(b_send, 2)
        part2 = jnp.concatenate([a[share:] + ay, b[share:] + bx], axis=1)
        extra = small_sums(qkv_sums, inner_sums, sums_one, sums_two)
        extra = jnp.pad(extra, (0, -extra.shape[0] % (8 * width))).reshape(-1, width)
        extra = extra + flip(extra, 1)
        layer_out = narrow(layer_out, own_rows)
        first = columns(wide(part1, part2), tensor)
        g2 = onward(g1, tensor, 2)
        _, _, extra, first[0], first[1], first[2], first[3], layer_out = stage(*g1, extra, *first, layer_out)

        u, d = up(first[1], tensor, 1), down(first[3], tensor, 1)
        extra = extra + flip(extra, 2)
        g3 = onward(g2, tensor, 3)
        _, _, u, d, part3, extra = stage(*g2, first[2] + u, first[2] + d, part3, extra)

        u, d = up(u, tensor, 2), down(d, tensor, 2)
        last = columns(part3, tensor)
        v, w = up(last[1], tensor, 1), down(last[3], tensor, 1)
        extra = extra + flip(extra, 4)
        _, _, u, d, v, w, extra = stage(*g3, first[3] + u, first[1] + d, last[2] + v, last[2] + w, extra)

        u, d, v, w = up(u, tensor, 3), down(d, tensor, 3), up(v, tensor, 2), down(w, tensor, 2)
        extra = extra + swap(extra, tensor, 1)
        grad_inputs = place(grad_x, [g1[0], g2[0], g3[0]], [g1[1], g2[1], g3[1]])
        gu = first[0] + u + d
        v, w, extra, gu, grad_inputs = stage(last[3] + v, last[1] + w, extra, gu, grad_inputs)

        gqkv = last[0] + up(v, tensor, 3) + down(w, tensor, 3)
        extra = extra + swap(extra, tensor, 2)
        gu, gi = gu[:share], gu[share:]
        gqkv, go = gqkv[:, : 3 * cols], gqkv[:, 3 * cols :]
        sums = extra.reshape(-1)

    span = 3 * cols + w_inner.shape[1]
    mine = lax.dynamic_slice_in_dim(sums, z * span, span, 0)
    rest = sums[span * tensor :][: 6 * width].reshape(6, width)
    return (
        layer_out,
        grad_inputs,
        gqkv[:, :cols],
        mine[:cols],
        gqkv[:, cols : 2 * cols],
        gqkv[:, 2 * cols :],
        mine[2 * cols : 3 * cols],
        go.T,
        rest[2],
        rest[0],
        rest[1],
        gi,
        mine[3 * cols :],
        gu.T,
        rest[5],
        rest[3],
        rest[4],
    )


def solution(mesh):
    wide, tall, vector = P(None, "tensor"), P("tensor", None), P("tensor")
    tokens, both = P("dp", None), P("dp", "tensor")
    in_specs = (
        tokens, wide, vector, wide, wide, vector, tall, P(), P(), P(), wide, vector, tall, P(), P(), P(), tokens,
    )
    out_specs = (
        tokens, tokens, both, vector, both, both, vector, P("tensor", "dp"), P(), P(), P(), both, vector,
        P("tensor", "dp"), P(), P(), P(),
    )
    body = partial(shards, mesh.shape["dp"], mesh.shape["tensor"])
    return jax.shard_map(body, mesh=mesh, in_specs=in_specs, out_specs=out_specs, check_vma=False)
```

```python
import math
from functools import partial
from typing import NamedTuple

import jax
import jax.numpy as jnp
from jax import lax
from jax.experimental import pallas as pl
from jax.experimental.pallas import tpu as pltpu
from jax.sharding import PartitionSpec as P

HEAD_DIM = 64
LENGTH = 512
EPSILON = 1e-12
F32 = jnp.float32
BF16 = jnp.bfloat16
SCALE = HEAD_DIM ** (-0.5)
EXP_SCALE = SCALE * 1.4426950408889634
ROWS = ((0,), (0,))
PLAIN = ((1,), (0,))
COLS = ((1,), (1,))


def dot(left, right, dims):
    return lax.dot_general(left, right, (dims, ((), ())), preferred_element_type=F32)


def norm_forward(values, gain, shift):
    center = values - jnp.mean(values, axis=-1, keepdims=True)
    inverse = lax.rsqrt(jnp.mean(center * center, axis=-1, keepdims=True) + EPSILON)
    normed = center * inverse
    return (normed * gain + shift, normed, inverse)


def norm_backward(upstream, gain, normed, inverse):
    scaled = upstream * gain
    first_mean = jnp.mean(scaled, axis=-1, keepdims=True)
    cross_mean = jnp.mean(scaled * normed, axis=-1, keepdims=True)
    return inverse * (scaled - first_mean - normed * cross_mean)


def by_rows(rows, step, body, carry=()):
    return lax.fori_loop(0, rows // step, lambda i, c: body(pl.ds(pl.multiple_of(i * step, step), step), c), carry)


def row_sums(values):
    return jnp.sum(values, axis=0, keepdims=True)


def size_of(shape, dtype):
    return math.prod(shape) * jnp.dtype(dtype).itemsize


def call(kernel, name, grid, ins, outs, flops, exps=0, scratch=(), prefetch=None, moved=None):
    if moved is None:
        moved = sum(size_of(a.shape, a.dtype) for a, _, _ in ins) + sum(size_of(s, t) for s, t, _, _ in outs)
    lead = () if prefetch is None else (prefetch,)
    return pl.pallas_call(
        kernel,
        grid_spec=pltpu.PrefetchScalarGridSpec(
            num_scalar_prefetch=len(lead),
            grid=grid,
            in_specs=[pl.BlockSpec(memory_space=m) if b is None else pl.BlockSpec(b, m) for _, b, m in ins],
            out_specs=[pl.BlockSpec(b, m) for _, _, b, m in outs],
            scratch_shapes=list(scratch),
        ),
        out_shape=[jax.ShapeDtypeStruct(s, t) for s, t, _, _ in outs],
        cost_estimate=pl.CostEstimate(flops=flops, bytes_accessed=moved, transcendentals=exps),
        compiler_params=pltpu.CompilerParams(vmem_limit_bytes=56 << 20),
        name=name,
    )(*lead, *(a for a, _, _ in ins))


class Stream(NamedTuple):
    local: jax.Array
    target: int
    pieces: list


def plan_of(locals_, pieces, wanted):
    plan, where = [], []
    for _, parts in pieces:
        plan.append([])
        for entry, sender, base, spans in parts:
            for row, rows, target, offset in spans:
                if target in wanted:
                    plan[-1].append((entry, base + row, rows, wanted.index(target)))
                    where.append(sender * (locals_[wanted.index(target)].shape[0] // 8) + offset)
    return plan, jnp.stack(where)


def piece_copies(plan, where_ref, pieces, holds, sems):
    found = []
    for piece, spans in zip(pieces, plan):
        for i, source, rows, target in spans:
            start = pl.multiple_of(where_ref[len(found)], 8)
            found.append(
                pltpu.make_async_copy(
                    piece.at[i, :, pl.ds(source, rows)], holds[target].at[:, pl.ds(start, rows)], sems.at[len(found)]
                )
            )
    return found


def call_with(body, name, grid, slot_of, weights, ins, outs, flops, exps=0, prefetch=None):
    axes = len(grid)
    at = lambda *ids: (slot_of(*ids[:axes]), 0, 0)
    if not isinstance(weights, Stream):
        ins = [(weights, (None,) + weights.shape[1:], at)] + ins
        if prefetch is not None:
            return *call(lambda _, *refs: body(*refs), name, grid, ins, outs, flops, exps, prefetch=prefetch), weights
        return *call(body, name, grid, ins, outs, flops, exps), weights
    local, target, pieces = weights
    others = pieces[0][0].shape[1]
    plan, where = plan_of([local], pieces, [target])
    used = [n for n, spans in enumerate(plan) if spans]
    plan, arrays = [plan[n] for n in used], [pieces[n][0] for n in used]
    lead, count, inner = int(prefetch is not None), len(arrays), len(ins)

    def kernel(*refs):
        refs = refs[lead:]
        where_ref, local_ref, refs = refs[0], refs[1], refs[2:]
        piece_refs, refs = refs[:count], refs[count:]
        full_ref, hold, sems = refs[-3:]
        ids = [pl.program_id(n) for n in range(axes)]
        slot = slot_of(*ids)
        first = sum(ids) == slot
        moves = piece_copies(plan, where_ref, piece_refs, [hold], sems)

        @pl.when(jnp.logical_and(first, slot == 0))
        def _():
            for move in moves:
                move.start()
            full_ref[...] = local_ref[...]

        @pl.when(jnp.logical_and(first, slot == 1))
        def _():
            for move in moves:
                move.wait()

        @pl.when(jnp.logical_and(first, slot > 0))
        def _():
            full_ref[...] = hold[jnp.maximum(slot - 1, 0)].astype(BF16)

        body(full_ref, *refs[:-3])

    rows, width = local.shape
    flat = lambda *ids: (0, 0)
    more = [(where, None, pltpu.SMEM), (local, local.shape, flat)] + [(a, None, pl.ANY) for a in arrays]
    full = ((others + 1, rows, width), BF16, (None, rows, width), at)
    scratch = [pltpu.VMEM((others, rows, width), F32), pltpu.SemaphoreType.DMA((where.shape[0],))]
    return call(kernel, name, grid, more + ins, outs + [full], flops, exps, scratch, prefetch)


def attend_kernel(x_ref, w_ref, bias_ref, ctx_ref):
    cols = w_ref.shape[0] // 3
    parts = []
    qkv = (dot(x_ref[...], w_ref[...], COLS) + bias_ref[...]).astype(BF16)
    for h in range(cols // HEAD_DIM):
        q, k, v = (qkv[:, i * cols + h * HEAD_DIM : i * cols + (h + 1) * HEAD_DIM] for i in range(3))
        scores = dot(q, k, COLS)
        largest = jnp.max(scores, axis=-1, keepdims=True)
        expon = jnp.exp2((scores - largest) * EXP_SCALE)
        totals = jnp.sum(expon, axis=-1, keepdims=True)
        parts.append((dot(expon.astype(BF16), v, PLAIN) / totals).astype(BF16).astype(F32))
    context = jnp.concatenate(parts, axis=1)
    step = ctx_ref.shape[0]
    folds = [context[i * step : (i + 1) * step] for i in range(LENGTH // step)]
    ctx_ref[...] = jnp.concatenate(folds, axis=1)


def fold_of(cols):
    return 1 if cols % 128 == 0 else 2


def attend_forward(inputs, weights, bias):
    rows, width = inputs.shape
    cols = weights.shape[0] // 3
    fold = fold_of(cols)
    flat = lambda i: (0, 0)
    return call(
        attend_kernel,
        "attend_forward",
        (rows // LENGTH,),
        [
            (inputs, (LENGTH, width), lambda i: (i, 0)),
            (weights, weights.shape, flat),
            (bias, bias.shape, flat),
        ],
        [((rows // fold, fold * cols), F32, (LENGTH // fold, fold * cols), lambda i: (i, 0))],
        flops=rows * cols * (6 * width + 4 * LENGTH),
        exps=rows * LENGTH * (cols // HEAD_DIM),
    )[0]


def output_kernel(w_ref, x_ref, ctx_ref, vec_ref, low_ref, hid_ref, hbf_ref, nrm_ref, inv_ref):
    slot = pl.program_id(1)
    cols = low_ref.shape[-1]
    folds = [ctx_ref[:, i : i + cols] for i in range(0, ctx_ref.shape[-1], cols)]
    context = jnp.concatenate(folds, axis=0).astype(BF16)
    low_ref[...] = context
    attn = dot(context, w_ref[...], PLAIN)

    @pl.when(slot == 0)
    def _():
        hid_ref[...] = attn

    @pl.when(slot > 0)
    def _():
        hid_ref[...] += attn

    @pl.when(slot == pl.num_programs(1) - 1)
    def _():
        bias, gain, shift = vec_ref[0:1], vec_ref[1:2], vec_ref[2:3]

        def block(at, carry):
            values = x_ref[at].astype(F32) + hid_ref[at] + bias
            hidden, normed, inverse = norm_forward(values, gain, shift)
            hid_ref[at] = hidden
            hbf_ref[at] = hidden.astype(BF16)
            nrm_ref[at] = normed
            inv_ref[at] = inverse
            return carry

        by_rows(LENGTH, 256, block)


def output_forward(slots_at, x, context, weights, vectors):
    rows, width = x.shape
    slots = slots_at.shape[0]
    cols = width // slots
    mine = lambda i, j, at: (i, 0)
    flat = lambda i, j, at: (0, 0)
    token = (LENGTH, width)
    heads = (None, LENGTH, cols)
    return call_with(
        output_kernel,
        "output_forward",
        (rows // LENGTH, slots),
        lambda i, j: j,
        weights,
        [
            (x, token, mine),
            (context, (None, LENGTH // fold_of(cols), fold_of(cols) * cols), lambda i, j, at: (at[j], i, 0)),
            (vectors, vectors.shape, flat),
        ],
        [
            ((slots, rows, cols), BF16, heads, lambda i, j, at: (j, i, 0)),
            ((rows, width), F32, token, mine),
            ((rows, width), BF16, token, mine),
            ((rows, width), F32, token, mine),
            ((rows, 1), F32, (LENGTH, 1), mine),
        ],
        flops=2 * rows * width * width,
        prefetch=slots_at,
    )


def attend_back_kernel(x_ref, ga_ref, gr_ref, w_ref, wo_ref, bias_ref, ctx_ref, gw_ref, gx_ref, sum_ref, gqkv_ref):
    slot = pl.program_id(1)
    cols = wo_ref.shape[0]
    gctx = dot(ga_ref[...], wo_ref[...], COLS).astype(BF16)
    qkv = (dot(x_ref[...], w_ref[...], COLS) + bias_ref[...]).astype(BF16)
    for h in range(cols // HEAD_DIM):
        at = [slice(i * cols + h * HEAD_DIM, i * cols + (h + 1) * HEAD_DIM) for i in range(3)]
        q, k, v = (qkv[:, s] for s in at)
        g = gctx[:, at[0]]
        scores = dot(k, q, COLS)
        largest = jnp.max(scores, axis=0, keepdims=True)
        expon = jnp.exp2((scores - largest) * EXP_SCALE)
        probs = expon * (1.0 / row_sums(expon))
        gqkv_ref[:, at[2]] = dot(probs.astype(BF16), g, PLAIN).astype(BF16)
        weighted = probs * dot(v, g, COLS)
        grad_scores = (weighted - probs * row_sums(weighted)).astype(BF16)
        gqkv_ref[:, at[0]] = (dot(grad_scores, k, ROWS) * SCALE).astype(BF16)
        gqkv_ref[:, at[1]] = (dot(grad_scores, q, PLAIN) * SCALE).astype(BF16)
    grads = gqkv_ref[...]
    sum_ref[...] = row_sums(grads.astype(F32))
    back = dot(grads, w_ref[...], PLAIN)
    gw_ref[:, : 3 * cols] = dot(x_ref[...], grads, ROWS)
    gw_ref[:, 3 * cols :] = dot(ga_ref[...], ctx_ref[...], ROWS)

    @pl.when(slot == 0)
    def _():
        gx_ref[...] = gr_ref[...] + back

    @pl.when(slot > 0)
    def _():
        gx_ref[...] += back


def attend_backward(x, grad_attn, grad_resid, weights, w_output, bias, context):
    rows, width = grad_attn.shape
    slots, cols, _ = w_output.shape
    mine = lambda i, j: (i, 0)
    token = (LENGTH, width)
    weight = lambda i, j: (j, 0, 0)
    return call(
        attend_back_kernel,
        "attend_backward",
        (rows // LENGTH, slots),
        [
            (x, token, mine),
            (grad_attn, token, mine),
            (grad_resid, token, mine),
            (weights, (None, 3 * cols, width), weight),
            (w_output, (None, cols, width), weight),
            (bias, (None, 1, 3 * cols), weight),
            (context, (None, LENGTH, cols), lambda i, j: (j, i, 0)),
        ],
        [
            ((width, slots * 4 * cols), F32, (width, 4 * cols), lambda i, j: (0, j)),
            ((rows, width), F32, token, mine),
            ((rows // LENGTH, slots, 1, 3 * cols), F32, (None, None, 1, 3 * cols), lambda i, j: (i, j, 0, 0)),
        ],
        flops=0,
        moved=0,
        scratch=[pltpu.VMEM((LENGTH, 3 * cols), BF16)],
    )


def inner_kernel(w_ref, h_ref, b_ref, act_ref, slope_ref):
    inner = dot(h_ref[...], w_ref[...], PLAIN) + b_ref[...]
    phi = 0.5 + 0.5 * lax.erf(inner * (0.5**0.5))
    bell = jnp.exp2(inner * inner * (-0.5 * 1.4426950408889634)) * 0.3989422804014327
    act_ref[...] = (inner * phi).astype(BF16)
    slope_ref[...] = phi + inner * bell


def inner_forward(hidden, weights, bias):
    rows, width = hidden.shape
    slots, _, units = bias.shape
    slot = lambda i, j: (i, j, 0)
    block = LENGTH // 2
    return call_with(
        inner_kernel,
        "inner_forward",
        (slots, rows // block),
        lambda i, j: i,
        weights,
        [
            (hidden, (block, width), lambda i, j: (j, 0)),
            (bias, (None, 1, units), lambda i, j: (i, 0, 0)),
        ],
        [
            ((slots, rows, units), BF16, (None, block, units), slot),
            ((slots, rows, units), F32, (None, block, units), slot),
        ],
        flops=2 * rows * width * slots * units,
        exps=2 * rows * slots * units,
    )


def outer_kernel(w_ref, act_ref, hid_ref, vec_ref, out_ref, nrm_ref, inv_ref):
    slot = pl.program_id(1)
    outer = dot(act_ref[...], w_ref[...], PLAIN)

    @pl.when(slot == 0)
    def _():
        out_ref[...] = outer

    @pl.when(slot > 0)
    def _():
        out_ref[...] += outer

    @pl.when(slot == pl.num_programs(1) - 1)
    def _():
        bias, gain, shift = vec_ref[3:4], vec_ref[4:5], vec_ref[5:6]

        def block(at, carry):
            values = hid_ref[at] + (out_ref[at] + bias)
            layer_out, normed, inverse = norm_forward(values, gain, shift)
            out_ref[at] = layer_out
            nrm_ref[at] = normed
            inv_ref[at] = inverse
            return carry

        by_rows(LENGTH, 256, block)


def outer_forward(active, weights, hidden, vectors):
    rows, width = hidden.shape
    slots, _, units = active.shape
    mine = lambda i, j: (i, 0)
    token = (LENGTH, width)
    return call_with(
        outer_kernel,
        "outer_forward",
        (rows // LENGTH, slots),
        lambda i, j: j,
        weights,
        [
            (active, (None, LENGTH, units), lambda i, j: (j, i, 0)),
            (hidden, token, mine),
            (vectors, vectors.shape, lambda i, j: (0, 0)),
        ],
        [
            ((rows, width), F32, token, mine),
            ((rows, width), F32, token, mine),
            ((rows, 1), F32, (LENGTH, 1), mine),
        ],
        flops=2 * rows * width * slots * units,
    )


def last_norm_kernel(cot_ref, nrm_ref, inv_ref, vec_ref, gr_ref, go_ref, sum_ref):
    upstream, normed = cot_ref[...].astype(F32), nrm_ref[...]
    grad = norm_backward(upstream, vec_ref[4:5], normed, inv_ref[...])
    rounded = grad.astype(BF16)
    gr_ref[...] = grad
    go_ref[...] = rounded
    found = (upstream * normed, upstream, rounded.astype(F32))

    @pl.when(pl.program_id(0) == 0)
    def _():
        sum_ref[...] = jnp.zeros_like(sum_ref)

    for i, value in enumerate(found):
        sum_ref[i : i + 1] += row_sums(value)


def last_norm_backward(cotangent, normed, inverse, vectors):
    rows, width = normed.shape
    block = 128
    mine = lambda i: (i, 0)
    flat = lambda i: (0, 0)
    token = (block, width)
    return call(
        last_norm_kernel,
        "last_norm_backward",
        (rows // block,),
        [
            (cotangent, token, mine),
            (normed, token, mine),
            (inverse, (block, 1), mine),
            (vectors, vectors.shape, flat),
        ],
        [
            ((rows, width), F32, token, mine),
            ((rows, width), BF16, token, mine),
            ((8, width), F32, (8, width), flat),
        ],
        flops=0,
        moved=0,
    )


def inner_back_kernel(go_ref, wu_ref, slope_ref, wi_ref, gr_ref, nrm_ref, inv_ref, vec_ref,
                      gi_ref, g1_ref, ga_ref, bsum_ref, sum_ref):
    slot = pl.program_id(1)
    grad_inner = (dot(go_ref[...], wu_ref[...], COLS) * slope_ref[...]).astype(BF16)
    gi_ref[...] = grad_inner
    bsum_ref[...] = row_sums(grad_inner.astype(F32))
    back = dot(grad_inner, wi_ref[...], COLS)

    @pl.when(slot == 0)
    def _():
        g1_ref[...] = gr_ref[...] + back

    @pl.when(slot > 0)
    def _():
        g1_ref[...] += back

    @pl.when(slot == pl.num_programs(1) - 1)
    def _():
        gain = vec_ref[1:2]

        def block(at, sums):
            upstream, normed = g1_ref[at], nrm_ref[at]
            grad = norm_backward(upstream, gain, normed, inv_ref[at])
            rounded = grad.astype(BF16)
            g1_ref[at] = grad
            ga_ref[at] = rounded
            found = (upstream * normed, upstream, rounded.astype(F32))
            return tuple(s + row_sums(f) for s, f in zip(sums, found))

        for i, total in enumerate(by_rows(LENGTH, 256, block, (jnp.zeros_like(gain),) * 3)):
            sum_ref[i : i + 1] = total


def inner_backward(grad_outer, w_outer, slope, w_inner, grad_resid2, normed, inverse, vectors):
    rows, width = grad_outer.shape
    slots, units, _ = w_outer.shape
    mine = lambda i, j: (i, 0)
    token = (LENGTH, width)
    slot = lambda i, j: (j, i, 0)
    weight = lambda i, j: (j, 0, 0)
    return call(
        inner_back_kernel,
        "inner_backward",
        (rows // LENGTH, slots),
        [
            (grad_outer, token, mine),
            (w_outer, (None, units, width), weight),
            (slope, (None, LENGTH, units), slot),
            (w_inner, (None, width, units), weight),
            (grad_resid2, token, mine),
            (normed, token, mine),
            (inverse, (LENGTH, 1), mine),
            (vectors, vectors.shape, lambda i, j: (0, 0)),
        ],
        [
            ((slots, rows, units), BF16, (None, LENGTH, units), slot),
            ((rows, width), F32, token, mine),
            ((rows, width), BF16, token, mine),
            ((rows // LENGTH, slots, 1, units), F32, (None, None, 1, units), lambda i, j: (i, j, 0, 0)),
            ((rows // LENGTH, 8, width), F32, (None, 8, width), lambda i, j: (i, 0, 0)),
        ],
        flops=0,
        moved=0,
    )


def narrow_kernel(x_ref, out_ref):
    out_ref[...] = x_ref[...].astype(BF16)


def narrow(values, block_rows):
    rows, width = values.shape
    at = lambda i: (i, 0)
    block = (block_rows, width)
    out = ((rows, width), BF16, block, at)
    return call(narrow_kernel, "narrow", (rows // block_rows,), [(values, block, at)], [out], 0)[0]


def shift_to(values, tensor, k):
    return lax.ppermute(values, "tensor", [(i, (i + k) % tensor) for i in range(tensor)])


def flip(values, bit):
    return lax.ppermute(values, "dp", [(i, i ^ bit) for i in range(8)])


def stage(*values):
    return lax.optimization_barrier(values)


def slots_kernel(slot_ref, local_ref, x_ref, out_ref):
    del slot_ref
    first = pl.program_id(0) == 0

    @pl.when(first)
    def _():
        out_ref[...] = local_ref[...]

    @pl.when(jnp.logical_not(first))
    def _():
        out_ref[...] = x_ref[...].reshape(out_ref.shape).astype(BF16)


def gather_plain(local, dp, tensor):
    rows, width = local.shape
    share = rows // dp
    piece = lax.dynamic_slice_in_dim(local, lax.axis_index("dp") * share, share, 0).astype(F32)
    full = lax.all_gather(piece, ("dp", "tensor"), axis=0).reshape(dp, tensor, share, width)
    order = (lax.axis_index("tensor") - jnp.arange(tensor, dtype=jnp.int32)) % tensor
    if share % 8:
        full = full.swapaxes(0, 1).reshape(1, tensor, rows, width)
    lead, _, part, _ = full.shape
    return pl.pallas_call(
        slots_kernel,
        grid_spec=pltpu.PrefetchScalarGridSpec(
            num_scalar_prefetch=1,
            grid=(tensor,),
            in_specs=[
                pl.BlockSpec((rows, width), lambda i, slot: (0, 0)),
                pl.BlockSpec((lead, None, part, width), lambda i, slot: (0, slot[i], 0, 0)),
            ],
            out_specs=pl.BlockSpec((None, rows, width), lambda i, slot: (i, 0, 0)),
        ),
        out_shape=jax.ShapeDtypeStruct((tensor, rows, width), BF16),
        cost_estimate=pl.CostEstimate(flops=0, bytes_accessed=6 * full.size, transcendentals=0),
        compiler_params=pltpu.CompilerParams(vmem_limit_bytes=48 << 20),
        name="slots",
    )(order, local, full)


def assemble_kernel(plan, where_ref, local_ref, *refs):
    *pieces, out_ref, hold, sems = refs
    moves = piece_copies(plan, where_ref, pieces, [hold], sems)
    for move in moves:
        move.start()
    out_ref[0] = local_ref[...]
    for move in moves:
        move.wait()
    for k in range(hold.shape[0]):

        def block(at, carry, k=k):
            out_ref[k + 1, at] = hold[k, at].astype(BF16)
            return carry

        by_rows(hold.shape[1], 96, block)


def assemble(stream):
    local, target, pieces = stream
    rows, width = local.shape
    others = pieces[0][0].shape[1]
    plan, where = plan_of([local], pieces, [target])
    space = pl.BlockSpec(memory_space=pltpu.VMEM)
    return pl.pallas_call(
        partial(assemble_kernel, plan),
        in_specs=[pl.BlockSpec(memory_space=pltpu.SMEM), space] + [pl.BlockSpec(memory_space=pl.ANY)] * len(pieces),
        out_specs=space,
        out_shape=jax.ShapeDtypeStruct((others + 1, rows, width), BF16),
        scratch_shapes=[pltpu.VMEM((others, rows, width), F32), pltpu.SemaphoreType.DMA((where.shape[0],))],
        cost_estimate=pl.CostEstimate(flops=0, bytes_accessed=others * rows * width * 6, transcendentals=0),
        compiler_params=pltpu.CompilerParams(vmem_limit_bytes=48 << 20),
        name="assemble",
    )(where, local, *(array for array, _ in pieces))


def shares(weights, dp=8):
    me = lax.axis_index("dp")
    cut = [lax.dynamic_slice_in_dim(w, me * (w.shape[0] // dp), w.shape[0] // dp, 0) for w in weights]
    return jnp.concatenate(cut, axis=0).astype(F32)


def across(values, tensor):
    return [shift_to(values, tensor, k) for k in range(1, tensor)]


def wide(v, w):
    return jnp.concatenate([v, w], axis=0)


def other_core(*values):
    return tuple(flip(v, 1) for v in values)


def copy_kernel(plan, count, *refs):
    ins, outs = refs[:count], refs[count:]
    for source, source_at, target, target_at in plan:
        outs[target][target_at] = ins[source][source_at]


def copies(ins, shapes, plan):
    space = pl.BlockSpec(memory_space=pltpu.VMEM)
    return pl.pallas_call(
        partial(copy_kernel, plan, len(ins)),
        in_specs=[space] * len(ins),
        out_specs=[space] * len(shapes),
        out_shape=[jax.ShapeDtypeStruct(shape, F32) for shape in shapes],
        cost_estimate=pl.CostEstimate(flops=0, bytes_accessed=0, transcendentals=0),
        compiler_params=pltpu.CompilerParams(vmem_limit_bytes=32 << 20),
        name="copies",
    )(*ins)


def halves(arrived, upper):
    rows, width = arrived[0].shape
    n = len(arrived)
    plan = [(k, (slice(0, upper),), 0, (0, k)) for k in range(n)]
    plan += [(k, (slice(upper, rows),), 1, (0, k)) for k in range(n)]
    return copies(arrived, [(1, n, upper, width), (1, n, rows - upper, width)], plan)


def join(a, ax, b, by):
    _, n, upper, width = a.shape
    lower = b.shape[2]
    plan = []
    for i, (v, w) in enumerate(((a, b), (ax, by))):
        every = slice(None)
        plan += [(2 * i, (0,), 0, (i,)), (2 * i + 1, (0,), 1, (i,))]
        plan += [(2 * i, (0,), 2, (i, every, slice(0, upper))), (2 * i + 1, (0,), 2, (i, every, slice(upper, upper + lower)))]
    shapes = [(2, n, upper, width), (2, n, lower, width), (2, n, upper + lower, width)]
    return copies([a, b, ax, by], shapes, plan)


def pieces_of(locals_, a, b, ay, bx, c, d):
    me = lax.axis_index("dp")
    cut_at, end = a.shape[2], a.shape[2] + b.shape[2]
    ends = [0]
    for w in locals_:
        ends.append(ends[-1] + w.shape[0] // 8)

    def spans(first, last):
        found = []
        for target in range(len(locals_)):
            low, high = max(first, ends[target]), min(last, ends[target + 1])
            if low < high:
                found.append((low - first, high - low, target, low - ends[target]))
        return found

    upper = lambda rels: [(i, me ^ r, 0, spans(0, cut_at)) for i, r in enumerate(rels)]
    lower = lambda rels, base=0: [(i, me ^ r, base, spans(cut_at, end)) for i, r in enumerate(rels)]
    return [
        (a, upper((0, 2))),
        (b, lower((0, 4))),
        (ay, upper((4, 6))),
        (bx, lower((2, 6))),
        (c, upper((1, 3)) + lower((1, 5), cut_at)),
        (d[0], upper((5, 7))),
        (d[1], lower((3, 7))),
    ]


def block_order(width):
    me = lax.axis_index("dp")
    share = width // 8
    rel = jnp.array([7, 5, 3, 1, 6, 4, 2, 0])
    source = (me ^ rel[jnp.arange(width) // share]) * share + jnp.arange(width) % share
    return (lax.broadcasted_iota(jnp.int32, (width, width), 0) == source[None, :]).astype(BF16)


def grad_kernel(count, *refs):
    order_ref, refs = refs[0], refs[1:]
    lefts, rights, (send_ref, keep_ref), holds = (
        refs[:count], refs[count : 2 * count], refs[2 * count : 2 * count + 2], refs[2 * count + 2 :],
    )

    @pl.when(pl.program_id(0) == 0)
    def _():
        for left, hold in zip(lefts, holds):
            hold[...] = dot(left[...], order_ref[...], PLAIN).astype(BF16)

    half = send_ref.shape[0]
    start = 0
    for hold, right in zip(holds, rights):
        span = slice(start, start + right.shape[-1])
        value = dot(hold[...], right[...], ROWS)
        send_ref[:, span] = value[:half]
        keep_ref[:, span] = value[half:]
        start = span.stop


def grad_rows(order, pairs):
    rows, width = pairs[0][0].shape
    slots = pairs[0][1].shape[0]
    cols = sum(r.shape[-1] for _, r in pairs)
    flat = lambda j: (0, 0)
    ins = [(order, order.shape, flat)]
    ins += [(left, left.shape, flat) for left, _ in pairs]
    ins += [(right, (None,) + right.shape[1:], lambda j: (j, 0, 0)) for _, right in pairs]
    out = ((width // 2, slots * cols), F32, (width // 2, cols), lambda j: (0, j))
    scratch = [pltpu.VMEM((rows, width), BF16)] * len(pairs)
    return call(
        partial(grad_kernel, len(pairs)), "grad_rows", (slots,), ins, [out, out], 0, 0, scratch, moved=0
    )


def full_kernel(count, *refs):
    lefts, rights, out_ref = refs[:count], refs[count:-1], refs[-1]
    start = 0
    for left, right in zip(lefts, rights):
        span = slice(start, start + right.shape[-1])
        out_ref[:, span] = dot(left[...], right[...], ROWS)
        start = span.stop


def grad_full(*pairs):
    rows, width = pairs[0][0].shape
    slots = pairs[0][1].shape[0]
    cols = sum(r.shape[-1] for _, r in pairs)
    ins = [(left, left.shape, lambda j: (0, 0)) for left, _ in pairs]
    ins += [(right, (None,) + right.shape[1:], lambda j: (j, 0, 0)) for _, right in pairs]
    return call(
        partial(full_kernel, len(pairs)),
        "grad_full",
        (slots,),
        ins,
        [((width, slots * cols), F32, (width, cols), lambda j: (0, j))],
        flops=0,
        moved=0,
    )[0]


def split_paths(held, share):
    mid = held.shape[1] // 2
    pick = lambda i, cols: held[i * share : (i + 1) * share, cols]
    a, b = slice(None, mid), slice(mid, None)
    join = lambda i, j, cols: jnp.concatenate([pick(i, cols), pick(j, cols)], axis=0)
    return (join(0, 2, a), join(1, 3, a)), (join(0, 1, b), join(2, 3, b))


def scatter_plain(grad, tensor):
    part = lax.psum_scatter(grad, "dp", scatter_dimension=0, tiled=True)
    part = columns(part, tensor)
    return sum((shift_to(part[k], tensor, tensor - k) for k in range(1, tensor)), part[0])


def columns(part, tensor):
    cols = part.shape[1] // tensor
    return [part[:, k * cols : (k + 1) * cols] for k in range(tensor)]


def up(values, tensor, step):
    return lax.ppermute(values, "tensor", [(i, i + 1) for i in range(step)])


def down(values, tensor, step):
    return lax.ppermute(values, "tensor", [(i, i - 1) for i in range(tensor - step, tensor)])


def place_kernel(z_ref, own_ref, *refs):
    *others, out_ref = refs
    count = len(others) // 2
    below, above = others[:count], others[count:]
    away = pl.program_id(0) - z_ref[0]

    @pl.when(away == 0)
    def _():
        out_ref[...] = own_ref[...]

    for k in range(count):

        @pl.when(away == -(k + 1))
        def _(k=k):
            out_ref[...] = below[k][...]

        @pl.when(away == k + 1)
        def _(k=k):
            out_ref[...] = above[k][...]


def place(own, below, above):
    rows, width = own.shape
    count = len(below) + 1
    whole = (rows, width)
    return call(
        place_kernel,
        "place",
        (count,),
        [(v, whole, lambda i, z: (0, 0)) for v in (own, *below, *above)],
        [((count * rows, width), F32, whole, lambda i, z: (i, 0))],
        flops=0,
        moved=0,
        prefetch=lax.axis_index("tensor").astype(jnp.int32).reshape(1),
    )[0]


def onward(values, tensor, step):
    u, d = values
    u = lax.ppermute(u, "tensor", [(i, i + 1) for i in range(step - 1, tensor - 1)])
    d = lax.ppermute(d, "tensor", [(i, i - 1) for i in range(1, tensor - step + 1)])
    return u, d


def swap(values, tensor, bit):
    return lax.ppermute(values, "tensor", [(i, i ^ bit) for i in range(tensor)])


def shards(
    dp,
    tensor,
    inputs,
    w_query,
    b_query,
    w_key,
    w_value,
    b_value,
    w_output,
    b_output,
    gain_attn,
    shift_attn,
    w_inner,
    b_inner,
    w_outer,
    b_outer,
    gain_ffn,
    shift_ffn,
    cotangent,
):
    tok_rows, width = inputs.shape
    own_rows = tok_rows // tensor
    cols = w_query.shape[1]
    z = lax.axis_index("tensor")
    own = lambda a: lax.dynamic_slice_in_dim(a, z * own_rows, own_rows, 0)
    row = lambda a: a.astype(F32)[None, :]

    vectors = row(jnp.concatenate([b_query, jnp.zeros_like(b_query), b_value, b_inner]))
    qkv_local = jnp.concatenate([w_query.T, w_key.T, w_value.T], axis=0)
    x, cot = own(inputs), own(cotangent)
    rows_of = (b_output, gain_attn, shift_attn, b_outer, gain_ffn, shift_ffn, b_outer, b_outer)
    wide_vectors = jnp.stack(rows_of).astype(F32)
    slots_at = (z - jnp.arange(tensor, dtype=jnp.int32)) % tensor
    staged = (
        dp == 8 and tensor == 4 and own_rows == LENGTH and width % 128 == 0
        and w_inner.shape == w_outer.shape == (width, width) and cols % 64 == 0
    )

    def rest_of_attention(context, weights):
        return output_forward(slots_at, x, context, weights, wide_vectors)


    def small_sums(qkv_sums, inner_sums, sums_one, sums_two):
        by_slot = jnp.concatenate([jnp.sum(qkv_sums, axis=0), jnp.sum(inner_sums, axis=0)], axis=-1)
        by_place = by_slot[slots_at].reshape(-1)
        rest = jnp.concatenate([jnp.sum(sums_one, axis=0)[:3], sums_two[:3]]).reshape(-1)
        return jnp.concatenate([by_place, rest])

    local_bias = vectors[:, : 3 * cols]
    context = attend_forward(inputs, qkv_local, local_bias)
    context = context.reshape(tensor, -1, context.shape[1])
    if not staged:
        vectors = jnp.stack([vectors] + across(vectors, tensor))
        qkv_bias, inner_bias = vectors[..., : 3 * cols], vectors[..., 3 * cols :]
        inner_full, output_full, outer_full, qkv_full = (
            gather_plain(w, dp, tensor) for w in (w_inner, w_output, w_outer, qkv_local)
        )
        context = lax.all_to_all(context, "tensor", 0, 0, tiled=True)
        context, hidden, hidden_bf, normed, inverse, output_full = rest_of_attention(context, output_full)
        active, slope, inner_full = inner_forward(hidden_bf, inner_full, inner_bias)
        layer_out, normed_two, inverse_two, outer_full = outer_forward(active, outer_full, hidden, wide_vectors)
        grad_resid2, grad_outer, sums_two = last_norm_backward(cot, normed_two, inverse_two, wide_vectors)
        layer_out = narrow(lax.all_gather(layer_out, "tensor", axis=0, tiled=True), own_rows)
        grad_inner, grad_resid1, grad_attn, inner_sums, sums_one = inner_backward(
            grad_outer, outer_full, slope, inner_full, grad_resid2, normed, inverse, wide_vectors
        )
        part3, grad_x, qkv_sums = attend_backward(x, grad_attn, grad_resid1, qkv_full, output_full, qkv_bias, context)
        grad_inputs = lax.all_gather(grad_x, "tensor", axis=0, tiled=True)
        gu = scatter_plain(grad_full((grad_outer, active)), tensor)
        gi = scatter_plain(grad_full((hidden_bf, grad_inner)), tensor)
        gqkv = scatter_plain(part3, tensor)
        gqkv, go = gqkv[:, : 3 * cols], gqkv[:, 3 * cols :]
        sums = lax.psum(small_sums(qkv_sums, inner_sums, sums_one, sums_two), ("dp", "tensor"))
    else:
        order = block_order(width)
        share = width // 8
        p1, p2, p3 = shares([w_inner, w_output]), shares([w_outer]), shares([qkv_local])
        n1, n2, n3 = (-(-p.shape[0] // 16) * 8 for p in (p1, p2, p3))

        z1, arrived = across(p1, tensor), across(vectors, tensor)
        vectors = jnp.stack([vectors] + arrived)
        a1, b1 = halves(z1, n1)
        a1, b1, p2, context, vectors = stage(a1, b1, p2, context, vectors)
        qkv_bias, inner_bias = vectors[..., : 3 * cols], vectors[..., 3 * cols :]

        ax, by, z2 = flip(a1, 2), flip(b1, 4), across(p2, tensor)
        a1, b1, ab1 = join(a1, ax, b1, by)
        a2, b2 = halves(z2, n2)
        a1, b1, ab1, a2, b2, context, x, order = stage(a1, b1, ab1, a2, b2, context, x, order)

        c1 = flip(ab1, 1)
        context, c1 = stage(context, c1)
        context = lax.all_to_all(context, "tensor", 0, 0, tiled=True)
        ay1, bx1, ax, by = flip(a1, 4), flip(b1, 2), flip(a2, 2), flip(b2, 4)
        a2, b2, ab2 = join(a2, ax, b2, by)
        d1 = other_core(ay1, bx1)
        ay1, bx1, a2, b2, ab2, p3 = stage(ay1, bx1, a2, b2, ab2, p3)

        c2, ay2, bx2 = flip(ab2, 1), flip(a2, 4), flip(b2, 2)
        pieces = pieces_of([w_inner, w_output], a1, b1, ay1, bx1, c1, d1)
        context, hidden, hidden_bf, normed, inverse, output_full = rest_of_attention(context, Stream(w_output, 1, pieces))
        active, slope, inner_full = inner_forward(hidden_bf, Stream(w_inner, 0, pieces), inner_bias)
        c2, ay2, bx2, p3, active = stage(c2, ay2, bx2, p3, active)

        d2, z3 = other_core(ay2, bx2), across(p3, tensor)
        pieces = pieces_of([w_outer], a2, b2, ay2, bx2, c2, d2)
        layer_out, normed_two, inverse_two, outer_full = outer_forward(
            active, Stream(w_outer, 0, pieces), hidden, wide_vectors
        )
        *z3, layer_out, normed_two = stage(*z3, layer_out, normed_two)

        layer_out = lax.all_gather(layer_out, "tensor", axis=0, tiled=True)
        a3, b3 = halves(z3, n3)
        ax, by = flip(a3, 2), flip(b3, 4)
        grad_resid2, grad_outer, sums_two = last_norm_backward(cot, normed_two, inverse_two, wide_vectors)
        a3, b3, ab3 = join(a3, ax, b3, by)
        a3, b3, ab3, grad_outer = stage(a3, b3, ab3, grad_outer)

        ay3, bx3, c3 = flip(a3, 4), flip(b3, 2), flip(ab3, 1)
        part1 = grad_full((grad_outer, active))
        part1, grad_outer = stage(part1, grad_outer)
        part1 = lax.psum_scatter(part1, "dp", scatter_dimension=0, tiled=True)
        grad_inner, grad_resid1, grad_attn, inner_sums, sums_one = inner_backward(
            grad_outer, outer_full, slope, inner_full, grad_resid2, normed, inverse, wide_vectors
        )
        ay3, bx3, c3, grad_inner, grad_attn = stage(ay3, bx3, c3, grad_inner, grad_attn)

        d3 = other_core(ay3, bx3)
        send, keep = grad_rows(order, [(hidden_bf, grad_inner)])
        *d3, send, grad_attn = stage(*d3, send, grad_attn)

        got = flip(send, 1)
        qkv_full = assemble(Stream(qkv_local, 0, pieces_of([qkv_local], a3, b3, ay3, bx3, c3, d3)))
        (a, ak), (b, bk) = split_paths(keep + got, share)
        a, b, qkv_full, grad_attn = stage(a, b, qkv_full, grad_attn)

        ax, by = flip(a, 2), flip(b, 4)
        part3, grad_x, qkv_sums = attend_backward(
            x, grad_attn, grad_resid1, qkv_full, output_full, qkv_bias, context
        )
        a, b = ak + ax, bk + by
        a_send, b_send = stage(a[:share], b[:share])

        part3 = lax.psum_scatter(part3, "dp", scatter_dimension=0, tiled=True)
        g1 = onward((grad_x, grad_x), tensor, 1)
        ay, bx = flip(a_send, 4), flip(b_send, 2)
        part2 = jnp.concatenate([a[share:] + ay, b[share:] + bx], axis=1)
        extra = small_sums(qkv_sums, inner_sums, sums_one, sums_two)
        extra = jnp.pad(extra, (0, -extra.shape[0] % (8 * width))).reshape(-1, width)
        extra = extra + flip(extra, 1)
        layer_out = narrow(layer_out, own_rows)
        first = columns(wide(part1, part2), tensor)
        g2 = onward(g1, tensor, 2)
        _, _, extra, first[0], first[1], first[2], first[3], layer_out = stage(*g1, extra, *first, layer_out)

        u, d = up(first[1], tensor, 1), down(first[3], tensor, 1)
        extra = extra + flip(extra, 2)
        g3 = onward(g2, tensor, 3)
        _, _, u, d, part3, extra = stage(*g2, first[2] + u, first[2] + d, part3, extra)

        u, d = up(u, tensor, 2), down(d, tensor, 2)
        last = columns(part3, tensor)
        v, w = up(last[1], tensor, 1), down(last[3], tensor, 1)
        extra = extra + flip(extra, 4)
        _, _, u, d, v, w, extra = stage(*g3, first[3] + u, first[1] + d, last[2] + v, last[2] + w, extra)

        u, d, v, w = up(u, tensor, 3), down(d, tensor, 3), up(v, tensor, 2), down(w, tensor, 2)
        extra = extra + swap(extra, tensor, 1)
        grad_inputs = place(grad_x, [g1[0], g2[0], g3[0]], [g1[1], g2[1], g3[1]])
        gu = first[0] + u + d
        v, w, extra, gu, grad_inputs = stage(last[3] + v, last[1] + w, extra, gu, grad_inputs)

        gqkv = last[0] + up(v, tensor, 3) + down(w, tensor, 3)
        extra = extra + swap(extra, tensor, 2)
        gu, gi = gu[:share], gu[share:]
        gqkv, go = gqkv[:, : 3 * cols], gqkv[:, 3 * cols :]
        sums = extra.reshape(-1)

    span = 3 * cols + w_inner.shape[1]
    mine = lax.dynamic_slice_in_dim(sums, z * span, span, 0)
    rest = sums[span * tensor :][: 6 * width].reshape(6, width)
    return (
        layer_out,
        grad_inputs,
        gqkv[:, :cols],
        mine[:cols],
        gqkv[:, cols : 2 * cols],
        gqkv[:, 2 * cols :],
        mine[2 * cols : 3 * cols],
        go.T,
        rest[2],
        rest[0],
        rest[1],
        gi,
        mine[3 * cols :],
        gu.T,
        rest[5],
        rest[3],
        rest[4],
    )


def solution(mesh):
    wide, tall, vector = P(None, "tensor"), P("tensor", None), P("tensor")
    tokens, both = P("dp", None), P("dp", "tensor")
    in_specs = (
        tokens, wide, vector, wide, wide, vector, tall, P(), P(), P(), wide, vector, tall, P(), P(), P(), tokens,
    )
    out_specs = (
        tokens, tokens, both, vector, both, both, vector, P("tensor", "dp"), P(), P(), P(), both, vector,
        P("tensor", "dp"), P(), P(), P(),
    )
    body = partial(shards, mesh.shape["dp"], mesh.shape["tensor"])
    return jax.shard_map(body, mesh=mesh, in_specs=in_specs, out_specs=out_specs, check_vma=False)
```

```python
import math
from functools import partial
from typing import NamedTuple

import jax
import jax.numpy as jnp
from jax import lax
from jax.experimental import pallas as pl
from jax.experimental.pallas import tpu as pltpu
from jax.sharding import PartitionSpec as P

HEAD_DIM = 64
LENGTH = 512
EPSILON = 1e-12
F32 = jnp.float32
BF16 = jnp.bfloat16
SCALE = HEAD_DIM ** (-0.5)
EXP_SCALE = SCALE * 1.4426950408889634
ROWS = ((0,), (0,))
PLAIN = ((1,), (0,))
COLS = ((1,), (1,))


def dot(left, right, dims):
    return lax.dot_general(left, right, (dims, ((), ())), preferred_element_type=F32)


def norm_forward(values, gain, shift):
    center = values - jnp.mean(values, axis=-1, keepdims=True)
    inverse = lax.rsqrt(jnp.mean(center * center, axis=-1, keepdims=True) + EPSILON)
    normed = center * inverse
    return (normed * gain + shift, normed, inverse)


def norm_backward(upstream, gain, normed, inverse):
    scaled = upstream * gain
    first_mean = jnp.mean(scaled, axis=-1, keepdims=True)
    cross_mean = jnp.mean(scaled * normed, axis=-1, keepdims=True)
    return inverse * (scaled - first_mean - normed * cross_mean)


def by_rows(rows, step, body, carry=()):
    return lax.fori_loop(0, rows // step, lambda i, c: body(pl.ds(pl.multiple_of(i * step, step), step), c), carry)


def row_sums(values):
    return jnp.sum(values, axis=0, keepdims=True)


def size_of(shape, dtype):
    return math.prod(shape) * jnp.dtype(dtype).itemsize


def call(kernel, name, grid, ins, outs, flops, exps=0, scratch=(), prefetch=None, moved=None):
    if moved is None:
        moved = sum(size_of(a.shape, a.dtype) for a, _, _ in ins) + sum(size_of(s, t) for s, t, _, _ in outs)
    lead = () if prefetch is None else (prefetch,)
    return pl.pallas_call(
        kernel,
        grid_spec=pltpu.PrefetchScalarGridSpec(
            num_scalar_prefetch=len(lead),
            grid=grid,
            in_specs=[pl.BlockSpec(memory_space=m) if b is None else pl.BlockSpec(b, m) for _, b, m in ins],
            out_specs=[pl.BlockSpec(b, m) for _, _, b, m in outs],
            scratch_shapes=list(scratch),
        ),
        out_shape=[jax.ShapeDtypeStruct(s, t) for s, t, _, _ in outs],
        cost_estimate=pl.CostEstimate(flops=flops, bytes_accessed=moved, transcendentals=exps),
        compiler_params=pltpu.CompilerParams(vmem_limit_bytes=56 << 20),
        name=name,
    )(*lead, *(a for a, _, _ in ins))


class Stream(NamedTuple):
    local: jax.Array
    target: int
    pieces: list


def plan_of(locals_, pieces, wanted):
    plan, where = [], []
    for _, parts in pieces:
        plan.append([])
        for entry, sender, base, spans in parts:
            for row, rows, target, offset in spans:
                if target in wanted:
                    plan[-1].append((entry, base + row, rows, wanted.index(target)))
                    where.append(sender * (locals_[wanted.index(target)].shape[0] // 8) + offset)
    return plan, jnp.stack(where)


def piece_copies(plan, where_ref, pieces, holds, sems):
    found = []
    for piece, spans in zip(pieces, plan):
        for i, source, rows, target in spans:
            start = pl.multiple_of(where_ref[len(found)], 8)
            found.append(
                pltpu.make_async_copy(
                    piece.at[i, :, pl.ds(source, rows)], holds[target].at[:, pl.ds(start, rows)], sems.at[len(found)]
                )
            )
    return found


def call_with(body, name, grid, slot_of, weights, ins, outs, flops, exps=0, prefetch=None):
    axes = len(grid)
    at = lambda *ids: (slot_of(*ids[:axes]), 0, 0)
    if not isinstance(weights, Stream):
        ins = [(weights, (None,) + weights.shape[1:], at)] + ins
        if prefetch is not None:
            return *call(lambda _, *refs: body(*refs), name, grid, ins, outs, flops, exps, prefetch=prefetch), weights
        return *call(body, name, grid, ins, outs, flops, exps), weights
    local, target, pieces = weights
    others = pieces[0][0].shape[1]
    plan, where = plan_of([local], pieces, [target])
    used = [n for n, spans in enumerate(plan) if spans]
    plan, arrays = [plan[n] for n in used], [pieces[n][0] for n in used]
    lead, count, inner = int(prefetch is not None), len(arrays), len(ins)

    def kernel(*refs):
        refs = refs[lead:]
        where_ref, local_ref, refs = refs[0], refs[1], refs[2:]
        piece_refs, refs = refs[:count], refs[count:]
        full_ref, hold, sems = refs[-3:]
        ids = [pl.program_id(n) for n in range(axes)]
        slot = slot_of(*ids)
        first = sum(ids) == slot
        moves = piece_copies(plan, where_ref, piece_refs, [hold], sems)

        @pl.when(jnp.logical_and(first, slot == 0))
        def _():
            for move in moves:
                move.start()
            full_ref[...] = local_ref[...]

        @pl.when(jnp.logical_and(first, slot == 1))
        def _():
            for move in moves:
                move.wait()

        @pl.when(jnp.logical_and(first, slot > 0))
        def _():
            full_ref[...] = hold[jnp.maximum(slot - 1, 0)].astype(BF16)

        body(full_ref, *refs[:-3])

    rows, width = local.shape
    flat = lambda *ids: (0, 0)
    more = [(where, None, pltpu.SMEM), (local, local.shape, flat)] + [(a, None, pl.ANY) for a in arrays]
    full = ((others + 1, rows, width), BF16, (None, rows, width), at)
    scratch = [pltpu.VMEM((others, rows, width), F32), pltpu.SemaphoreType.DMA((where.shape[0],))]
    return call(kernel, name, grid, more + ins, outs + [full], flops, exps, scratch, prefetch)


def attend_kernel(x_ref, w_ref, bias_ref, ctx_ref):
    cols = w_ref.shape[0] // 3
    parts = []
    qkv = (dot(x_ref[...], w_ref[...], COLS) + bias_ref[...]).astype(BF16)
    for h in range(cols // HEAD_DIM):
        q, k, v = (qkv[:, i * cols + h * HEAD_DIM : i * cols + (h + 1) * HEAD_DIM] for i in range(3))
        scores = dot(q, k, COLS)
        largest = jnp.max(scores, axis=-1, keepdims=True)
        expon = jnp.exp2((scores - largest) * EXP_SCALE)
        totals = jnp.sum(expon, axis=-1, keepdims=True)
        parts.append((dot(expon.astype(BF16), v, PLAIN) / totals).astype(BF16).astype(F32))
    context = jnp.concatenate(parts, axis=1)
    step = ctx_ref.shape[0]
    folds = [context[i * step : (i + 1) * step] for i in range(LENGTH // step)]
    ctx_ref[...] = jnp.concatenate(folds, axis=1)


def fold_of(cols):
    return 1 if cols % 128 == 0 else 2


def attend_forward(inputs, weights, bias):
    rows, width = inputs.shape
    cols = weights.shape[0] // 3
    fold = fold_of(cols)
    flat = lambda i: (0, 0)
    return call(
        attend_kernel,
        "attend_forward",
        (rows // LENGTH,),
        [
            (inputs, (LENGTH, width), lambda i: (i, 0)),
            (weights, weights.shape, flat),
            (bias, bias.shape, flat),
        ],
        [((rows // fold, fold * cols), F32, (LENGTH // fold, fold * cols), lambda i: (i, 0))],
        flops=rows * cols * (6 * width + 4 * LENGTH),
        exps=rows * LENGTH * (cols // HEAD_DIM),
    )[0]


def output_kernel(w_ref, x_ref, ctx_ref, vec_ref, low_ref, hid_ref, hbf_ref, nrm_ref, inv_ref):
    slot = pl.program_id(1)
    cols = low_ref.shape[-1]
    folds = [ctx_ref[:, i : i + cols] for i in range(0, ctx_ref.shape[-1], cols)]
    context = jnp.concatenate(folds, axis=0).astype(BF16)
    low_ref[...] = context
    attn = dot(context, w_ref[...], PLAIN)

    @pl.when(slot == 0)
    def _():
        hid_ref[...] = attn

    @pl.when(slot > 0)
    def _():
        hid_ref[...] += attn

    @pl.when(slot == pl.num_programs(1) - 1)
    def _():
        bias, gain, shift = vec_ref[0:1], vec_ref[1:2], vec_ref[2:3]

        def block(at, carry):
            values = x_ref[at].astype(F32) + hid_ref[at] + bias
            hidden, normed, inverse = norm_forward(values, gain, shift)
            hid_ref[at] = hidden
            hbf_ref[at] = hidden.astype(BF16)
            nrm_ref[at] = normed
            inv_ref[at] = inverse
            return carry

        by_rows(LENGTH, 256, block)


def output_forward(slots_at, x, context, weights, vectors):
    rows, width = x.shape
    slots = slots_at.shape[0]
    cols = width // slots
    mine = lambda i, j, at: (i, 0)
    flat = lambda i, j, at: (0, 0)
    token = (LENGTH, width)
    heads = (None, LENGTH, cols)
    return call_with(
        output_kernel,
        "output_forward",
        (rows // LENGTH, slots),
        lambda i, j: j,
        weights,
        [
            (x, token, mine),
            (context, (None, LENGTH // fold_of(cols), fold_of(cols) * cols), lambda i, j, at: (at[j], i, 0)),
            (vectors, vectors.shape, flat),
        ],
        [
            ((slots, rows, cols), BF16, heads, lambda i, j, at: (j, i, 0)),
            ((rows, width), F32, token, mine),
            ((rows, width), BF16, token, mine),
            ((rows, width), F32, token, mine),
            ((rows, 1), F32, (LENGTH, 1), mine),
        ],
        flops=2 * rows * width * width,
        prefetch=slots_at,
    )


def attend_back_kernel(x_ref, ga_ref, gr_ref, w_ref, wo_ref, bias_ref, ctx_ref, gw_ref, gx_ref, sum_ref, gqkv_ref):
    slot = pl.program_id(1)
    cols = wo_ref.shape[0]
    gctx = dot(ga_ref[...], wo_ref[...], COLS).astype(BF16)
    qkv = (dot(x_ref[...], w_ref[...], COLS) + bias_ref[...]).astype(BF16)
    for h in range(cols // HEAD_DIM):
        at = [slice(i * cols + h * HEAD_DIM, i * cols + (h + 1) * HEAD_DIM) for i in range(3)]
        q, k, v = (qkv[:, s] for s in at)
        g = gctx[:, at[0]]
        scores = dot(k, q, COLS)
        largest = jnp.max(scores, axis=0, keepdims=True)
        expon = jnp.exp2((scores - largest) * EXP_SCALE)
        probs = expon * (1.0 / row_sums(expon))
        gqkv_ref[:, at[2]] = dot(probs.astype(BF16), g, PLAIN).astype(BF16)
        weighted = probs * dot(v, g, COLS)
        grad_scores = (weighted - probs * row_sums(weighted)).astype(BF16)
        gqkv_ref[:, at[0]] = (dot(grad_scores, k, ROWS) * SCALE).astype(BF16)
        gqkv_ref[:, at[1]] = (dot(grad_scores, q, PLAIN) * SCALE).astype(BF16)
    grads = gqkv_ref[...]
    sum_ref[...] = row_sums(grads.astype(F32))
    back = dot(grads, w_ref[...], PLAIN)
    gw_ref[:, : 3 * cols] = dot(x_ref[...], grads, ROWS)
    gw_ref[:, 3 * cols :] = dot(ga_ref[...], ctx_ref[...], ROWS)

    @pl.when(slot == 0)
    def _():
        gx_ref[...] = gr_ref[...] + back

    @pl.when(slot > 0)
    def _():
        gx_ref[...] += back


def attend_backward(x, grad_attn, grad_resid, weights, w_output, bias, context):
    rows, width = grad_attn.shape
    slots, cols, _ = w_output.shape
    mine = lambda i, j: (i, 0)
    token = (LENGTH, width)
    weight = lambda i, j: (j, 0, 0)
    return call(
        attend_back_kernel,
        "attend_backward",
        (rows // LENGTH, slots),
        [
            (x, token, mine),
            (grad_attn, token, mine),
            (grad_resid, token, mine),
            (weights, (None, 3 * cols, width), weight),
            (w_output, (None, cols, width), weight),
            (bias, (None, 1, 3 * cols), weight),
            (context, (None, LENGTH, cols), lambda i, j: (j, i, 0)),
        ],
        [
            ((width, slots * 4 * cols), F32, (width, 4 * cols), lambda i, j: (0, j)),
            ((rows, width), F32, token, mine),
            ((rows // LENGTH, slots, 1, 3 * cols), F32, (None, None, 1, 3 * cols), lambda i, j: (i, j, 0, 0)),
        ],
        flops=0,
        moved=0,
        scratch=[pltpu.VMEM((LENGTH, 3 * cols), BF16)],
    )


def inner_kernel(w_ref, h_ref, b_ref, act_ref, slope_ref):
    inner = dot(h_ref[...], w_ref[...], PLAIN) + b_ref[...]
    phi = 0.5 + 0.5 * lax.erf(inner * (0.5**0.5))
    bell = jnp.exp2(inner * inner * (-0.5 * 1.4426950408889634)) * 0.3989422804014327
    act_ref[...] = (inner * phi).astype(BF16)
    slope_ref[...] = phi + inner * bell


def inner_forward(hidden, weights, bias):
    rows, width = hidden.shape
    slots, _, units = bias.shape
    slot = lambda i, j: (i, j, 0)
    block = LENGTH // 2
    return call_with(
        inner_kernel,
        "inner_forward",
        (slots, rows // block),
        lambda i, j: i,
        weights,
        [
            (hidden, (block, width), lambda i, j: (j, 0)),
            (bias, (None, 1, units), lambda i, j: (i, 0, 0)),
        ],
        [
            ((slots, rows, units), BF16, (None, block, units), slot),
            ((slots, rows, units), F32, (None, block, units), slot),
        ],
        flops=2 * rows * width * slots * units,
        exps=2 * rows * slots * units,
    )


def outer_kernel(w_ref, act_ref, hid_ref, vec_ref, out_ref, nrm_ref, inv_ref):
    slot = pl.program_id(1)
    outer = dot(act_ref[...], w_ref[...], PLAIN)

    @pl.when(slot == 0)
    def _():
        out_ref[...] = outer

    @pl.when(slot > 0)
    def _():
        out_ref[...] += outer

    @pl.when(slot == pl.num_programs(1) - 1)
    def _():
        bias, gain, shift = vec_ref[3:4], vec_ref[4:5], vec_ref[5:6]

        def block(at, carry):
            values = hid_ref[at] + (out_ref[at] + bias)
            layer_out, normed, inverse = norm_forward(values, gain, shift)
            out_ref[at] = layer_out
            nrm_ref[at] = normed
            inv_ref[at] = inverse
            return carry

        by_rows(LENGTH, 256, block)


def outer_forward(active, weights, hidden, vectors):
    rows, width = hidden.shape
    slots, _, units = active.shape
    mine = lambda i, j: (i, 0)
    token = (LENGTH, width)
    return call_with(
        outer_kernel,
        "outer_forward",
        (rows // LENGTH, slots),
        lambda i, j: j,
        weights,
        [
            (active, (None, LENGTH, units), lambda i, j: (j, i, 0)),
            (hidden, token, mine),
            (vectors, vectors.shape, lambda i, j: (0, 0)),
        ],
        [
            ((rows, width), F32, token, mine),
            ((rows, width), F32, token, mine),
            ((rows, 1), F32, (LENGTH, 1), mine),
        ],
        flops=2 * rows * width * slots * units,
    )


def last_norm_kernel(cot_ref, nrm_ref, inv_ref, vec_ref, gr_ref, go_ref, sum_ref):
    upstream, normed = cot_ref[...].astype(F32), nrm_ref[...]
    grad = norm_backward(upstream, vec_ref[4:5], normed, inv_ref[...])
    rounded = grad.astype(BF16)
    gr_ref[...] = grad
    go_ref[...] = rounded
    found = (upstream * normed, upstream, rounded.astype(F32))

    @pl.when(pl.program_id(0) == 0)
    def _():
        sum_ref[...] = jnp.zeros_like(sum_ref)

    for i, value in enumerate(found):
        sum_ref[i : i + 1] += row_sums(value)


def last_norm_backward(cotangent, normed, inverse, vectors):
    rows, width = normed.shape
    block = 128
    mine = lambda i: (i, 0)
    flat = lambda i: (0, 0)
    token = (block, width)
    return call(
        last_norm_kernel,
        "last_norm_backward",
        (rows // block,),
        [
            (cotangent, token, mine),
            (normed, token, mine),
            (inverse, (block, 1), mine),
            (vectors, vectors.shape, flat),
        ],
        [
            ((rows, width), F32, token, mine),
            ((rows, width), BF16, token, mine),
            ((8, width), F32, (8, width), flat),
        ],
        flops=0,
        moved=0,
    )


def inner_back_kernel(go_ref, wu_ref, slope_ref, wi_ref, gr_ref, nrm_ref, inv_ref, vec_ref,
                      gi_ref, g1_ref, ga_ref, bsum_ref, sum_ref):
    slot = pl.program_id(1)
    grad_inner = (dot(go_ref[...], wu_ref[...], COLS) * slope_ref[...]).astype(BF16)
    gi_ref[...] = grad_inner
    bsum_ref[...] = row_sums(grad_inner.astype(F32))
    back = dot(grad_inner, wi_ref[...], COLS)

    @pl.when(slot == 0)
    def _():
        g1_ref[...] = gr_ref[...] + back

    @pl.when(slot > 0)
    def _():
        g1_ref[...] += back

    @pl.when(slot == pl.num_programs(1) - 1)
    def _():
        gain = vec_ref[1:2]

        def block(at, sums):
            upstream, normed = g1_ref[at], nrm_ref[at]
            grad = norm_backward(upstream, gain, normed, inv_ref[at])
            rounded = grad.astype(BF16)
            g1_ref[at] = grad
            ga_ref[at] = rounded
            found = (upstream * normed, upstream, rounded.astype(F32))
            return tuple(s + row_sums(f) for s, f in zip(sums, found))

        for i, total in enumerate(by_rows(LENGTH, 256, block, (jnp.zeros_like(gain),) * 3)):
            sum_ref[i : i + 1] = total


def inner_backward(grad_outer, w_outer, slope, w_inner, grad_resid2, normed, inverse, vectors):
    rows, width = grad_outer.shape
    slots, units, _ = w_outer.shape
    mine = lambda i, j: (i, 0)
    token = (LENGTH, width)
    slot = lambda i, j: (j, i, 0)
    weight = lambda i, j: (j, 0, 0)
    return call(
        inner_back_kernel,
        "inner_backward",
        (rows // LENGTH, slots),
        [
            (grad_outer, token, mine),
            (w_outer, (None, units, width), weight),
            (slope, (None, LENGTH, units), slot),
            (w_inner, (None, width, units), weight),
            (grad_resid2, token, mine),
            (normed, token, mine),
            (inverse, (LENGTH, 1), mine),
            (vectors, vectors.shape, lambda i, j: (0, 0)),
        ],
        [
            ((slots, rows, units), BF16, (None, LENGTH, units), slot),
            ((rows, width), F32, token, mine),
            ((rows, width), BF16, token, mine),
            ((rows // LENGTH, slots, 1, units), F32, (None, None, 1, units), lambda i, j: (i, j, 0, 0)),
            ((rows // LENGTH, 8, width), F32, (None, 8, width), lambda i, j: (i, 0, 0)),
        ],
        flops=0,
        moved=0,
    )


def narrow_kernel(x_ref, out_ref):
    out_ref[...] = x_ref[...].astype(BF16)


def narrow(values, block_rows):
    rows, width = values.shape
    at = lambda i: (i, 0)
    block = (block_rows, width)
    out = ((rows, width), BF16, block, at)
    return call(narrow_kernel, "narrow", (rows // block_rows,), [(values, block, at)], [out], 0)[0]


def shift_to(values, tensor, k):
    return lax.ppermute(values, "tensor", [(i, (i + k) % tensor) for i in range(tensor)])


def flip(values, bit):
    return lax.ppermute(values, "dp", [(i, i ^ bit) for i in range(8)])


def stage(*values):
    return lax.optimization_barrier(values)


def slots_kernel(slot_ref, local_ref, x_ref, out_ref):
    del slot_ref
    first = pl.program_id(0) == 0

    @pl.when(first)
    def _():
        out_ref[...] = local_ref[...]

    @pl.when(jnp.logical_not(first))
    def _():
        out_ref[...] = x_ref[...].reshape(out_ref.shape).astype(BF16)


def gather_plain(local, dp, tensor):
    rows, width = local.shape
    share = rows // dp
    piece = lax.dynamic_slice_in_dim(local, lax.axis_index("dp") * share, share, 0).astype(F32)
    full = lax.all_gather(piece, ("dp", "tensor"), axis=0).reshape(dp, tensor, share, width)
    order = (lax.axis_index("tensor") - jnp.arange(tensor, dtype=jnp.int32)) % tensor
    if share % 8:
        full = full.swapaxes(0, 1).reshape(1, tensor, rows, width)
    lead, _, part, _ = full.shape
    return pl.pallas_call(
        slots_kernel,
        grid_spec=pltpu.PrefetchScalarGridSpec(
            num_scalar_prefetch=1,
            grid=(tensor,),
            in_specs=[
                pl.BlockSpec((rows, width), lambda i, slot: (0, 0)),
                pl.BlockSpec((lead, None, part, width), lambda i, slot: (0, slot[i], 0, 0)),
            ],
            out_specs=pl.BlockSpec((None, rows, width), lambda i, slot: (i, 0, 0)),
        ),
        out_shape=jax.ShapeDtypeStruct((tensor, rows, width), BF16),
        cost_estimate=pl.CostEstimate(flops=0, bytes_accessed=6 * full.size, transcendentals=0),
        compiler_params=pltpu.CompilerParams(vmem_limit_bytes=48 << 20),
        name="slots",
    )(order, local, full)


def assemble_kernel(plan, where_ref, local_ref, *refs):
    *pieces, out_ref, hold, sems = refs
    moves = piece_copies(plan, where_ref, pieces, [hold], sems)
    for move in moves:
        move.start()
    out_ref[0] = local_ref[...]
    for move in moves:
        move.wait()
    for k in range(hold.shape[0]):

        def block(at, carry, k=k):
            out_ref[k + 1, at] = hold[k, at].astype(BF16)
            return carry

        by_rows(hold.shape[1], 96, block)


def assemble(stream):
    local, target, pieces = stream
    rows, width = local.shape
    others = pieces[0][0].shape[1]
    plan, where = plan_of([local], pieces, [target])
    space = pl.BlockSpec(memory_space=pltpu.VMEM)
    return pl.pallas_call(
        partial(assemble_kernel, plan),
        in_specs=[pl.BlockSpec(memory_space=pltpu.SMEM), space] + [pl.BlockSpec(memory_space=pl.ANY)] * len(pieces),
        out_specs=space,
        out_shape=jax.ShapeDtypeStruct((others + 1, rows, width), BF16),
        scratch_shapes=[pltpu.VMEM((others, rows, width), F32), pltpu.SemaphoreType.DMA((where.shape[0],))],
        cost_estimate=pl.CostEstimate(flops=0, bytes_accessed=others * rows * width * 6, transcendentals=0),
        compiler_params=pltpu.CompilerParams(vmem_limit_bytes=48 << 20),
        name="assemble",
    )(where, local, *(array for array, _ in pieces))


def shares(weights, dp=8):
    me = lax.axis_index("dp")
    cut = [lax.dynamic_slice_in_dim(w, me * (w.shape[0] // dp), w.shape[0] // dp, 0) for w in weights]
    return jnp.concatenate(cut, axis=0).astype(F32)


def across(values, tensor):
    return [shift_to(values, tensor, k) for k in range(1, tensor)]


def wide(v, w):
    return jnp.concatenate([v, w], axis=0)


def other_core(*values):
    return tuple(flip(v, 1) for v in values)


def copy_kernel(plan, count, *refs):
    ins, outs = refs[:count], refs[count:]
    for source, source_at, target, target_at in plan:
        outs[target][target_at] = ins[source][source_at]


def copies(ins, shapes, plan):
    space = pl.BlockSpec(memory_space=pltpu.VMEM)
    return pl.pallas_call(
        partial(copy_kernel, plan, len(ins)),
        in_specs=[space] * len(ins),
        out_specs=[space] * len(shapes),
        out_shape=[jax.ShapeDtypeStruct(shape, F32) for shape in shapes],
        cost_estimate=pl.CostEstimate(flops=0, bytes_accessed=0, transcendentals=0),
        compiler_params=pltpu.CompilerParams(vmem_limit_bytes=32 << 20),
        name="copies",
    )(*ins)


def halves(arrived, upper):
    rows, width = arrived[0].shape
    n = len(arrived)
    plan = [(k, (slice(0, upper),), 0, (0, k)) for k in range(n)]
    plan += [(k, (slice(upper, rows),), 1, (0, k)) for k in range(n)]
    return copies(arrived, [(1, n, upper, width), (1, n, rows - upper, width)], plan)


def join(a, ax, b, by):
    _, n, upper, width = a.shape
    lower = b.shape[2]
    plan = []
    for i, (v, w) in enumerate(((a, b), (ax, by))):
        every = slice(None)
        plan += [(2 * i, (0,), 0, (i,)), (2 * i + 1, (0,), 1, (i,))]
        plan += [(2 * i, (0,), 2, (i, every, slice(0, upper))), (2 * i + 1, (0,), 2, (i, every, slice(upper, upper + lower)))]
    shapes = [(2, n, upper, width), (2, n, lower, width), (2, n, upper + lower, width)]
    return copies([a, b, ax, by], shapes, plan)


def pieces_of(locals_, a, b, ay, bx, c, d):
    me = lax.axis_index("dp")
    cut_at, end = a.shape[2], a.shape[2] + b.shape[2]
    ends = [0]
    for w in locals_:
        ends.append(ends[-1] + w.shape[0] // 8)

    def spans(first, last):
        found = []
        for target in range(len(locals_)):
            low, high = max(first, ends[target]), min(last, ends[target + 1])
            if low < high:
                found.append((low - first, high - low, target, low - ends[target]))
        return found

    upper = lambda rels: [(i, me ^ r, 0, spans(0, cut_at)) for i, r in enumerate(rels)]
    lower = lambda rels, base=0: [(i, me ^ r, base, spans(cut_at, end)) for i, r in enumerate(rels)]
    return [
        (a, upper((0, 2))),
        (b, lower((0, 4))),
        (ay, upper((4, 6))),
        (bx, lower((2, 6))),
        (c, upper((1, 3)) + lower((1, 5), cut_at)),
        (d[0], upper((5, 7))),
        (d[1], lower((3, 7))),
    ]


def block_order(width):
    me = lax.axis_index("dp")
    share = width // 8
    rel = jnp.array([7, 5, 3, 1, 6, 4, 2, 0])
    source = (me ^ rel[jnp.arange(width) // share]) * share + jnp.arange(width) % share
    return (lax.broadcasted_iota(jnp.int32, (width, width), 0) == source[None, :]).astype(BF16)


def grad_kernel(count, *refs):
    order_ref, refs = refs[0], refs[1:]
    lefts, rights, (send_ref, keep_ref), holds = (
        refs[:count], refs[count : 2 * count], refs[2 * count : 2 * count + 2], refs[2 * count + 2 :],
    )

    @pl.when(pl.program_id(0) == 0)
    def _():
        for left, hold in zip(lefts, holds):
            hold[...] = dot(left[...], order_ref[...], PLAIN).astype(BF16)

    half = send_ref.shape[0]
    start = 0
    for hold, right in zip(holds, rights):
        span = slice(start, start + right.shape[-1])
        value = dot(hold[...], right[...], ROWS)
        send_ref[:, span] = value[:half]
        keep_ref[:, span] = value[half:]
        start = span.stop


def grad_rows(order, pairs):
    rows, width = pairs[0][0].shape
    slots = pairs[0][1].shape[0]
    cols = sum(r.shape[-1] for _, r in pairs)
    flat = lambda j: (0, 0)
    ins = [(order, order.shape, flat)]
    ins += [(left, left.shape, flat) for left, _ in pairs]
    ins += [(right, (None,) + right.shape[1:], lambda j: (j, 0, 0)) for _, right in pairs]
    out = ((width // 2, slots * cols), F32, (width // 2, cols), lambda j: (0, j))
    scratch = [pltpu.VMEM((rows, width), BF16)] * len(pairs)
    return call(
        partial(grad_kernel, len(pairs)), "grad_rows", (slots,), ins, [out, out], 0, 0, scratch, moved=0
    )


def full_kernel(count, *refs):
    lefts, rights, out_ref = refs[:count], refs[count:-1], refs[-1]
    start = 0
    for left, right in zip(lefts, rights):
        span = slice(start, start + right.shape[-1])
        out_ref[:, span] = dot(left[...], right[...], ROWS)
        start = span.stop


def grad_full(*pairs):
    rows, width = pairs[0][0].shape
    slots = pairs[0][1].shape[0]
    cols = sum(r.shape[-1] for _, r in pairs)
    ins = [(left, left.shape, lambda j: (0, 0)) for left, _ in pairs]
    ins += [(right, (None,) + right.shape[1:], lambda j: (j, 0, 0)) for _, right in pairs]
    return call(
        partial(full_kernel, len(pairs)),
        "grad_full",
        (slots,),
        ins,
        [((width, slots * cols), F32, (width, cols), lambda j: (0, j))],
        flops=0,
        moved=0,
    )[0]


def split_paths(held, share):
    mid = held.shape[1] // 2
    pick = lambda i, cols: held[i * share : (i + 1) * share, cols]
    a, b = slice(None, mid), slice(mid, None)
    join = lambda i, j, cols: jnp.concatenate([pick(i, cols), pick(j, cols)], axis=0)
    return (join(0, 2, a), join(1, 3, a)), (join(0, 1, b), join(2, 3, b))


def scatter_plain(grad, tensor):
    part = lax.psum_scatter(grad, "dp", scatter_dimension=0, tiled=True)
    part = columns(part, tensor)
    return sum((shift_to(part[k], tensor, tensor - k) for k in range(1, tensor)), part[0])


def columns(part, tensor):
    cols = part.shape[1] // tensor
    return [part[:, k * cols : (k + 1) * cols] for k in range(tensor)]


def up(values, tensor, step):
    return lax.ppermute(values, "tensor", [(i, i + 1) for i in range(step)])


def down(values, tensor, step):
    return lax.ppermute(values, "tensor", [(i, i - 1) for i in range(tensor - step, tensor)])


def place_kernel(z_ref, own_ref, *refs):
    *others, out_ref = refs
    count = len(others) // 2
    below, above = others[:count], others[count:]
    away = pl.program_id(0) - z_ref[0]

    @pl.when(away == 0)
    def _():
        out_ref[...] = own_ref[...]

    for k in range(count):

        @pl.when(away == -(k + 1))
        def _(k=k):
            out_ref[...] = below[k][...]

        @pl.when(away == k + 1)
        def _(k=k):
            out_ref[...] = above[k][...]


def place(own, below, above):
    rows, width = own.shape
    count = len(below) + 1
    whole = (rows, width)
    return call(
        place_kernel,
        "place",
        (count,),
        [(v, whole, lambda i, z: (0, 0)) for v in (own, *below, *above)],
        [((count * rows, width), F32, whole, lambda i, z: (i, 0))],
        flops=0,
        moved=0,
        prefetch=lax.axis_index("tensor").astype(jnp.int32).reshape(1),
    )[0]


def onward(values, tensor, step):
    u, d = values
    u = lax.ppermute(u, "tensor", [(i, i + 1) for i in range(step - 1, tensor - 1)])
    d = lax.ppermute(d, "tensor", [(i, i - 1) for i in range(1, tensor - step + 1)])
    return u, d


def swap(values, tensor, bit):
    return lax.ppermute(values, "tensor", [(i, i ^ bit) for i in range(tensor)])


def shards(
    dp,
    tensor,
    inputs,
    w_query,
    b_query,
    w_key,
    w_value,
    b_value,
    w_output,
    b_output,
    gain_attn,
    shift_attn,
    w_inner,
    b_inner,
    w_outer,
    b_outer,
    gain_ffn,
    shift_ffn,
    cotangent,
):
    tok_rows, width = inputs.shape
    own_rows = tok_rows // tensor
    cols = w_query.shape[1]
    z = lax.axis_index("tensor")
    own = lambda a: lax.dynamic_slice_in_dim(a, z * own_rows, own_rows, 0)
    row = lambda a: a.astype(F32)[None, :]

    vectors = row(jnp.concatenate([b_query, jnp.zeros_like(b_query), b_value, b_inner]))
    qkv_local = jnp.concatenate([w_query.T, w_key.T, w_value.T], axis=0)
    x, cot = own(inputs), own(cotangent)
    rows_of = (b_output, gain_attn, shift_attn, b_outer, gain_ffn, shift_ffn, b_outer, b_outer)
    wide_vectors = jnp.stack(rows_of).astype(F32)
    slots_at = (z - jnp.arange(tensor, dtype=jnp.int32)) % tensor
    staged = (
        dp == 8 and tensor == 4 and own_rows == LENGTH and width % 128 == 0
        and w_inner.shape == w_outer.shape == (width, width) and cols % 64 == 0
    )

    def rest_of_attention(context, weights):
        return output_forward(slots_at, x, context, weights, wide_vectors)


    def small_sums(qkv_sums, inner_sums, sums_one, sums_two):
        by_slot = jnp.concatenate([jnp.sum(qkv_sums, axis=0), jnp.sum(inner_sums, axis=0)], axis=-1)
        by_place = by_slot[slots_at].reshape(-1)
        rest = jnp.concatenate([jnp.sum(sums_one, axis=0)[:3], sums_two[:3]]).reshape(-1)
        return jnp.concatenate([by_place, rest])

    local_bias = vectors[:, : 3 * cols]
    context = attend_forward(inputs, qkv_local, local_bias)
    context = context.reshape(tensor, -1, context.shape[1])
    if not staged:
        vectors = jnp.stack([vectors] + across(vectors, tensor))
        qkv_bias, inner_bias = vectors[..., : 3 * cols], vectors[..., 3 * cols :]
        inner_full, output_full, outer_full, qkv_full = (
            gather_plain(w, dp, tensor) for w in (w_inner, w_output, w_outer, qkv_local)
        )
        context = lax.all_to_all(context, "tensor", 0, 0, tiled=True)
        context, hidden, hidden_bf, normed, inverse, output_full = rest_of_attention(context, output_full)
        active, slope, inner_full = inner_forward(hidden_bf, inner_full, inner_bias)
        layer_out, normed_two, inverse_two, outer_full = outer_forward(active, outer_full, hidden, wide_vectors)
        grad_resid2, grad_outer, sums_two = last_norm_backward(cot, normed_two, inverse_two, wide_vectors)
        layer_out = narrow(lax.all_gather(layer_out, "tensor", axis=0, tiled=True), own_rows)
        grad_inner, grad_resid1, grad_attn, inner_sums, sums_one = inner_backward(
            grad_outer, outer_full, slope, inner_full, grad_resid2, normed, inverse, wide_vectors
        )
        part3, grad_x, qkv_sums = attend_backward(x, grad_attn, grad_resid1, qkv_full, output_full, qkv_bias, context)
        grad_inputs = lax.all_gather(grad_x, "tensor", axis=0, tiled=True)
        gu = scatter_plain(grad_full((grad_outer, active)), tensor)
        gi = scatter_plain(grad_full((hidden_bf, grad_inner)), tensor)
        gqkv = scatter_plain(part3, tensor)
        gqkv, go = gqkv[:, : 3 * cols], gqkv[:, 3 * cols :]
        sums = lax.psum(small_sums(qkv_sums, inner_sums, sums_one, sums_two), ("dp", "tensor"))
    else:
        order = block_order(width)
        share = width // 8
        p1, p2, p3 = shares([w_inner, w_output]), shares([w_outer]), shares([qkv_local])
        n1, n2, n3 = (-(-p.shape[0] // 16) * 8 for p in (p1, p2, p3))

        z1, arrived = across(p1, tensor), across(vectors, tensor)
        vectors = jnp.stack([vectors] + arrived)
        a1, b1 = halves(z1, n1)
        a1, b1, p2, context, vectors = stage(a1, b1, p2, context, vectors)
        qkv_bias, inner_bias = vectors[..., : 3 * cols], vectors[..., 3 * cols :]

        ax, by, z2 = flip(a1, 2), flip(b1, 4), across(p2, tensor)
        a1, b1, ab1 = join(a1, ax, b1, by)
        a2, b2 = halves(z2, n2)
        a1, b1, ab1, a2, b2, context, x, order = stage(a1, b1, ab1, a2, b2, context, x, order)

        c1 = flip(ab1, 1)
        context, c1 = stage(context, c1)
        context = lax.all_to_all(context, "tensor", 0, 0, tiled=True)
        ay1, bx1, ax, by = flip(a1, 4), flip(b1, 2), flip(a2, 2), flip(b2, 4)
        a2, b2, ab2 = join(a2, ax, b2, by)
        d1 = other_core(ay1, bx1)
        ay1, bx1, a2, b2, ab2, p3 = stage(ay1, bx1, a2, b2, ab2, p3)

        c2, ay2, bx2 = flip(ab2, 1), flip(a2, 4), flip(b2, 2)
        pieces = pieces_of([w_inner, w_output], a1, b1, ay1, bx1, c1, d1)
        context, hidden, hidden_bf, normed, inverse, output_full = rest_of_attention(context, Stream(w_output, 1, pieces))
        active, slope, inner_full = inner_forward(hidden_bf, Stream(w_inner, 0, pieces), inner_bias)
        c2, ay2, bx2, p3, active = stage(c2, ay2, bx2, p3, active)

        d2, z3 = other_core(ay2, bx2), across(p3, tensor)
        pieces = pieces_of([w_outer], a2, b2, ay2, bx2, c2, d2)
        layer_out, normed_two, inverse_two, outer_full = outer_forward(
            active, Stream(w_outer, 0, pieces), hidden, wide_vectors
        )
        *z3, layer_out, normed_two = stage(*z3, layer_out, normed_two)

        layer_out = lax.all_gather(layer_out, "tensor", axis=0, tiled=True)
        a3, b3 = halves(z3, n3)
        ax, by = flip(a3, 2), flip(b3, 4)
        grad_resid2, grad_outer, sums_two = last_norm_backward(cot, normed_two, inverse_two, wide_vectors)
        a3, b3, ab3 = join(a3, ax, b3, by)
        a3, b3, ab3, grad_outer = stage(a3, b3, ab3, grad_outer)

        ay3, bx3, c3 = flip(a3, 4), flip(b3, 2), flip(ab3, 1)
        part1 = grad_full((grad_outer, active))
        part1, grad_outer = stage(part1, grad_outer)
        part1 = lax.psum_scatter(part1, "dp", scatter_dimension=0, tiled=True)
        grad_inner, grad_resid1, grad_attn, inner_sums, sums_one = inner_backward(
            grad_outer, outer_full, slope, inner_full, grad_resid2, normed, inverse, wide_vectors
        )
        ay3, bx3, c3, grad_inner, grad_attn = stage(ay3, bx3, c3, grad_inner, grad_attn)

        d3 = other_core(ay3, bx3)
        send, keep = grad_rows(order, [(hidden_bf, grad_inner)])
        *d3, send, grad_attn = stage(*d3, send, grad_attn)

        got = flip(send, 1)
        qkv_full = assemble(Stream(qkv_local, 0, pieces_of([qkv_local], a3, b3, ay3, bx3, c3, d3)))
        (a, ak), (b, bk) = split_paths(keep + got, share)
        a, b, qkv_full, grad_attn = stage(a, b, qkv_full, grad_attn)

        ax, by = flip(a, 2), flip(b, 4)
        part3, grad_x, qkv_sums = attend_backward(
            x, grad_attn, grad_resid1, qkv_full, output_full, qkv_bias, context
        )
        a, b = ak + ax, bk + by
        a_send, b_send = stage(a[:share], b[:share])

        part3 = lax.psum_scatter(part3, "dp", scatter_dimension=0, tiled=True)
        g1 = onward((grad_x, grad_x), tensor, 1)
        ay, bx = flip(a_send, 4), flip(b_send, 2)
        part2 = jnp.concatenate([a[share:] + ay, b[share:] + bx], axis=1)
        extra = small_sums(qkv_sums, inner_sums, sums_one, sums_two)
        extra = jnp.pad(extra, (0, -extra.shape[0] % (8 * width))).reshape(-1, width)
        extra = extra + flip(extra, 1)
        layer_out = narrow(layer_out, own_rows)
        first = columns(wide(part1, part2), tensor)
        g2 = onward(g1, tensor, 2)
        _, _, extra, first[0], first[1], first[2], first[3], layer_out = stage(*g1, extra, *first, layer_out)

        u, d = up(first[1], tensor, 1), down(first[3], tensor, 1)
        extra = extra + flip(extra, 2)
        g3 = onward(g2, tensor, 3)
        _, _, u, d, part3, extra = stage(*g2, first[2] + u, first[2] + d, part3, extra)

        u, d = up(u, tensor, 2), down(d, tensor, 2)
        last = columns(part3, tensor)
        v, w = up(last[1], tensor, 1), down(last[3], tensor, 1)
        extra = extra + flip(extra, 4)
        v, w, extra = stage(last[2] + v, last[2] + w, extra)

        v, w = up(v, tensor, 2), down(w, tensor, 2)
        extra = extra + swap(extra, tensor, 1)
        _, _, u, d, v, w, extra = stage(*g3, first[3] + u, first[1] + d, last[3] + v, last[1] + w, extra)

        u, d, v, w = up(u, tensor, 3), down(d, tensor, 3), up(v, tensor, 3), down(w, tensor, 3)
        extra = extra + swap(extra, tensor, 2)
        v, w, grad_x = stage(v, w, grad_x)
        grad_inputs = place(grad_x, [g1[0], g2[0], g3[0]], [g1[1], g2[1], g3[1]])
        gu, gqkv = first[0] + u + d, last[0] + v + w
        gu, gi = gu[:share], gu[share:]
        gqkv, go = gqkv[:, : 3 * cols], gqkv[:, 3 * cols :]
        sums = extra.reshape(-1)

    span = 3 * cols + w_inner.shape[1]
    mine = lax.dynamic_slice_in_dim(sums, z * span, span, 0)
    rest = sums[span * tensor :][: 6 * width].reshape(6, width)
    return (
        layer_out,
        grad_inputs,
        gqkv[:, :cols],
        mine[:cols],
        gqkv[:, cols : 2 * cols],
        gqkv[:, 2 * cols :],
        mine[2 * cols : 3 * cols],
        go.T,
        rest[2],
        rest[0],
        rest[1],
        gi,
        mine[3 * cols :],
        gu.T,
        rest[5],
        rest[3],
        rest[4],
    )


def solution(mesh):
    wide, tall, vector = P(None, "tensor"), P("tensor", None), P("tensor")
    tokens, both = P("dp", None), P("dp", "tensor")
    in_specs = (
        tokens, wide, vector, wide, wide, vector, tall, P(), P(), P(), wide, vector, tall, P(), P(), P(), tokens,
    )
    out_specs = (
        tokens, tokens, both, vector, both, both, vector, P("tensor", "dp"), P(), P(), P(), both, vector,
        P("tensor", "dp"), P(), P(), P(),
    )
    body = partial(shards, mesh.shape["dp"], mesh.shape["tensor"])
    return jax.shard_map(body, mesh=mesh, in_specs=in_specs, out_specs=out_specs, check_vma=False)
```

```python
import math
from functools import partial
from typing import NamedTuple

import jax
import jax.numpy as jnp
from jax import lax
from jax.experimental import pallas as pl
from jax.experimental.pallas import tpu as pltpu
from jax.sharding import PartitionSpec as P

HEAD_DIM = 64
LENGTH = 512
EPSILON = 1e-12
F32 = jnp.float32
BF16 = jnp.bfloat16
SCALE = HEAD_DIM ** (-0.5)
EXP_SCALE = SCALE * 1.4426950408889634
ROWS = ((0,), (0,))
PLAIN = ((1,), (0,))
COLS = ((1,), (1,))


def dot(left, right, dims):
    return lax.dot_general(left, right, (dims, ((), ())), preferred_element_type=F32)


def norm_forward(values, gain, shift):
    center = values - jnp.mean(values, axis=-1, keepdims=True)
    inverse = lax.rsqrt(jnp.mean(center * center, axis=-1, keepdims=True) + EPSILON)
    normed = center * inverse
    return (normed * gain + shift, normed, inverse)


def norm_backward(upstream, gain, normed, inverse):
    scaled = upstream * gain
    first_mean = jnp.mean(scaled, axis=-1, keepdims=True)
    cross_mean = jnp.mean(scaled * normed, axis=-1, keepdims=True)
    return inverse * (scaled - first_mean - normed * cross_mean)


def by_rows(rows, step, body, carry=()):
    return lax.fori_loop(0, rows // step, lambda i, c: body(pl.ds(pl.multiple_of(i * step, step), step), c), carry)


def row_sums(values):
    return jnp.sum(values, axis=0, keepdims=True)


def size_of(shape, dtype):
    return math.prod(shape) * jnp.dtype(dtype).itemsize


def call(kernel, name, grid, ins, outs, flops, exps=0, scratch=(), prefetch=None, moved=None):
    if moved is None:
        moved = sum(size_of(a.shape, a.dtype) for a, _, _ in ins) + sum(size_of(s, t) for s, t, _, _ in outs)
    lead = () if prefetch is None else (prefetch,)
    return pl.pallas_call(
        kernel,
        grid_spec=pltpu.PrefetchScalarGridSpec(
            num_scalar_prefetch=len(lead),
            grid=grid,
            in_specs=[pl.BlockSpec(memory_space=m) if b is None else pl.BlockSpec(b, m) for _, b, m in ins],
            out_specs=[pl.BlockSpec(b, m) for _, _, b, m in outs],
            scratch_shapes=list(scratch),
        ),
        out_shape=[jax.ShapeDtypeStruct(s, t) for s, t, _, _ in outs],
        cost_estimate=pl.CostEstimate(flops=flops, bytes_accessed=moved, transcendentals=exps),
        compiler_params=pltpu.CompilerParams(vmem_limit_bytes=56 << 20),
        name=name,
    )(*lead, *(a for a, _, _ in ins))


class Stream(NamedTuple):
    local: jax.Array
    target: int
    pieces: list


def plan_of(locals_, pieces, wanted):
    plan, where = [], []
    for _, parts in pieces:
        plan.append([])
        for entry, sender, base, spans in parts:
            for row, rows, target, offset in spans:
                if target in wanted:
                    plan[-1].append((entry, base + row, rows, wanted.index(target)))
                    where.append(sender * (locals_[wanted.index(target)].shape[0] // 8) + offset)
    return plan, jnp.stack(where)


def piece_copies(plan, where_ref, pieces, holds, sems):
    found = []
    for piece, spans in zip(pieces, plan):
        for i, source, rows, target in spans:
            start = pl.multiple_of(where_ref[len(found)], 8)
            found.append(
                pltpu.make_async_copy(
                    piece.at[i, :, pl.ds(source, rows)], holds[target].at[:, pl.ds(start, rows)], sems.at[len(found)]
                )
            )
    return found


def call_with(body, name, grid, slot_of, weights, ins, outs, flops, exps=0, prefetch=None):
    axes = len(grid)
    at = lambda *ids: (slot_of(*ids[:axes]), 0, 0)
    if not isinstance(weights, Stream):
        ins = [(weights, (None,) + weights.shape[1:], at)] + ins
        if prefetch is not None:
            return *call(lambda _, *refs: body(*refs), name, grid, ins, outs, flops, exps, prefetch=prefetch), weights
        return *call(body, name, grid, ins, outs, flops, exps), weights
    local, target, pieces = weights
    others = pieces[0][0].shape[1]
    plan, where = plan_of([local], pieces, [target])
    used = [n for n, spans in enumerate(plan) if spans]
    plan, arrays = [plan[n] for n in used], [pieces[n][0] for n in used]
    lead, count, inner = int(prefetch is not None), len(arrays), len(ins)

    def kernel(*refs):
        refs = refs[lead:]
        where_ref, local_ref, refs = refs[0], refs[1], refs[2:]
        piece_refs, refs = refs[:count], refs[count:]
        full_ref, hold, sems = refs[-3:]
        ids = [pl.program_id(n) for n in range(axes)]
        slot = slot_of(*ids)
        first = sum(ids) == slot
        moves = piece_copies(plan, where_ref, piece_refs, [hold], sems)

        @pl.when(jnp.logical_and(first, slot == 0))
        def _():
            for move in moves:
                move.start()
            full_ref[...] = local_ref[...]

        @pl.when(jnp.logical_and(first, slot == 1))
        def _():
            for move in moves:
                move.wait()

        @pl.when(jnp.logical_and(first, slot > 0))
        def _():
            full_ref[...] = hold[jnp.maximum(slot - 1, 0)].astype(BF16)

        body(full_ref, *refs[:-3])

    rows, width = local.shape
    flat = lambda *ids: (0, 0)
    more = [(where, None, pltpu.SMEM), (local, local.shape, flat)] + [(a, None, pl.ANY) for a in arrays]
    full = ((others + 1, rows, width), BF16, (None, rows, width), at)
    scratch = [pltpu.VMEM((others, rows, width), F32), pltpu.SemaphoreType.DMA((where.shape[0],))]
    return call(kernel, name, grid, more + ins, outs + [full], flops, exps, scratch, prefetch)


def attend_kernel(x_ref, w_ref, bias_ref, ctx_ref):
    cols = w_ref.shape[0] // 3
    parts = []
    qkv = (dot(x_ref[...], w_ref[...], COLS) + bias_ref[...]).astype(BF16)
    for h in range(cols // HEAD_DIM):
        q, k, v = (qkv[:, i * cols + h * HEAD_DIM : i * cols + (h + 1) * HEAD_DIM] for i in range(3))
        scores = dot(q, k, COLS)
        largest = jnp.max(scores, axis=-1, keepdims=True)
        expon = jnp.exp2((scores - largest) * EXP_SCALE)
        totals = jnp.sum(expon, axis=-1, keepdims=True)
        parts.append((dot(expon.astype(BF16), v, PLAIN) / totals).astype(BF16).astype(F32))
    context = jnp.concatenate(parts, axis=1)
    step = ctx_ref.shape[0]
    folds = [context[i * step : (i + 1) * step] for i in range(LENGTH // step)]
    ctx_ref[...] = jnp.concatenate(folds, axis=1)


def fold_of(cols):
    return 1 if cols % 128 == 0 else 2


def attend_forward(inputs, weights, bias):
    rows, width = inputs.shape
    cols = weights.shape[0] // 3
    fold = fold_of(cols)
    flat = lambda i: (0, 0)
    return call(
        attend_kernel,
        "attend_forward",
        (rows // LENGTH,),
        [
            (inputs, (LENGTH, width), lambda i: (i, 0)),
            (weights, weights.shape, flat),
            (bias, bias.shape, flat),
        ],
        [((rows // fold, fold * cols), F32, (LENGTH // fold, fold * cols), lambda i: (i, 0))],
        flops=rows * cols * (6 * width + 4 * LENGTH),
        exps=rows * LENGTH * (cols // HEAD_DIM),
    )[0]


def output_kernel(w_ref, x_ref, ctx_ref, vec_ref, low_ref, hid_ref, hbf_ref, nrm_ref, inv_ref):
    slot = pl.program_id(1)
    cols = low_ref.shape[-1]
    folds = [ctx_ref[:, i : i + cols] for i in range(0, ctx_ref.shape[-1], cols)]
    context = jnp.concatenate(folds, axis=0).astype(BF16)
    low_ref[...] = context
    attn = dot(context, w_ref[...], PLAIN)

    @pl.when(slot == 0)
    def _():
        hid_ref[...] = attn

    @pl.when(slot > 0)
    def _():
        hid_ref[...] += attn

    @pl.when(slot == pl.num_programs(1) - 1)
    def _():
        bias, gain, shift = vec_ref[0:1], vec_ref[1:2], vec_ref[2:3]

        def block(at, carry):
            values = x_ref[at].astype(F32) + hid_ref[at] + bias
            hidden, normed, inverse = norm_forward(values, gain, shift)
            hid_ref[at] = hidden
            hbf_ref[at] = hidden.astype(BF16)
            nrm_ref[at] = normed
            inv_ref[at] = inverse
            return carry

        by_rows(LENGTH, 256, block)


def output_forward(slots_at, x, context, weights, vectors):
    rows, width = x.shape
    slots = slots_at.shape[0]
    cols = width // slots
    mine = lambda i, j, at: (i, 0)
    flat = lambda i, j, at: (0, 0)
    token = (LENGTH, width)
    heads = (None, LENGTH, cols)
    return call_with(
        output_kernel,
        "output_forward",
        (rows // LENGTH, slots),
        lambda i, j: j,
        weights,
        [
            (x, token, mine),
            (context, (None, LENGTH // fold_of(cols), fold_of(cols) * cols), lambda i, j, at: (at[j], i, 0)),
            (vectors, vectors.shape, flat),
        ],
        [
            ((slots, rows, cols), BF16, heads, lambda i, j, at: (j, i, 0)),
            ((rows, width), F32, token, mine),
            ((rows, width), BF16, token, mine),
            ((rows, width), F32, token, mine),
            ((rows, 1), F32, (LENGTH, 1), mine),
        ],
        flops=2 * rows * width * width,
        prefetch=slots_at,
    )


def attend_back_kernel(x_ref, ga_ref, gr_ref, w_ref, wo_ref, bias_ref, ctx_ref, gw_ref, gx_ref, sum_ref, gqkv_ref):
    slot = pl.program_id(1)
    cols = wo_ref.shape[0]
    gctx = dot(ga_ref[...], wo_ref[...], COLS).astype(BF16)
    qkv = (dot(x_ref[...], w_ref[...], COLS) + bias_ref[...]).astype(BF16)
    for h in range(cols // HEAD_DIM):
        at = [slice(i * cols + h * HEAD_DIM, i * cols + (h + 1) * HEAD_DIM) for i in range(3)]
        q, k, v = (qkv[:, s] for s in at)
        g = gctx[:, at[0]]
        scores = dot(k, q, COLS)
        largest = jnp.max(scores, axis=0, keepdims=True)
        expon = jnp.exp2((scores - largest) * EXP_SCALE)
        probs = expon * (1.0 / row_sums(expon))
        gqkv_ref[:, at[2]] = dot(probs.astype(BF16), g, PLAIN).astype(BF16)
        weighted = probs * dot(v, g, COLS)
        grad_scores = (weighted - probs * row_sums(weighted)).astype(BF16)
        gqkv_ref[:, at[0]] = (dot(grad_scores, k, ROWS) * SCALE).astype(BF16)
        gqkv_ref[:, at[1]] = (dot(grad_scores, q, PLAIN) * SCALE).astype(BF16)
    grads = gqkv_ref[...]
    sum_ref[...] = row_sums(grads.astype(F32))
    back = dot(grads, w_ref[...], PLAIN)
    gw_ref[:, : 3 * cols] = dot(x_ref[...], grads, ROWS)
    gw_ref[:, 3 * cols :] = dot(ga_ref[...], ctx_ref[...], ROWS)

    @pl.when(slot == 0)
    def _():
        gx_ref[...] = gr_ref[...] + back

    @pl.when(slot > 0)
    def _():
        gx_ref[...] += back


def attend_backward(x, grad_attn, grad_resid, weights, w_output, bias, context):
    rows, width = grad_attn.shape
    slots, cols, _ = w_output.shape
    mine = lambda i, j: (i, 0)
    token = (LENGTH, width)
    weight = lambda i, j: (j, 0, 0)
    return call(
        attend_back_kernel,
        "attend_backward",
        (rows // LENGTH, slots),
        [
            (x, token, mine),
            (grad_attn, token, mine),
            (grad_resid, token, mine),
            (weights, (None, 3 * cols, width), weight),
            (w_output, (None, cols, width), weight),
            (bias, (None, 1, 3 * cols), weight),
            (context, (None, LENGTH, cols), lambda i, j: (j, i, 0)),
        ],
        [
            ((width, slots * 4 * cols), F32, (width, 4 * cols), lambda i, j: (0, j)),
            ((rows, width), F32, token, mine),
            ((rows // LENGTH, slots, 1, 3 * cols), F32, (None, None, 1, 3 * cols), lambda i, j: (i, j, 0, 0)),
        ],
        flops=0,
        moved=0,
        scratch=[pltpu.VMEM((LENGTH, 3 * cols), BF16)],
    )


def inner_kernel(w_ref, h_ref, b_ref, act_ref, slope_ref):
    inner = dot(h_ref[...], w_ref[...], PLAIN) + b_ref[...]
    phi = 0.5 + 0.5 * lax.erf(inner * (0.5**0.5))
    bell = jnp.exp2(inner * inner * (-0.5 * 1.4426950408889634)) * 0.3989422804014327
    act_ref[...] = (inner * phi).astype(BF16)
    slope_ref[...] = phi + inner * bell


def inner_forward(hidden, weights, bias):
    rows, width = hidden.shape
    slots, _, units = bias.shape
    slot = lambda i, j: (i, j, 0)
    block = LENGTH // 2
    return call_with(
        inner_kernel,
        "inner_forward",
        (slots, rows // block),
        lambda i, j: i,
        weights,
        [
            (hidden, (block, width), lambda i, j: (j, 0)),
            (bias, (None, 1, units), lambda i, j: (i, 0, 0)),
        ],
        [
            ((slots, rows, units), BF16, (None, block, units), slot),
            ((slots, rows, units), F32, (None, block, units), slot),
        ],
        flops=2 * rows * width * slots * units,
        exps=2 * rows * slots * units,
    )


def outer_kernel(w_ref, act_ref, hid_ref, vec_ref, out_ref, nrm_ref, inv_ref):
    slot = pl.program_id(1)
    outer = dot(act_ref[...], w_ref[...], PLAIN)

    @pl.when(slot == 0)
    def _():
        out_ref[...] = outer

    @pl.when(slot > 0)
    def _():
        out_ref[...] += outer

    @pl.when(slot == pl.num_programs(1) - 1)
    def _():
        bias, gain, shift = vec_ref[3:4], vec_ref[4:5], vec_ref[5:6]

        def block(at, carry):
            values = hid_ref[at] + (out_ref[at] + bias)
            layer_out, normed, inverse = norm_forward(values, gain, shift)
            out_ref[at] = layer_out
            nrm_ref[at] = normed
            inv_ref[at] = inverse
            return carry

        by_rows(LENGTH, 256, block)


def outer_forward(active, weights, hidden, vectors):
    rows, width = hidden.shape
    slots, _, units = active.shape
    mine = lambda i, j: (i, 0)
    token = (LENGTH, width)
    return call_with(
        outer_kernel,
        "outer_forward",
        (rows // LENGTH, slots),
        lambda i, j: j,
        weights,
        [
            (active, (None, LENGTH, units), lambda i, j: (j, i, 0)),
            (hidden, token, mine),
            (vectors, vectors.shape, lambda i, j: (0, 0)),
        ],
        [
            ((rows, width), F32, token, mine),
            ((rows, width), F32, token, mine),
            ((rows, 1), F32, (LENGTH, 1), mine),
        ],
        flops=2 * rows * width * slots * units,
    )


def last_norm_kernel(cot_ref, nrm_ref, inv_ref, vec_ref, gr_ref, go_ref, sum_ref):
    upstream, normed = cot_ref[...].astype(F32), nrm_ref[...]
    grad = norm_backward(upstream, vec_ref[4:5], normed, inv_ref[...])
    rounded = grad.astype(BF16)
    gr_ref[...] = grad
    go_ref[...] = rounded
    found = (upstream * normed, upstream, rounded.astype(F32))

    @pl.when(pl.program_id(0) == 0)
    def _():
        sum_ref[...] = jnp.zeros_like(sum_ref)

    for i, value in enumerate(found):
        sum_ref[i : i + 1] += row_sums(value)


def last_norm_backward(cotangent, normed, inverse, vectors):
    rows, width = normed.shape
    block = 128
    mine = lambda i: (i, 0)
    flat = lambda i: (0, 0)
    token = (block, width)
    return call(
        last_norm_kernel,
        "last_norm_backward",
        (rows // block,),
        [
            (cotangent, token, mine),
            (normed, token, mine),
            (inverse, (block, 1), mine),
            (vectors, vectors.shape, flat),
        ],
        [
            ((rows, width), F32, token, mine),
            ((rows, width), BF16, token, mine),
            ((8, width), F32, (8, width), flat),
        ],
        flops=0,
        moved=0,
    )


def inner_back_kernel(go_ref, wu_ref, slope_ref, wi_ref, gr_ref, nrm_ref, inv_ref, vec_ref,
                      gi_ref, g1_ref, ga_ref, bsum_ref, sum_ref):
    slot = pl.program_id(1)
    grad_inner = (dot(go_ref[...], wu_ref[...], COLS) * slope_ref[...]).astype(BF16)
    gi_ref[...] = grad_inner
    bsum_ref[...] = row_sums(grad_inner.astype(F32))
    back = dot(grad_inner, wi_ref[...], COLS)

    @pl.when(slot == 0)
    def _():
        g1_ref[...] = gr_ref[...] + back

    @pl.when(slot > 0)
    def _():
        g1_ref[...] += back

    @pl.when(slot == pl.num_programs(1) - 1)
    def _():
        gain = vec_ref[1:2]

        def block(at, sums):
            upstream, normed = g1_ref[at], nrm_ref[at]
            grad = norm_backward(upstream, gain, normed, inv_ref[at])
            rounded = grad.astype(BF16)
            g1_ref[at] = grad
            ga_ref[at] = rounded
            found = (upstream * normed, upstream, rounded.astype(F32))
            return tuple(s + row_sums(f) for s, f in zip(sums, found))

        for i, total in enumerate(by_rows(LENGTH, 256, block, (jnp.zeros_like(gain),) * 3)):
            sum_ref[i : i + 1] = total


def inner_backward(grad_outer, w_outer, slope, w_inner, grad_resid2, normed, inverse, vectors):
    rows, width = grad_outer.shape
    slots, units, _ = w_outer.shape
    mine = lambda i, j: (i, 0)
    token = (LENGTH, width)
    slot = lambda i, j: (j, i, 0)
    weight = lambda i, j: (j, 0, 0)
    return call(
        inner_back_kernel,
        "inner_backward",
        (rows // LENGTH, slots),
        [
            (grad_outer, token, mine),
            (w_outer, (None, units, width), weight),
            (slope, (None, LENGTH, units), slot),
            (w_inner, (None, width, units), weight),
            (grad_resid2, token, mine),
            (normed, token, mine),
            (inverse, (LENGTH, 1), mine),
            (vectors, vectors.shape, lambda i, j: (0, 0)),
        ],
        [
            ((slots, rows, units), BF16, (None, LENGTH, units), slot),
            ((rows, width), F32, token, mine),
            ((rows, width), BF16, token, mine),
            ((rows // LENGTH, slots, 1, units), F32, (None, None, 1, units), lambda i, j: (i, j, 0, 0)),
            ((rows // LENGTH, 8, width), F32, (None, 8, width), lambda i, j: (i, 0, 0)),
        ],
        flops=0,
        moved=0,
    )


def narrow_kernel(x_ref, out_ref):
    out_ref[...] = x_ref[...].astype(BF16)


def narrow(values, block_rows):
    rows, width = values.shape
    at = lambda i: (i, 0)
    block = (block_rows, width)
    out = ((rows, width), BF16, block, at)
    return call(narrow_kernel, "narrow", (rows // block_rows,), [(values, block, at)], [out], 0)[0]


def shift_to(values, tensor, k):
    return lax.ppermute(values, "tensor", [(i, (i + k) % tensor) for i in range(tensor)])


def flip(values, bit):
    return lax.ppermute(values, "dp", [(i, i ^ bit) for i in range(8)])


def stage(*values):
    return lax.optimization_barrier(values)


def slots_kernel(slot_ref, local_ref, x_ref, out_ref):
    del slot_ref
    first = pl.program_id(0) == 0

    @pl.when(first)
    def _():
        out_ref[...] = local_ref[...]

    @pl.when(jnp.logical_not(first))
    def _():
        out_ref[...] = x_ref[...].reshape(out_ref.shape).astype(BF16)


def gather_plain(local, dp, tensor):
    rows, width = local.shape
    share = rows // dp
    piece = lax.dynamic_slice_in_dim(local, lax.axis_index("dp") * share, share, 0).astype(F32)
    full = lax.all_gather(piece, ("dp", "tensor"), axis=0).reshape(dp, tensor, share, width)
    order = (lax.axis_index("tensor") - jnp.arange(tensor, dtype=jnp.int32)) % tensor
    if share % 8:
        full = full.swapaxes(0, 1).reshape(1, tensor, rows, width)
    lead, _, part, _ = full.shape
    return pl.pallas_call(
        slots_kernel,
        grid_spec=pltpu.PrefetchScalarGridSpec(
            num_scalar_prefetch=1,
            grid=(tensor,),
            in_specs=[
                pl.BlockSpec((rows, width), lambda i, slot: (0, 0)),
                pl.BlockSpec((lead, None, part, width), lambda i, slot: (0, slot[i], 0, 0)),
            ],
            out_specs=pl.BlockSpec((None, rows, width), lambda i, slot: (i, 0, 0)),
        ),
        out_shape=jax.ShapeDtypeStruct((tensor, rows, width), BF16),
        cost_estimate=pl.CostEstimate(flops=0, bytes_accessed=6 * full.size, transcendentals=0),
        compiler_params=pltpu.CompilerParams(vmem_limit_bytes=48 << 20),
        name="slots",
    )(order, local, full)


def assemble_kernel(plan, where_ref, local_ref, *refs):
    *pieces, out_ref, hold, sems = refs
    moves = piece_copies(plan, where_ref, pieces, [hold], sems)
    for move in moves:
        move.start()
    out_ref[0] = local_ref[...]
    for move in moves:
        move.wait()
    for k in range(hold.shape[0]):

        def block(at, carry, k=k):
            out_ref[k + 1, at] = hold[k, at].astype(BF16)
            return carry

        by_rows(hold.shape[1], 96, block)


def assemble(stream):
    local, target, pieces = stream
    rows, width = local.shape
    others = pieces[0][0].shape[1]
    plan, where = plan_of([local], pieces, [target])
    space = pl.BlockSpec(memory_space=pltpu.VMEM)
    return pl.pallas_call(
        partial(assemble_kernel, plan),
        in_specs=[pl.BlockSpec(memory_space=pltpu.SMEM), space] + [pl.BlockSpec(memory_space=pl.ANY)] * len(pieces),
        out_specs=space,
        out_shape=jax.ShapeDtypeStruct((others + 1, rows, width), BF16),
        scratch_shapes=[pltpu.VMEM((others, rows, width), F32), pltpu.SemaphoreType.DMA((where.shape[0],))],
        cost_estimate=pl.CostEstimate(flops=0, bytes_accessed=others * rows * width * 6, transcendentals=0),
        compiler_params=pltpu.CompilerParams(vmem_limit_bytes=48 << 20),
        name="assemble",
    )(where, local, *(array for array, _ in pieces))


def shares(weights, dp=8):
    me = lax.axis_index("dp")
    cut = [lax.dynamic_slice_in_dim(w, me * (w.shape[0] // dp), w.shape[0] // dp, 0) for w in weights]
    return jnp.concatenate(cut, axis=0).astype(F32)


def across(values, tensor):
    return [shift_to(values, tensor, k) for k in range(1, tensor)]


def wide(v, w):
    return jnp.concatenate([v, w], axis=0)


def other_core(*values):
    return tuple(flip(v, 1) for v in values)


def copy_kernel(plan, count, *refs):
    ins, outs = refs[:count], refs[count:]
    for source, source_at, target, target_at in plan:
        outs[target][target_at] = ins[source][source_at]


def copies(ins, shapes, plan):
    space = pl.BlockSpec(memory_space=pltpu.VMEM)
    return pl.pallas_call(
        partial(copy_kernel, plan, len(ins)),
        in_specs=[space] * len(ins),
        out_specs=[space] * len(shapes),
        out_shape=[jax.ShapeDtypeStruct(shape, F32) for shape in shapes],
        cost_estimate=pl.CostEstimate(flops=0, bytes_accessed=0, transcendentals=0),
        compiler_params=pltpu.CompilerParams(vmem_limit_bytes=32 << 20),
        name="copies",
    )(*ins)


def halves(arrived, upper):
    rows, width = arrived[0].shape
    n = len(arrived)
    plan = [(k, (slice(0, upper),), 0, (0, k)) for k in range(n)]
    plan += [(k, (slice(upper, rows),), 1, (0, k)) for k in range(n)]
    return copies(arrived, [(1, n, upper, width), (1, n, rows - upper, width)], plan)


def join(a, ax, b, by):
    _, n, upper, width = a.shape
    lower = b.shape[2]
    plan = []
    for i, (v, w) in enumerate(((a, b), (ax, by))):
        every = slice(None)
        plan += [(2 * i, (0,), 0, (i,)), (2 * i + 1, (0,), 1, (i,))]
        plan += [(2 * i, (0,), 2, (i, every, slice(0, upper))), (2 * i + 1, (0,), 2, (i, every, slice(upper, upper + lower)))]
    shapes = [(2, n, upper, width), (2, n, lower, width), (2, n, upper + lower, width)]
    return copies([a, b, ax, by], shapes, plan)


def pieces_of(locals_, a, b, ay, bx, c, d):
    me = lax.axis_index("dp")
    cut_at, end = a.shape[2], a.shape[2] + b.shape[2]
    ends = [0]
    for w in locals_:
        ends.append(ends[-1] + w.shape[0] // 8)

    def spans(first, last):
        found = []
        for target in range(len(locals_)):
            low, high = max(first, ends[target]), min(last, ends[target + 1])
            if low < high:
                found.append((low - first, high - low, target, low - ends[target]))
        return found

    upper = lambda rels: [(i, me ^ r, 0, spans(0, cut_at)) for i, r in enumerate(rels)]
    lower = lambda rels, base=0: [(i, me ^ r, base, spans(cut_at, end)) for i, r in enumerate(rels)]
    return [
        (a, upper((0, 2))),
        (b, lower((0, 4))),
        (ay, upper((4, 6))),
        (bx, lower((2, 6))),
        (c, upper((1, 3)) + lower((1, 5), cut_at)),
        (d[0], upper((5, 7))),
        (d[1], lower((3, 7))),
    ]


def block_order(width):
    me = lax.axis_index("dp")
    share = width // 8
    rel = jnp.array([7, 5, 3, 1, 6, 4, 2, 0])
    source = (me ^ rel[jnp.arange(width) // share]) * share + jnp.arange(width) % share
    return (lax.broadcasted_iota(jnp.int32, (width, width), 0) == source[None, :]).astype(BF16)


def grad_kernel(count, *refs):
    order_ref, refs = refs[0], refs[1:]
    lefts, rights, (send_ref, keep_ref), holds = (
        refs[:count], refs[count : 2 * count], refs[2 * count : 2 * count + 2], refs[2 * count + 2 :],
    )

    @pl.when(pl.program_id(0) == 0)
    def _():
        for left, hold in zip(lefts, holds):
            hold[...] = dot(left[...], order_ref[...], PLAIN).astype(BF16)

    half = send_ref.shape[0]
    start = 0
    for hold, right in zip(holds, rights):
        span = slice(start, start + right.shape[-1])
        value = dot(hold[...], right[...], ROWS)
        send_ref[:, span] = value[:half]
        keep_ref[:, span] = value[half:]
        start = span.stop


def grad_rows(order, pairs):
    rows, width = pairs[0][0].shape
    slots = pairs[0][1].shape[0]
    cols = sum(r.shape[-1] for _, r in pairs)
    flat = lambda j: (0, 0)
    ins = [(order, order.shape, flat)]
    ins += [(left, left.shape, flat) for left, _ in pairs]
    ins += [(right, (None,) + right.shape[1:], lambda j: (j, 0, 0)) for _, right in pairs]
    out = ((width // 2, slots * cols), F32, (width // 2, cols), lambda j: (0, j))
    scratch = [pltpu.VMEM((rows, width), BF16)] * len(pairs)
    return call(
        partial(grad_kernel, len(pairs)), "grad_rows", (slots,), ins, [out, out], 0, 0, scratch, moved=0
    )


def full_kernel(count, *refs):
    lefts, rights, out_ref = refs[:count], refs[count:-1], refs[-1]
    start = 0
    for left, right in zip(lefts, rights):
        span = slice(start, start + right.shape[-1])
        out_ref[:, span] = dot(left[...], right[...], ROWS)
        start = span.stop


def grad_full(*pairs):
    rows, width = pairs[0][0].shape
    slots = pairs[0][1].shape[0]
    cols = sum(r.shape[-1] for _, r in pairs)
    ins = [(left, left.shape, lambda j: (0, 0)) for left, _ in pairs]
    ins += [(right, (None,) + right.shape[1:], lambda j: (j, 0, 0)) for _, right in pairs]
    return call(
        partial(full_kernel, len(pairs)),
        "grad_full",
        (slots,),
        ins,
        [((width, slots * cols), F32, (width, cols), lambda j: (0, j))],
        flops=0,
        moved=0,
    )[0]


def split_paths(held, share):
    mid = held.shape[1] // 2
    pick = lambda i, cols: held[i * share : (i + 1) * share, cols]
    a, b = slice(None, mid), slice(mid, None)
    join = lambda i, j, cols: jnp.concatenate([pick(i, cols), pick(j, cols)], axis=0)
    return (join(0, 2, a), join(1, 3, a)), (join(0, 1, b), join(2, 3, b))


def scatter_plain(grad, tensor):
    part = lax.psum_scatter(grad, "dp", scatter_dimension=0, tiled=True)
    part = columns(part, tensor)
    return sum((shift_to(part[k], tensor, tensor - k) for k in range(1, tensor)), part[0])


def columns(part, tensor):
    cols = part.shape[1] // tensor
    return [part[:, k * cols : (k + 1) * cols] for k in range(tensor)]


def up(values, tensor, step):
    return lax.ppermute(values, "tensor", [(i, i + 1) for i in range(step)])


def down(values, tensor, step):
    return lax.ppermute(values, "tensor", [(i, i - 1) for i in range(tensor - step, tensor)])


def place_kernel(z_ref, own_ref, *refs):
    *others, out_ref = refs
    count = len(others) // 2
    below, above = others[:count], others[count:]
    away = pl.program_id(0) - z_ref[0]

    @pl.when(away == 0)
    def _():
        out_ref[...] = own_ref[...]

    for k in range(count):

        @pl.when(away == -(k + 1))
        def _(k=k):
            out_ref[...] = below[k][...]

        @pl.when(away == k + 1)
        def _(k=k):
            out_ref[...] = above[k][...]


def place(own, below, above):
    rows, width = own.shape
    count = len(below) + 1
    whole = (rows, width)
    return call(
        place_kernel,
        "place",
        (count,),
        [(v, whole, lambda i, z: (0, 0)) for v in (own, *below, *above)],
        [((count * rows, width), F32, whole, lambda i, z: (i, 0))],
        flops=0,
        moved=0,
        prefetch=lax.axis_index("tensor").astype(jnp.int32).reshape(1),
    )[0]


def onward(values, tensor, step):
    u, d = values
    u = lax.ppermute(u, "tensor", [(i, i + 1) for i in range(step - 1, tensor - 1)])
    d = lax.ppermute(d, "tensor", [(i, i - 1) for i in range(1, tensor - step + 1)])
    return u, d


def swap(values, tensor, bit):
    return lax.ppermute(values, "tensor", [(i, i ^ bit) for i in range(tensor)])


def shards(
    dp,
    tensor,
    inputs,
    w_query,
    b_query,
    w_key,
    w_value,
    b_value,
    w_output,
    b_output,
    gain_attn,
    shift_attn,
    w_inner,
    b_inner,
    w_outer,
    b_outer,
    gain_ffn,
    shift_ffn,
    cotangent,
):
    tok_rows, width = inputs.shape
    own_rows = tok_rows // tensor
    cols = w_query.shape[1]
    z = lax.axis_index("tensor")
    own = lambda a: lax.dynamic_slice_in_dim(a, z * own_rows, own_rows, 0)
    row = lambda a: a.astype(F32)[None, :]

    vectors = row(jnp.concatenate([b_query, jnp.zeros_like(b_query), b_value, b_inner]))
    qkv_local = jnp.concatenate([w_query.T, w_key.T, w_value.T], axis=0)
    x, cot = own(inputs), own(cotangent)
    rows_of = (b_output, gain_attn, shift_attn, b_outer, gain_ffn, shift_ffn, b_outer, b_outer)
    wide_vectors = jnp.stack(rows_of).astype(F32)
    slots_at = (z - jnp.arange(tensor, dtype=jnp.int32)) % tensor
    staged = (
        dp == 8 and tensor == 4 and own_rows == LENGTH and width % 128 == 0
        and w_inner.shape == w_outer.shape == (width, width) and cols % 64 == 0
    )

    def rest_of_attention(context, weights):
        return output_forward(slots_at, x, context, weights, wide_vectors)


    def small_sums(qkv_sums, inner_sums, sums_one, sums_two):
        by_slot = jnp.concatenate([jnp.sum(qkv_sums, axis=0), jnp.sum(inner_sums, axis=0)], axis=-1)
        by_place = by_slot[slots_at].reshape(-1)
        rest = jnp.concatenate([jnp.sum(sums_one, axis=0)[:3], sums_two[:3]]).reshape(-1)
        return jnp.concatenate([by_place, rest])

    local_bias = vectors[:, : 3 * cols]
    context = attend_forward(inputs, qkv_local, local_bias)
    context = context.reshape(tensor, -1, context.shape[1])
    if not staged:
        vectors = jnp.stack([vectors] + across(vectors, tensor))
        qkv_bias, inner_bias = vectors[..., : 3 * cols], vectors[..., 3 * cols :]
        inner_full, output_full, outer_full, qkv_full = (
            gather_plain(w, dp, tensor) for w in (w_inner, w_output, w_outer, qkv_local)
        )
        context = lax.all_to_all(context, "tensor", 0, 0, tiled=True)
        context, hidden, hidden_bf, normed, inverse, output_full = rest_of_attention(context, output_full)
        active, slope, inner_full = inner_forward(hidden_bf, inner_full, inner_bias)
        layer_out, normed_two, inverse_two, outer_full = outer_forward(active, outer_full, hidden, wide_vectors)
        grad_resid2, grad_outer, sums_two = last_norm_backward(cot, normed_two, inverse_two, wide_vectors)
        layer_out = narrow(lax.all_gather(layer_out, "tensor", axis=0, tiled=True), own_rows)
        grad_inner, grad_resid1, grad_attn, inner_sums, sums_one = inner_backward(
            grad_outer, outer_full, slope, inner_full, grad_resid2, normed, inverse, wide_vectors
        )
        part3, grad_x, qkv_sums = attend_backward(x, grad_attn, grad_resid1, qkv_full, output_full, qkv_bias, context)
        grad_inputs = lax.all_gather(grad_x, "tensor", axis=0, tiled=True)
        gu = scatter_plain(grad_full((grad_outer, active)), tensor)
        gi = scatter_plain(grad_full((hidden_bf, grad_inner)), tensor)
        gqkv = scatter_plain(part3, tensor)
        gqkv, go = gqkv[:, : 3 * cols], gqkv[:, 3 * cols :]
        sums = lax.psum(small_sums(qkv_sums, inner_sums, sums_one, sums_two), ("dp", "tensor"))
    else:
        order = block_order(width)
        share = width // 8
        p1, p2, p3 = shares([w_inner, w_output]), shares([w_outer]), shares([qkv_local])
        n1, n2, n3 = (-(-p.shape[0] // 16) * 8 for p in (p1, p2, p3))

        z1, arrived = across(p1, tensor), across(vectors, tensor)
        vectors = jnp.stack([vectors] + arrived)
        a1, b1 = halves(z1, n1)
        a1, b1, p2, context, vectors = stage(a1, b1, p2, context, vectors)
        qkv_bias, inner_bias = vectors[..., : 3 * cols], vectors[..., 3 * cols :]

        ax, by, z2 = flip(a1, 2), flip(b1, 4), across(p2, tensor)
        a1, b1, ab1 = join(a1, ax, b1, by)
        a2, b2 = halves(z2, n2)
        a1, b1, ab1, a2, b2, context, x, order = stage(a1, b1, ab1, a2, b2, context, x, order)

        c1 = flip(ab1, 1)
        context, c1 = stage(context, c1)
        context = lax.all_to_all(context, "tensor", 0, 0, tiled=True)
        ay1, bx1, ax, by = flip(a1, 4), flip(b1, 2), flip(a2, 2), flip(b2, 4)
        a2, b2, ab2 = join(a2, ax, b2, by)
        d1 = other_core(ay1, bx1)
        ay1, bx1, a2, b2, ab2, p3 = stage(ay1, bx1, a2, b2, ab2, p3)

        c2, ay2, bx2 = flip(ab2, 1), flip(a2, 4), flip(b2, 2)
        pieces = pieces_of([w_inner, w_output], a1, b1, ay1, bx1, c1, d1)
        context, hidden, hidden_bf, normed, inverse, output_full = rest_of_attention(context, Stream(w_output, 1, pieces))
        hidden_bf, c2, p3 = stage(hidden_bf, c2, p3)
        z3 = across(p3, tensor)
        active, slope, inner_full = inner_forward(hidden_bf, Stream(w_inner, 0, pieces), inner_bias)
        ay2, bx2, *z3, active = stage(ay2, bx2, *z3, active)

        d2 = other_core(ay2, bx2)
        a3, b3 = halves(z3, n3)
        ax, by = flip(a3, 2), flip(b3, 4)
        pieces = pieces_of([w_outer], a2, b2, ay2, bx2, c2, d2)
        layer_out, normed_two, inverse_two, outer_full = outer_forward(
            active, Stream(w_outer, 0, pieces), hidden, wide_vectors
        )
        ax, by, layer_out, normed_two = stage(ax, by, layer_out, normed_two)

        layer_out = lax.all_gather(layer_out, "tensor", axis=0, tiled=True)
        grad_resid2, grad_outer, sums_two = last_norm_backward(cot, normed_two, inverse_two, wide_vectors)
        a3, b3, ab3 = join(a3, ax, b3, by)
        a3, b3, ab3, grad_outer = stage(a3, b3, ab3, grad_outer)

        ay3, bx3, c3 = flip(a3, 4), flip(b3, 2), flip(ab3, 1)
        part1 = grad_full((grad_outer, active))
        part1, grad_outer = stage(part1, grad_outer)
        part1 = lax.psum_scatter(part1, "dp", scatter_dimension=0, tiled=True)
        grad_inner, grad_resid1, grad_attn, inner_sums, sums_one = inner_backward(
            grad_outer, outer_full, slope, inner_full, grad_resid2, normed, inverse, wide_vectors
        )
        ay3, bx3, c3, grad_inner, grad_attn = stage(ay3, bx3, c3, grad_inner, grad_attn)

        d3 = other_core(ay3, bx3)
        send, keep = grad_rows(order, [(hidden_bf, grad_inner)])
        *d3, send, grad_attn = stage(*d3, send, grad_attn)

        got = flip(send, 1)
        qkv_full = assemble(Stream(qkv_local, 0, pieces_of([qkv_local], a3, b3, ay3, bx3, c3, d3)))
        (a, ak), (b, bk) = split_paths(keep + got, share)
        a, b, qkv_full, grad_attn = stage(a, b, qkv_full, grad_attn)

        ax, by = flip(a, 2), flip(b, 4)
        part3, grad_x, qkv_sums = attend_backward(
            x, grad_attn, grad_resid1, qkv_full, output_full, qkv_bias, context
        )
        a, b = ak + ax, bk + by
        a_send, b_send = stage(a[:share], b[:share])

        part3 = lax.psum_scatter(part3, "dp", scatter_dimension=0, tiled=True)
        g1 = onward((grad_x, grad_x), tensor, 1)
        ay, bx = flip(a_send, 4), flip(b_send, 2)
        part2 = jnp.concatenate([a[share:] + ay, b[share:] + bx], axis=1)
        extra = small_sums(qkv_sums, inner_sums, sums_one, sums_two)
        extra = jnp.pad(extra, (0, -extra.shape[0] % (8 * width))).reshape(-1, width)
        extra = extra + flip(extra, 1)
        layer_out = narrow(layer_out, own_rows)
        first = columns(wide(part1, part2), tensor)
        g2 = onward(g1, tensor, 2)
        _, _, extra, first[0], first[1], first[2], first[3], layer_out = stage(*g1, extra, *first, layer_out)

        u, d = up(first[1], tensor, 1), down(first[3], tensor, 1)
        extra = extra + flip(extra, 2)
        g3 = onward(g2, tensor, 3)
        _, _, u, d, part3, extra = stage(*g2, first[2] + u, first[2] + d, part3, extra)

        u, d = up(u, tensor, 2), down(d, tensor, 2)
        last = columns(part3, tensor)
        v, w = up(last[1], tensor, 1), down(last[3], tensor, 1)
        extra = extra + flip(extra, 4)
        v, w, extra = stage(last[2] + v, last[2] + w, extra)

        v, w = up(v, tensor, 2), down(w, tensor, 2)
        extra = extra + swap(extra, tensor, 1)
        _, _, u, d, v, w, extra = stage(*g3, first[3] + u, first[1] + d, last[3] + v, last[1] + w, extra)

        u, d, v, w = up(u, tensor, 3), down(d, tensor, 3), up(v, tensor, 3), down(w, tensor, 3)
        extra = extra + swap(extra, tensor, 2)
        v, w, grad_x = stage(v, w, grad_x)
        grad_inputs = place(grad_x, [g1[0], g2[0], g3[0]], [g1[1], g2[1], g3[1]])
        gu, gqkv = first[0] + u + d, last[0] + v + w
        gu, gi = gu[:share], gu[share:]
        gqkv, go = gqkv[:, : 3 * cols], gqkv[:, 3 * cols :]
        sums = extra.reshape(-1)

    span = 3 * cols + w_inner.shape[1]
    mine = lax.dynamic_slice_in_dim(sums, z * span, span, 0)
    rest = sums[span * tensor :][: 6 * width].reshape(6, width)
    return (
        layer_out,
        grad_inputs,
        gqkv[:, :cols],
        mine[:cols],
        gqkv[:, cols : 2 * cols],
        gqkv[:, 2 * cols :],
        mine[2 * cols : 3 * cols],
        go.T,
        rest[2],
        rest[0],
        rest[1],
        gi,
        mine[3 * cols :],
        gu.T,
        rest[5],
        rest[3],
        rest[4],
    )


def solution(mesh):
    wide, tall, vector = P(None, "tensor"), P("tensor", None), P("tensor")
    tokens, both = P("dp", None), P("dp", "tensor")
    in_specs = (
        tokens, wide, vector, wide, wide, vector, tall, P(), P(), P(), wide, vector, tall, P(), P(), P(), tokens,
    )
    out_specs = (
        tokens, tokens, both, vector, both, both, vector, P("tensor", "dp"), P(), P(), P(), both, vector,
        P("tensor", "dp"), P(), P(), P(),
    )
    body = partial(shards, mesh.shape["dp"], mesh.shape["tensor"])
    return jax.shard_map(body, mesh=mesh, in_specs=in_specs, out_specs=out_specs, check_vma=False)
```
